32 devices in a mesh: dp: 4 (over z), seq: 8 (over y, x, core).
Axes of the slice: x: 2, y: 2, z: 4, core: 2. Of those that a mesh axis runs over, the one named last changes fastest.
Arguments:
- layer_input: bfloat16 [2, 4, 2048, 1152], P(None, 'dp', 'seq'), may hold values from -6 to 6
- out_cotangent: bfloat16 [2, 4, 2048, 1152], P(None, 'dp', 'seq'), may hold values from -6 to 6
- seq_lengths: int32 [2, 4, 2], P(None, 'dp'), may hold values from 0 to 2048, as said below
- inputnorm: bfloat16 [1152], P(('dp', 'seq')), may hold values from -0.5 to 0.5
- queryproj: bfloat16 [1152, 1024], P(('dp', 'seq')), may hold values from -0.1875 to 0.1875
- keyproj: bfloat16 [1152, 256], P(('dp', 'seq')), may hold values from -0.1875 to 0.1875
- valueproj: bfloat16 [1152, 256], P(('dp', 'seq')), may hold values from -0.1875 to 0.1875
- querynorm: bfloat16 [256], P(('dp', 'seq')), may hold values from 0.29882812 to 0.69921875
- keynorm: bfloat16 [256], P(('dp', 'seq')), may hold values from 0.29882812 to 0.69921875
- outproj: bfloat16 [1024, 1152], P(('dp', 'seq')), may hold values from -0.1875 to 0.1875
- attnnorm: bfloat16 [1152], P(('dp', 'seq')), may hold values from -0.5 to 0.5
- prefeednorm: bfloat16 [1152], P(('dp', 'seq')), may hold values from -0.5 to 0.5
- gateproj: bfloat16 [1152, 6912], P(('dp', 'seq')), may hold values from -0.1875 to 0.1875
- upproj: bfloat16 [1152, 6912], P(('dp', 'seq')), may hold values from -0.1875 to 0.1875
- downproj: bfloat16 [6912, 1152], P(('dp', 'seq')), may hold values from -0.078125 to 0.078125
- postfeednorm: bfloat16 [1152], P(('dp', 'seq')), may hold values from -0.5 to 0.5
Outputs:
- layer_output: float32 [2, 4, 2048, 1152], P(None, 'dp', 'seq')
- input_grad: float32 [2, 4, 2048, 1152], P(None, 'dp', 'seq')
- inputnorm_grad: float32 [1152], P(('dp', 'seq'))
- queryproj_grad: float32 [1152, 1024], P(('dp', 'seq'))
- keyproj_grad: float32 [1152, 256], P(('dp', 'seq'))
- valueproj_grad: float32 [1152, 256], P(('dp', 'seq'))
- querynorm_grad: float32 [256], P(('dp', 'seq'))
- keynorm_grad: float32 [256], P(('dp', 'seq'))
- outproj_grad: float32 [1024, 1152], P(('dp', 'seq'))
- attnnorm_grad: float32 [1152], P(('dp', 'seq'))
- prefeednorm_grad: float32 [1152], P(('dp', 'seq'))
- gateproj_grad: float32 [1152, 6912], P(('dp', 'seq'))
- upproj_grad: float32 [1152, 6912], P(('dp', 'seq'))
- downproj_grad: float32 [6912, 1152], P(('dp', 'seq'))
- postfeednorm_grad: float32 [1152], P(('dp', 'seq'))
The draws below stay inside these ranges and needn't reach their ends.
Inputs may be any that keep to these rules, and one draw needn't show every extreme that they name: `seq_lengths`: in each row the nonzero lengths come first, are equal, and are 2048 divided by a power of two no larger than 2, so that they sum to 2048. For each index of dp, one micro-batch drawn from the seed holds a single sequence of 2048 tokens.
All inputs are finite; a program needn't handle non-finite values.
Results may differ from the reference program's by a relative error of at most 0.02.
Values may be sent and summed in bfloat16 or wider, within the bound.
No kernel may reach another device: no remote copies, remote signals or barrier semaphores. Data moves between devices by JAX's collectives and lax.ppermute only.
A program may use at most 576 MiB of HBM per device.

```python
import math
import jax
import jax.numpy as jnp
from jax import lax

D = 1152
HEADS = 4
HD = 256
FF = 6912
WINDOW = 512
MB = 2
QD = 1024
ROW = 2048
SLOTS = 2
GROUPS = 4


def draw_seq_lengths(key, part):
    key_whole = jax.random.fold_in(key, 11)
    key_split = jax.random.fold_in(key, 12)
    levels = SLOTS.bit_length() - 1
    whole_batch = jax.random.randint(key_whole, (GROUPS,), 0, MB)
    powers = jax.random.randint(key_split, (MB, GROUPS), 0, levels + 1)
    batch_index = jnp.arange(MB, dtype=jnp.int32)[:, None]
    powers = jnp.where(batch_index == whole_batch[None, :], 0, powers)
    pieces = jnp.left_shift(jnp.int32(1), powers.astype(jnp.int32))
    length = jnp.int32(ROW) // pieces
    slot_index = jnp.arange(SLOTS, dtype=jnp.int32)[None, None, :]
    return jnp.where(slot_index < pieces[:, :, None], length[:, :, None], 0).astype(jnp.int32)


def shard_levels(stream_key, dims, cuts, smallest, top_value):
    gain, own = 1.0, jax.random.fold_in(stream_key, 6)
    for dim, shards_of in cuts:
        steps = jnp.exp(jax.random.uniform(jax.random.fold_in(own, dim), (shards_of,), jnp.float32, smallest / len(cuts), top_value / len(cuts)))
        gain = gain * jnp.repeat(steps, dims[dim] // shards_of).reshape([-1 if axis == dim else 1 for axis in range(len(dims))])
    return gain


def centred(stream_key, shape, scale, bound, cuts=(), held_as=jnp.bfloat16):
    drawn = scale * jax.random.normal(stream_key, shape, jnp.float32)
    if cuts:
        drawn = drawn * shard_levels(stream_key, shape, cuts, -0.22, 0.18)
    return jnp.clip(drawn, -bound, bound).astype(held_as)


def setup_inputs(seed: int = 0) -> dict:
    seeds = jax.random.split(jax.random.key(seed), 17)
    return {
        "layer_input": centred(seeds[0], (MB, GROUPS, ROW, D), 1.0, 6.0, ((1, 4), (2, 8))),
        "out_cotangent": centred(seeds[1], (MB, GROUPS, ROW, D), 1.0, 6.0, ((1, 4), (2, 8))),
        "seq_lengths": draw_seq_lengths(jax.random.fold_in(seeds[16], 71), 0),
        "inputnorm": jnp.clip(jax.random.uniform(seeds[3], (D,), jnp.float32, -0.5, 0.5) * shard_levels(seeds[3], (D,), ((0, 32),), -0.4, 0.0), -0.5, 0.5).astype(jnp.bfloat16),
        "queryproj": centred(seeds[4], (D, QD), D ** -0.5, 0.1875, ((0, 32),)),
        "keyproj": centred(seeds[5], (D, HD), D ** -0.5, 0.1875, ((0, 32),)),
        "valueproj": centred(seeds[6], (D, HD), D ** -0.5, 0.1875, ((0, 32),)),
        "querynorm": jnp.clip(0.29882812 + 0.40039062 * jax.random.uniform(seeds[7], (HD,), jnp.float32) ** shard_levels(seeds[7], (HD,), ((0, 32),), -0.2, 0.2), 0.29882812, 0.69921875).astype(jnp.bfloat16),
        "keynorm": jnp.clip(0.29882812 + 0.40039062 * jax.random.uniform(seeds[8], (HD,), jnp.float32) ** shard_levels(seeds[8], (HD,), ((0, 32),), -0.2, 0.2), 0.29882812, 0.69921875).astype(jnp.bfloat16),
        "outproj": centred(seeds[9], (QD, D), QD ** -0.5, 0.1875, ((0, 32),)),
        "attnnorm": jnp.clip(jax.random.uniform(seeds[10], (D,), jnp.float32, -0.5, 0.5) * shard_levels(seeds[10], (D,), ((0, 32),), -0.4, 0.0), -0.5, 0.5).astype(jnp.bfloat16),
        "prefeednorm": jnp.clip(jax.random.uniform(seeds[11], (D,), jnp.float32, -0.5, 0.5) * shard_levels(seeds[11], (D,), ((0, 32),), -0.4, 0.0), -0.5, 0.5).astype(jnp.bfloat16),
        "gateproj": centred(seeds[12], (D, FF), D ** -0.5, 0.1875, ((0, 32),)),
        "upproj": centred(seeds[13], (D, FF), D ** -0.5, 0.1875, ((0, 32),)),
        "downproj": centred(seeds[14], (FF, D), FF ** -0.5, 0.078125, ((0, 32),)),
        "postfeednorm": jnp.clip(jax.random.uniform(seeds[15], (D,), jnp.float32, -0.5, 0.5) * shard_levels(seeds[15], (D,), ((0, 32),), -0.4, 0.0), -0.5, 0.5).astype(jnp.bfloat16),
    }


@jax.custom_vjp
def low(v):
    return lax.optimization_barrier(v.astype(jnp.bfloat16)).astype(jnp.float32)

@jax.custom_vjp
def low_back(v):
    return v

def low_keep(v):
    return (low(v), None)

def low_pass(kept, grad):
    return (grad,)

def back_keep(v):
    return (v, None)

def back_low(kept, grad):
    return (low(grad),)
low.defvjp(low_keep, low_pass)
low_back.defvjp(back_keep, back_low)
norm_eps = 1e-06

def rms_scale(values, gain_vec):
    mean_square = lax.optimization_barrier(jnp.mean(values * values, axis=-1, keepdims=True))
    return values * lax.rsqrt(mean_square + norm_eps) * (1.0 + gain_vec)

def rotate_half(values):
    middle = values.shape[-1] // 2
    return jnp.concatenate([-values[..., middle:], values[..., :middle]], axis=-1)

def rope_tables(relative):
    middle = HD // 2
    counter = jnp.arange(middle, dtype=jnp.float32)
    inverse = jnp.power(jnp.float32(10000.0), -2.0 * counter / HD)
    angles = relative.astype(jnp.float32)[:, None] * inverse[None, :]
    cosine = jnp.cos(angles)
    sine_table = jnp.sin(angles)
    return (jnp.concatenate([cosine, cosine], -1), jnp.concatenate([sine_table, sine_table], -1))

def prepare_heads(values, gain_vec, cosine, sine_table, factor):
    row_count = values.shape[0]
    head_view = values.reshape(row_count, -1, gain_vec.shape[0])
    normed = rms_scale(head_view, gain_vec)
    turned = normed * cosine[:, None, :] + rotate_half(normed) * sine_table[:, None, :]
    return (turned * factor).reshape(row_count, -1)

def gelu_gate(gate_raw, up_raw):
    return jax.nn.gelu(gate_raw, approximate=True) * up_raw

def locate(positions, starts):
    is_after = positions[:, None] >= starts[None, :]
    segment = lax.optimization_barrier(jnp.sum(is_after.astype(jnp.int32), axis=1))
    first_pos = lax.optimization_barrier(jnp.max(jnp.where(is_after, starts[None, :], 0), axis=1))
    return (segment, positions - first_pos)

def matmul_high(left_side, right_side):
    return jnp.dot(left_side, right_side, precision=lax.Precision.HIGHEST)

def attend(query_low, keys_low, value_low, segment):
    block_rows = min(512, ROW)
    count_blocks = ROW // block_rows
    keys_pad = jnp.concatenate([jnp.zeros((WINDOW, HD), keys_low.dtype), keys_low], 0)
    value_pad = jnp.concatenate([jnp.zeros((WINDOW, HD), value_low.dtype), value_low], 0)
    segment_pad = jnp.concatenate([jnp.full((WINDOW,), -1, jnp.int32), segment.astype(jnp.int32)], 0)

    def one_block(begin_row):
        query_block = lax.dynamic_slice_in_dim(query_low, begin_row, block_rows, 0)
        query_seg = lax.dynamic_slice_in_dim(segment.astype(jnp.int32), begin_row, block_rows, 0)
        keys_block = lax.dynamic_slice_in_dim(keys_pad, begin_row, block_rows + WINDOW, 0)
        value_block = lax.dynamic_slice_in_dim(value_pad, begin_row, block_rows + WINDOW, 0)
        keys_seg = lax.dynamic_slice_in_dim(segment_pad, begin_row, block_rows + WINDOW, 0)
        query_pos = begin_row + jnp.arange(block_rows, dtype=jnp.int32)
        keys_pos = begin_row - WINDOW + jnp.arange(block_rows + WINDOW, dtype=jnp.int32)
        allowed = (keys_seg[None, :] == query_seg[:, None]) & (keys_pos[None, :] >= 0)
        allowed = allowed & (keys_pos[None, :] <= query_pos[:, None]) & (query_pos[:, None] - keys_pos[None, :] < WINDOW)
        head_view = query_block.reshape(block_rows, HEADS, HD)
        scores = low_back(jnp.einsum('qhd,kd->hqk', head_view, keys_block, precision=lax.Precision.HIGHEST))
        masked = jnp.where(allowed[None], scores, -1e+30)
        row_max = lax.optimization_barrier(jnp.max(masked, axis=-1, keepdims=True))
        log_total = row_max + jnp.log(lax.optimization_barrier(jnp.sum(jnp.exp(masked - row_max), axis=-1, keepdims=True)))
        attn_probs = low(jnp.exp(masked - log_total))
        mixed_out = jnp.einsum('hqk,kd->qhd', attn_probs, value_block, precision=lax.Precision.HIGHEST)
        return mixed_out.reshape(block_rows, HEADS * HD)
    begin_all = jnp.arange(count_blocks, dtype=jnp.int32) * block_rows
    return lax.map(jax.checkpoint(one_block), begin_all).reshape(ROW, HEADS * HD)

def layer(row_value, params, segment, relative):
    inputnorm, queryproj, keyproj, valueproj, querynorm, keynorm, outproj, attnnorm, prefeednorm, gateproj, upproj, downproj, postfeednorm = params
    cosine, sine_table = rope_tables(relative)
    normed_in = low(rms_scale(row_value, inputnorm))
    query_raw = low_back(matmul_high(normed_in, queryproj))
    keys_raw = low_back(matmul_high(normed_in, keyproj))
    value_low = low_back(low(matmul_high(normed_in, valueproj)))
    query_low = low(prepare_heads(query_raw, querynorm, cosine, sine_table, 1.0 / math.sqrt(HD)))
    keys_low = low(prepare_heads(keys_raw, keynorm, cosine, sine_table, 1.0))
    attended = low_back(low(attend(query_low, keys_low, value_low, segment)))
    attn_out = low_back(matmul_high(attended, outproj))
    hidden_one = row_value + rms_scale(attn_out, attnnorm)
    normed_ffn = low(rms_scale(hidden_one, prefeednorm))
    gate_raw = low_back(matmul_high(normed_ffn, gateproj))
    up_raw = low_back(matmul_high(normed_ffn, upproj))
    activated = low(gelu_gate(gate_raw, up_raw))
    ffn_out = low_back(matmul_high(activated, downproj))
    return hidden_one + rms_scale(ffn_out, postfeednorm)

def reference(layer_input, out_cotangent, seq_lengths, inputnorm, queryproj, keyproj, valueproj, querynorm, keynorm, outproj, attnnorm, prefeednorm, gateproj, upproj, downproj, postfeednorm):
    weights = tuple((weight_arg.astype(jnp.float32) for weight_arg in (inputnorm, queryproj, keyproj, valueproj, querynorm, keynorm, outproj, attnnorm, prefeednorm, gateproj, upproj, downproj, postfeednorm)))
    row_inputs = layer_input.astype(jnp.float32).reshape(MB * GROUPS, ROW, D)
    row_cots = out_cotangent.astype(jnp.float32).reshape(MB * GROUPS, ROW, D)
    row_lengths = seq_lengths.astype(jnp.int32).reshape(MB * GROUPS, SLOTS)

    def one_row(totals, row_item):
        row_input, row_cot, lengths_row = row_item
        starts = jnp.cumsum(lengths_row) - lengths_row
        positions = jnp.arange(ROW, dtype=jnp.int32)
        segment, relative = locate(positions, starts.astype(jnp.int32))

        def forward(row_value, *params):
            return layer(row_value, params, segment, relative)
        row_out, back_fn = jax.vjp(forward, row_input, *weights)
        grads = back_fn(row_cot)
        totals = tuple((running + update for running, update in zip(totals, grads[1:])))
        return (totals, (row_out, grads[0]))
    zeros_init = tuple((jnp.zeros_like(weight_arg) for weight_arg in weights))
    totals, (outputs, input_grads) = lax.scan(one_row, zeros_init, (row_inputs, row_cots, row_lengths))
    return (outputs.reshape(MB, GROUPS, ROW, D), input_grads.reshape(MB, GROUPS, ROW, D), totals[0], totals[1], totals[2], totals[3], totals[4], totals[5], totals[6], totals[7], totals[8], totals[9], totals[10], totals[11], totals[12])
```

```python
import math

import jax
import jax.numpy as jnp
from jax import lax
from jax.sharding import PartitionSpec as P

HEADS = 4
HD = 256
WINDOW = 512
EPS = 1e-06
LANES = 128

BF = jnp.bfloat16
F32 = jnp.float32
BOTH = ("dp", "seq")


def dot(left, right, dims=((1,), (0,))):
    return lax.dot_general(left, right, (dims, ((), ())), preferred_element_type=F32)


NT = ((1,), (1,))
TN = ((0,), (0,))


def rms(values, gain):
    scale = lax.rsqrt(jnp.mean(values * values, axis=-1, keepdims=True) + EPS)
    return values * scale * (1.0 + gain), scale


def rms_back(grad, values, scale, gain):
    normed = values * scale
    inner = grad * (1.0 + gain)
    back = scale * (inner - normed * jnp.mean(inner * normed, axis=-1, keepdims=True))
    return back, grad * normed


def rotate(values):
    middle = values.shape[-1] // 2
    return jnp.concatenate([-values[..., middle:], values[..., :middle]], axis=-1)


def rotate_back(values):
    middle = values.shape[-1] // 2
    return jnp.concatenate([values[..., middle:], -values[..., :middle]], axis=-1)


def xor_permute(value, bit, size):
    return lax.ppermute(value, "seq", [(i, i ^ bit) for i in range(size)])


def from_behind(value, by, size):
    pairs = [(i, i + by) for i in range(size) if 0 <= i + by < size]
    return lax.ppermute(value, "seq", pairs)


def gather_tokens(own, size):
    if size != 8:
        return lax.all_gather(own, "seq", axis=0, tiled=True)
    near = [xor_permute(own, bit, size) for bit in (2, 4, 6)]
    mine = jnp.concatenate([own] + near, axis=0)
    other = xor_permute(mine, 1, size)
    return jnp.concatenate([mine, other], axis=0)


def scatter_tokens(parts, size):
    if size != 8:
        return lax.psum_scatter(parts.astype(BF), "seq", scatter_dimension=0, tiled=True).astype(F32)
    half = parts.shape[0] // 2
    rows = half // 4
    got = xor_permute(parts[half:].astype(BF), 1, size)
    mine = parts[:half] + got.astype(F32)
    total = mine[:rows]
    for index, bit in enumerate((2, 4, 6), 1):
        block = mine[index * rows : (index + 1) * rows].astype(BF)
        total = total + xor_permute(block, bit, size).astype(F32)
    return total


def shards(
    dp,
    seq,
    layer_input,
    out_cotangent,
    seq_lengths,
    inputnorm,
    queryproj,
    keyproj,
    valueproj,
    querynorm,
    keynorm,
    outproj,
    attnnorm,
    prefeednorm,
    gateproj,
    upproj,
    downproj,
    postfeednorm,
):
    micro, _, rows, width = layer_input.shape
    devices = dp * seq
    wrows = width // devices
    qd = queryproj.shape[1]
    ff = gateproj.shape[1]
    chunk = ff // devices
    own_ff = dp * chunk
    pad_ff = -(-own_ff // LANES) * LANES
    reach = WINDOW // rows
    keys_rows = (reach + 1) * rows

    short = querynorm.shape[0]
    gains = jnp.stack(
        [
            inputnorm,
            attnnorm,
            prefeednorm,
            postfeednorm,
            jnp.pad(querynorm, (0, wrows - short)),
            jnp.pad(keynorm, (0, wrows - short)),
        ],
        axis=1,
    )
    packed = jnp.concatenate(
        [queryproj, keyproj, valueproj, jnp.pad(gains, ((0, 0), (0, LANES - 6)))], axis=1
    )
    gathered = lax.all_gather(packed, BOTH, axis=0, tiled=True)
    w_in = gathered[:, : qd + 2 * HD]
    gain_rows = gathered[:, qd + 2 * HD :].astype(F32).T
    g_in, g_attn, g_pre, g_post = (gain_rows[i] for i in range(4))
    g_query = gain_rows[4].reshape(devices, wrows)[:, :short].reshape(HD)
    g_keys = gain_rows[5].reshape(devices, wrows)[:, :short].reshape(HD)
    w_out = lax.all_gather(outproj, BOTH, axis=0, tiled=True)

    def by_owner(shard):
        cut = shard.reshape(wrows, dp, seq, chunk).transpose(2, 0, 1, 3).reshape(seq, wrows, own_ff)
        return jnp.pad(cut, ((0, 0), (0, 0), (0, pad_ff - own_ff)))

    gate_up = jnp.concatenate([by_owner(gateproj), by_owner(upproj)], axis=2)
    gate_up = lax.all_to_all(gate_up, "seq", 0, 0)
    w_gu = lax.all_gather(gate_up.reshape(seq * wrows, 2 * pad_ff), "dp", axis=0, tiled=True)
    w_gate = w_gu[:, :pad_ff]
    w_up = w_gu[:, pad_ff:]
    w_down = lax.all_gather(downproj, "dp", axis=0, tiled=True)
    w_down = jnp.pad(w_down, ((0, pad_ff - own_ff), (0, 0)))

    base = lax.axis_index("seq") * rows
    query_pos = base + jnp.arange(rows, dtype=jnp.int32)
    keys_pos = base - reach * rows + jnp.arange(keys_rows, dtype=jnp.int32)
    counter = jnp.arange(HD // 2, dtype=F32)
    inverse = jnp.power(F32(10000.0), -2.0 * counter / HD)

    def heads_forward(raw, gain, cosine, sine, factor):
        view = raw.reshape(raw.shape[0], -1, HD)
        normed, scale = rms(view, gain)
        turned = normed * cosine[:, None, :] + rotate(normed) * sine[:, None, :]
        return (turned * factor).reshape(raw.shape).astype(BF), scale

    def heads_backward(grad, raw, scale, gain, cosine, sine, factor):
        view = raw.reshape(raw.shape[0], -1, HD)
        grad = grad.reshape(view.shape) * factor
        grad = grad * cosine[:, None, :] + rotate_back(grad * sine[:, None, :])
        back, terms = rms_back(grad, view, scale, gain)
        return back.reshape(raw.shape).astype(BF), jnp.sum(terms, axis=(0, 1))

    def to_heads(values):
        return values.reshape(rows, HEADS, HD).transpose(1, 0, 2).reshape(HEADS * rows, HD)

    def from_heads(values):
        return values.reshape(HEADS, rows, HD).transpose(1, 0, 2).reshape(rows, HEADS * HD)

    states = []
    for index in range(micro):
        length = seq_lengths[index, 0, 0]
        relative = query_pos & (length - 1)
        same = (keys_pos & -length)[None, :] == (query_pos & -length)[:, None]
        behind = query_pos[:, None] - keys_pos[None, :]
        allowed = same & (behind >= 0) & (behind < WINDOW)
        mask = jnp.tile(allowed, (HEADS, 1))
        angles = relative.astype(F32)[:, None] * inverse[None, :]
        cosine = jnp.concatenate([jnp.cos(angles)] * 2, -1)
        sine = jnp.concatenate([jnp.sin(angles)] * 2, -1)
        value_in = layer_input[index, 0].astype(F32)
        normed32, scale_in = rms(value_in, g_in)
        normed_in = normed32.astype(BF)
        raw = dot(normed_in, w_in)
        raw_q = raw[:, :qd]
        raw_k = raw[:, qd : qd + HD]
        value_low = raw[:, qd + HD :].astype(BF)
        query_low, scale_q = heads_forward(raw_q, g_query, cosine, sine, 1.0 / math.sqrt(HD))
        keys_low, scale_k = heads_forward(raw_k, g_keys, cosine, sine, 1.0)
        pair = jnp.concatenate([keys_low, value_low], axis=1)
        arrived = [from_behind(pair, by, seq) for by in range(reach, 0, -1)]
        pairs = jnp.concatenate(arrived + [pair], axis=0)
        keys_all = pairs[:, :HD]
        values_all = pairs[:, HD:]
        query_heads = to_heads(query_low)
        scores = jnp.where(mask, dot(query_heads, keys_all, NT), -1e30)
        top = jnp.max(scores, axis=-1, keepdims=True)
        lse = top + jnp.log(jnp.sum(jnp.exp(scores - top), axis=-1, keepdims=True))
        probs = jnp.exp(scores - lse).astype(BF)
        attended = from_heads(dot(probs, values_all)).astype(BF)
        attn_out = dot(attended, w_out)
        post_attn, scale_attn = rms(attn_out, g_attn)
        hidden = value_in + post_attn
        normed_ffn, scale_pre = rms(hidden, g_pre)
        states.append(
            dict(
                mask=mask, cosine=cosine, sine=sine, value_in=value_in, scale_in=scale_in, normed_in=normed_in,
                raw_q=raw_q, raw_k=raw_k, scale_q=scale_q, scale_k=scale_k, keys_all=keys_all, values_all=values_all,
                query_heads=query_heads, lse=lse, attended=attended, attn_out=attn_out, scale_attn=scale_attn,
                hidden=hidden, scale_pre=scale_pre, normed_ffn=normed_ffn.astype(BF),
            )
        )

    outputs = []
    for index in range(micro):
        s = states[index]
        s["tokens"] = gather_tokens(s["normed_ffn"], seq)
        s["gate"] = dot(s["tokens"], w_gate)
        s["up"] = dot(s["tokens"], w_up)
        s["act"] = (jax.nn.gelu(s["gate"], approximate=True) * s["up"]).astype(BF)
        ffn_out = scatter_tokens(dot(s["act"], w_down), seq)
        post, scale_post = rms(ffn_out, g_post)
        outputs.append(s["hidden"] + post)
        s["dy"] = out_cotangent[index, 0].astype(F32)
        d_ffn, s["t_post"] = rms_back(s["dy"], ffn_out, scale_post, g_post)
        s["d_ffn"] = d_ffn.astype(BF)

    in_grads = []
    for index in range(micro):
        s = states[index]
        s["d_tokens"] = gather_tokens(s["d_ffn"], seq)
        d_act = dot(s["d_tokens"], w_down, NT)
        _, back = jax.vjp(lambda a, b: jax.nn.gelu(a, approximate=True) * b, s["gate"], s["up"])
        d_gate, d_up = back(d_act)
        s["d_gate"] = d_gate.astype(BF)
        s["d_up"] = d_up.astype(BF)
        d_normed = scatter_tokens(dot(s["d_gate"], w_gate, NT) + dot(s["d_up"], w_up, NT), seq)
        d_hidden, s["t_pre"] = rms_back(d_normed, s["hidden"], s["scale_pre"], g_pre)
        d_hidden = s["dy"] + d_hidden
        d_attn, s["t_attn"] = rms_back(d_hidden, s["attn_out"], s["scale_attn"], g_attn)
        s["d_attn"] = d_attn.astype(BF)
        d_heads = to_heads(dot(s["d_attn"], w_out, NT).astype(BF))
        scores = jnp.where(s["mask"], dot(s["query_heads"], s["keys_all"], NT), -1e30)
        probs = jnp.exp(scores - s["lse"])
        d_probs = dot(d_heads, s["values_all"], NT)
        inner = jnp.sum(probs * d_probs, axis=-1, keepdims=True)
        d_scores = (probs * (d_probs - inner)).astype(BF)
        d_query = from_heads(dot(d_scores, s["keys_all"]))
        d_pairs = jnp.concatenate(
            [dot(d_scores, s["query_heads"], TN), dot(probs.astype(BF), d_heads, TN)], axis=1
        )
        own = d_pairs[reach * rows :]
        for by in range(1, reach + 1):
            start = (reach - by) * rows
            own = own + from_behind(d_pairs[start : start + rows].astype(BF), -by, seq).astype(F32)
        d_raw_q, s["t_query"] = heads_backward(
            d_query, s["raw_q"], s["scale_q"], g_query, s["cosine"], s["sine"], 1.0 / math.sqrt(HD)
        )
        d_raw_k, s["t_keys"] = heads_backward(
            own[:, :HD], s["raw_k"], s["scale_k"], g_keys, s["cosine"], s["sine"], 1.0
        )
        s["d_raw"] = jnp.concatenate([d_raw_q, d_raw_k, own[:, HD:].astype(BF)], axis=1)
        d_normed_in = dot(s["d_raw"], w_in, NT)
        d_in, s["t_in"] = rms_back(d_normed_in, s["value_in"], s["scale_in"], g_in)
        in_grads.append(d_hidden + d_in)

    def over_micro(left, right):
        return dot(
            jnp.concatenate([s[left] for s in states], axis=0),
            jnp.concatenate([s[right] for s in states], axis=0),
            TN,
        )

    down_terms = over_micro("act", "d_tokens")[:own_ff].astype(BF)
    down_grad = lax.psum_scatter(down_terms, "dp", scatter_dimension=0, tiled=True).astype(F32)

    gu_terms = jnp.concatenate([over_micro("tokens", "d_gate"), over_micro("tokens", "d_up")], axis=1).astype(BF)
    gu_sum = lax.psum_scatter(gu_terms, "dp", scatter_dimension=0, tiled=True)
    gu_sum = lax.all_to_all(gu_sum.reshape(seq, wrows, 2 * pad_ff), "seq", 0, 0)

    def to_columns(part):
        cut = part[:, :, :own_ff].reshape(seq, wrows, dp, chunk).transpose(1, 2, 0, 3)
        return cut.reshape(wrows, ff).astype(F32)

    gate_grad = to_columns(gu_sum[:, :, :pad_ff])
    up_grad = to_columns(gu_sum[:, :, pad_ff:])

    out_grad = lax.psum_scatter(
        over_micro("attended", "d_attn").astype(BF), BOTH, scatter_dimension=0, tiled=True
    ).astype(F32)

    def summed(name):
        return sum(jnp.sum(s[name], axis=0) for s in states)

    def spread(vector):
        return jnp.pad(vector.reshape(devices, short), ((0, 0), (0, wrows - short))).reshape(width)

    gain_terms = jnp.stack(
        [summed("t_in"), summed("t_attn"), summed("t_pre"), summed("t_post")]
        + [spread(sum(s[name] for s in states)) for name in ("t_query", "t_keys")],
        axis=0,
    )
    gain_cols = jnp.pad(gain_terms, ((0, LANES - 6), (0, 0))).T
    in_terms = jnp.concatenate([over_micro("normed_in", "d_raw"), gain_cols], axis=1).astype(BF)
    in_sum = lax.psum_scatter(in_terms.reshape(devices, wrows, -1), BOTH, scatter_dimension=0, tiled=True)
    in_sum = in_sum.reshape(wrows, -1).astype(F32)
    gain_sum = in_sum[:, qd + 2 * HD :]

    return (
        jnp.stack(outputs)[:, None],
        jnp.stack(in_grads)[:, None],
        gain_sum[:, 0],
        in_sum[:, :qd],
        in_sum[:, qd : qd + HD],
        in_sum[:, qd + HD : qd + 2 * HD],
        gain_sum[:short, 4],
        gain_sum[:short, 5],
        out_grad,
        gain_sum[:, 1],
        gain_sum[:, 2],
        gate_grad,
        up_grad,
        down_grad,
        gain_sum[:, 3],
    )


def solution(mesh):
    dp, seq = mesh.shape["dp"], mesh.shape["seq"]
    acts = P(None, "dp", "seq", None)
    vector = P(BOTH)
    matrix = P(BOTH, None)

    def run(*args):
        return shards(dp, seq, *args)

    return jax.shard_map(
        run,
        mesh=mesh,
        in_specs=(acts, acts, P(None, "dp", None), vector)
        + (matrix,) * 3
        + (vector,) * 2
        + (matrix, vector, vector)
        + (matrix,) * 3
        + (vector,),
        out_specs=(acts, acts, vector) + (matrix,) * 3 + (vector,) * 2 + (matrix, vector, vector) + (matrix,) * 3 + (vector,),
        check_vma=False,
    )
```

```python
import functools
import math

import jax
import jax.numpy as jnp
from jax import lax
from jax.experimental import pallas as pl
from jax.experimental.pallas import tpu as pltpu
from jax.sharding import PartitionSpec as P

HEADS = 4
HD = 256
HALF = HD // 2
WINDOW = 512
EPS = 1e-06
LANES = 128
FACTOR = 1.0 / math.sqrt(HD)
GELU_C = math.sqrt(2.0 / math.pi)
NEG = -1e30

BF = jnp.bfloat16
F32 = jnp.float32
BOTH = ("dp", "seq")
NN = ((1,), (0,))
NT = ((1,), (1,))
TN = ((0,), (0,))


def dot(left, right, dims=NN):
    return lax.dot_general(left, right, (dims, ((), ())), preferred_element_type=F32)


def shape(dims, dtype):
    return jax.ShapeDtypeStruct(dims, dtype)


def whole(array):
    return pl.BlockSpec(array.shape, lambda *_: (0,) * array.ndim)


def call(body, grid, inputs, outs, scratch=(), aliases=None, name=None):
    return pl.pallas_call(
        body,
        **({} if grid is None else {"grid": grid}),
        in_specs=[spec for _, spec in inputs],
        out_specs=[spec for _, spec in outs],
        out_shape=[made for made, _ in outs],
        scratch_shapes=list(scratch),
        input_output_aliases=aliases or {},
        compiler_params=pltpu.CompilerParams(vmem_limit_bytes=58 * 2**20),
        cost_estimate=pl.CostEstimate(flops=0, bytes_accessed=1, transcendentals=0),
        name=name,
    )(*[array for array, _ in inputs])


def scale_of(values):
    return lax.rsqrt(jnp.mean(values * values, axis=-1, keepdims=True) + EPS)


def rms(values, gain):
    return values * scale_of(values) * (1.0 + gain)


def rms_back(grad, values, gain):
    scale = scale_of(values)
    normed = values * scale
    inner = grad * (1.0 + gain)
    back = scale * (inner - normed * jnp.mean(inner * normed, axis=-1, keepdims=True))
    return back, jnp.sum(grad * normed, axis=0, keepdims=True)


def turn(values, cosine, sine):
    first, second = values[:, :HALF], values[:, HALF:]
    return jnp.concatenate([first * cosine - second * sine, second * cosine + first * sine], axis=1)


def turn_back(grad, cosine, sine):
    first, second = grad[:, :HALF], grad[:, HALF:]
    return jnp.concatenate([first * cosine + second * sine, second * cosine - first * sine], axis=1)


def gelu_parts(value):
    inner = GELU_C * (value + 0.044715 * value * value * value)
    tanh = jnp.tanh(inner)
    gelu = 0.5 * value * (1.0 + tanh)
    slope = 0.5 * (1.0 + tanh) + 0.5 * value * (1.0 - tanh * tanh) * GELU_C * (1.0 + 3 * 0.044715 * value * value)
    return gelu, slope


def spots(short, wrows, width):
    row = lax.broadcasted_iota(jnp.int32, (width, HD), 0)
    entry = lax.broadcasted_iota(jnp.int32, (width, HD), 1)
    bits = short.bit_length() - 1
    return (row == (entry >> bits) * wrows + (entry & (short - 1))).astype(F32).astype(BF)


def project_kernel(
    short, wrows, x_ref, w_ref, packed_ref, cos_ref, sin_ref, normed_ref, raw_ref, q_ref, pair_ref, gains_ref
):
    qd = q_ref.shape[-1]
    width = x_ref.shape[-1]
    gains_ref[...] = jnp.transpose(packed_ref[...].astype(F32))[:8]
    heads = dot(packed_ref[...], spots(short, wrows, width), TN)
    gains_ref[4:6, :HD] = heads[4:6]
    g_q, g_k = heads[4:5], heads[5:6]
    normed = rms(x_ref[0, 0].astype(F32), gains_ref[0:1]).astype(BF)
    normed_ref[0] = normed
    raw = dot(normed, w_ref[...])
    raw_ref[0] = raw[:, : qd + HD]
    cosine, sine = cos_ref[0], sin_ref[0]
    for head in range(qd // HD):
        at = slice(head * HD, (head + 1) * HD)
        q_ref[0, :, at] = (turn(rms(raw[:, at], g_q), cosine, sine) * FACTOR).astype(BF)
    keys = turn(rms(raw[:, qd : qd + HD], g_k), cosine, sine)
    pair_ref[0, :, :HD] = keys.astype(BF)
    pair_ref[0, :, HD:] = raw[:, qd + HD :].astype(BF)


def masks_of(rows, reach, place):
    length, base = place[0], place[1]
    query = lax.broadcasted_iota(jnp.int32, (rows, rows), 0)
    keys = lax.broadcasted_iota(jnp.int32, (rows, rows), 1)
    first = base & -length
    masks = []
    for by in range(reach + 1):
        behind = query - keys + by * rows
        valid = jnp.where(base - by * rows >= first, WINDOW, -1)
        masks.append((behind >= 0) & (behind < valid))
    return masks


def probs_of(query, pairs, masks):
    scores = [jnp.where(m, dot(query, p[:, :HD], NT), NEG) for p, m in zip(pairs, masks)]
    top = functools.reduce(jnp.maximum, [jnp.max(s, axis=-1, keepdims=True) for s in scores])
    raised = [jnp.exp(s - top) for s in scores]
    total = functools.reduce(jnp.add, [jnp.sum(e, axis=-1, keepdims=True) for e in raised])
    return [e * (1.0 / total) for e in raised]


def attend_kernel(reach, place, x_ref, q_ref, *rest):
    pairs_refs, (w_out, gains, att_ref, out_ref, hidden_ref, nf_ref) = rest[: reach + 1], rest[reach + 1 :]
    pairs = [p[...].reshape(p.shape[-2:]) for p in pairs_refs]
    masks = masks_of(pairs[0].shape[0], reach, place)
    qd = q_ref.shape[-1]
    for head in range(qd // HD):
        at = slice(head * HD, (head + 1) * HD)
        probs = probs_of(q_ref[0, :, at], pairs, masks)
        mixed = sum(dot(p.astype(BF), v[:, HD:]) for p, v in zip(probs, pairs))
        att_ref[:, at] = mixed.astype(BF)
    out = dot(att_ref[...], w_out[...])
    out_ref[...] = out
    hidden = x_ref[0, 0].astype(F32) + rms(out, gains[1:2])
    hidden_ref[...] = hidden
    nf_ref[...] = rms(hidden, gains[2:3]).astype(BF)


def gelu_gate(gate, up):
    return 0.5 * gate * (1.0 + jnp.tanh(GELU_C * (gate + 0.044715 * gate * gate * gate))) * up


def ffn_rows(tokens, w_gu, w_down, store):
    total = None
    for half, (gu, down) in enumerate(zip(w_gu, w_down)):
        pad = down.shape[0]
        both = dot(tokens, gu[...])
        gate, up = both[:, :pad], both[:, pad:]
        act = gelu_gate(gate, up).astype(BF)
        store(half, gate.astype(BF), up.astype(BF), act)
        part = dot(act, down[...])
        total = part if total is None else total + part
    return total.astype(BF)


def ffn_back_rows(tokens, kept, w_gu, w_down, store):
    total = None
    for half, (gu, down) in enumerate(zip(w_gu, w_down)):
        gate, up = kept(half)
        d_act = dot(tokens, down[...], NT)
        gelu, slope = gelu_parts(gate.astype(F32))
        d_gate = (d_act * up.astype(F32) * slope).astype(BF)
        d_up = (d_act * gelu).astype(BF)
        store(half, d_gate, d_up)
        pad = down.shape[0]
        part = dot(d_gate, gu[:, :pad], NT) + dot(d_up, gu[:, pad:], NT)
        total = part if total is None else total + part
    return total.astype(BF)


def ffn_grid_kernel(halves, t_ref, *refs):
    w_gu, w_down, refs = refs[:halves], refs[halves : 2 * halves], refs[2 * halves :]

    def store(half, *values):
        for kind, value in enumerate(values):
            refs[kind * halves + half][...] = value

    refs[-1][...] = ffn_rows(t_ref[...], w_gu, w_down, store)


def ffn_back_grid_kernel(halves, t_ref, *refs):
    gates, ups, w_gu, w_down = (refs[i * halves : (i + 1) * halves] for i in range(4))
    refs = refs[4 * halves :]

    def store(half, *values):
        for kind, value in enumerate(values):
            refs[kind * halves + half][...] = value

    kept = lambda half: (gates[half][...], ups[half][...])
    refs[-1][...] = ffn_back_rows(t_ref[...], kept, w_gu, w_down, store)


class Leaving:
    def __init__(self, sems):
        self.sems, self.copies = sems, []

    def send(self, source, target):
        copy = pltpu.make_async_copy(source, target, self.sems.at[len(self.copies)])
        copy.start()
        self.copies.append(copy)

    def wait(self):
        for copy in self.copies:
            copy.wait()


def ffn_kernel(count, halves, *refs):
    tokens, refs = refs[:count], refs[count:]
    w_gu, w_down, refs = refs[:halves], refs[halves : 2 * halves], refs[2 * halves :]
    t_out, outs, parts = refs[0], refs[1 : 1 + 3 * halves], refs[1 + 3 * halves : 1 + 3 * halves + count]
    buffers, sems = refs[1 + 3 * halves + count : -1], refs[-1]
    leaving = Leaving(sems)
    rows = tokens[0].shape[0]
    for index in range(count):
        at = pl.ds(index * rows, rows)
        leaving.send(tokens[index], t_out.at[at])

        def store(half, *values):
            for kind, value in enumerate(values):
                slot = kind * halves + half
                buffers[slot][at] = value
                leaving.send(buffers[slot].at[at], outs[slot].at[at])

        parts[index][...] = ffn_rows(tokens[index][...], w_gu, w_down, store)
    leaving.wait()


def ffn_back_kernel(count, halves, *refs):
    tokens, refs = refs[:count], refs[count:]
    gates, ups, w_gu, w_down = (refs[i * halves : (i + 1) * halves] for i in range(4))
    t_out, refs = refs[4 * halves], refs[4 * halves + 1 :]
    outs, parts = refs[: 2 * halves], refs[2 * halves : 2 * halves + count]
    kept_in, buffers, sems, in_sems = refs[2 * halves + count : -2 - 2 * halves], refs[-2 - 2 * halves : -2], refs[-2], refs[-1]
    leaving = Leaving(sems)
    rows = tokens[0].shape[0]
    arriving = {}
    for index in range(count):
        at = pl.ds(index * rows, rows)
        for half in range(halves):
            for kind, source in enumerate((gates[half], ups[half])):
                slot = kind * halves + half
                copy = pltpu.make_async_copy(source.at[at], kept_in[slot].at[at], in_sems.at[index * 2 * halves + slot])
                copy.start()
                arriving[index, slot] = copy
    for index in range(count):
        at = pl.ds(index * rows, rows)
        leaving.send(tokens[index], t_out.at[at])

        def kept(half):
            for slot in (half, halves + half):
                arriving[index, slot].wait()
            return kept_in[half][at], kept_in[halves + half][at]

        def store(half, *values):
            for kind, value in enumerate(values):
                slot = kind * halves + half
                buffers[slot][at] = value
                leaving.send(buffers[slot].at[at], outs[slot].at[at])

        parts[index][...] = ffn_back_rows(tokens[index][...], kept, w_gu, w_down, store)
    leaving.wait()


def untangle_kernel(dp, seq, place, *refs):
    lines, (in_ref, out_ref) = refs[:-2], refs[-2:]
    columns = in_ref.shape[1]
    in_rows, out_rows = in_ref.shape[0] // (dp * seq), out_ref.shape[0] // (dp * seq)

    def body(me):
        for index, ref in enumerate(lines):
            at = me ^ (index % 4 * 2) ^ (index // 4)
            for d in range(dp):
                start, to = d * in_rows, d * seq + at
                in_ref[to * in_rows : (to + 1) * in_rows] = ref[start : start + in_rows, :columns]
                out_ref[to * out_rows : (to + 1) * out_rows] = ref[start : start + out_rows, columns:]

    on_value(place[0], seq, body)


def pad_kernel(in_ref, out_ref):
    rows = in_ref.shape[0]
    out_ref[:rows] = in_ref[...]
    out_ref[rows:] = jnp.zeros((out_ref.shape[0] - rows, out_ref.shape[1]), out_ref.dtype)


def join_kernel(*refs):
    pieces, out, sems = refs[:-2], refs[-2], refs[-1]
    rows = pieces[0].shape[0]
    copies = []
    for index, piece in enumerate(pieces):
        copies.append(pltpu.make_async_copy(piece, out.at[pl.ds(index * rows, rows)], sems.at[index]))
        copies[-1].start()
    for copy in copies:
        copy.wait()


def owner_kernel(dp, gate_ref, up_ref, out_ref):
    seq, rows, columns = out_ref.shape
    pad = columns // 2
    chunk = gate_ref.shape[1] // (dp * seq)
    zeros = [] if pad == dp * chunk else [jnp.zeros((rows, pad - dp * chunk), BF)]
    for to in range(seq):
        for half, ref in enumerate((gate_ref, up_ref)):
            cuts = [ref[:, (d * seq + to) * chunk : (d * seq + to + 1) * chunk] for d in range(dp)]
            out_ref[to, :, half * pad : (half + 1) * pad] = jnp.concatenate(cuts + zeros, axis=1)


def columns_kernel(dp, in_ref, out_ref):
    seq = in_ref.shape[0]
    chunk = out_ref.shape[1] // (dp * seq)
    for d in range(dp):
        for at in range(seq):
            start = (d * seq + at) * chunk
            out_ref[:, start : start + chunk] = in_ref[at, :, d * chunk : (d + 1) * chunk].astype(F32)


def add_up(refs):
    total = refs[0][...].astype(F32)
    for ref in refs[1:]:
        total = total + ref[...].astype(F32)
    return total


def middle_kernel(count, chained, *refs):
    parts, (dy_ref, hidden_ref, gains), (out_ref, d_ref, t_ref) = refs[:count], refs[count : count + 3], refs[-3:]
    g_post = gains[3:4]
    ffn_out = add_up(parts)
    out_ref[0, 0] = hidden_ref[...] + rms(ffn_out, g_post)
    back, terms = rms_back(dy_ref[0, 0].astype(F32), ffn_out, g_post)
    d_ref[...] = back.astype(BF)
    t_ref[...] = terms


def attend_back_kernel(reach, count, place, *refs):
    parts, refs = refs[:count], refs[count:]
    dy_ref, hidden_ref, out_ref, q_ref, raw_ref, cos_ref, sin_ref, w_out, gains = refs[:9]
    pairs_refs, refs = refs[9 : 10 + reach], refs[10 + reach :]
    g_attn, g_pre, g_q = gains[1:2], gains[2:3], gains[4:5, :HD]
    dh_ref, da_ref, dq_ref, t_pre, t_attn, t_q = refs[:6]
    back_refs, own_ref, sums = refs[6 : 6 + reach], refs[6 + reach], refs[7 + reach :]
    d_hidden, terms = rms_back(add_up(parts), hidden_ref[...], g_pre)
    t_pre[...] = terms
    d_hidden = d_hidden + dy_ref[0, 0].astype(F32)
    dh_ref[...] = d_hidden
    d_attn, terms = rms_back(d_hidden, out_ref[...], g_attn)
    t_attn[...] = terms
    d_attn = d_attn.astype(BF)
    da_ref[...] = d_attn
    d_heads = dot(d_attn, w_out[...], NT).astype(BF)
    pairs = [p[...].reshape(p.shape[-2:]) for p in pairs_refs]
    masks = masks_of(pairs[0].shape[0], reach, place)
    into = (own_ref,) + tuple(sums)
    total_q = None
    for head in range(q_ref.shape[-1] // HD):
        at = slice(head * HD, (head + 1) * HD)
        query, d_head = q_ref[0, :, at], d_heads[:, at]
        probs = probs_of(query, pairs, masks)
        d_probs = [dot(d_head, p[:, HD:], NT) for p in pairs]
        inner = sum(jnp.sum(p * d, axis=-1, keepdims=True) for p, d in zip(probs, d_probs))
        d_scores = [(p * (d - inner)).astype(BF) for p, d in zip(probs, d_probs)]
        d_query = sum(dot(d, p[:, :HD]) for d, p in zip(d_scores, pairs))
        for ref, d, p in zip(into, d_scores, probs):
            d_keys = dot(d, query, TN)
            d_value = dot(p.astype(BF), d_head, TN)
            if head == 0:
                ref[:, :HD] = d_keys
                ref[:, HD:] = d_value
            else:
                ref[:, :HD] += d_keys
                ref[:, HD:] += d_value
        d_turned = turn_back(d_query * FACTOR, cos_ref[0], sin_ref[0])
        back, terms = rms_back(d_turned, raw_ref[0, :, at], g_q)
        dq_ref[:, at] = back.astype(BF)
        total_q = terms if total_q is None else total_q + terms
    t_q[...] = total_q
    for ref, value in zip(back_refs, sums):
        ref[...] = value[...].astype(BF)


def project_back_kernel(count, chained, *refs):
    parts, refs = refs[:count], refs[count:]
    raw_ref, dq_ref, cos_ref, sin_ref, w_ref, x_ref, dh_ref, gains = refs[:8]
    g_in, g_k = gains[0:1], gains[5:6, :HD]
    in_ref, d_ref, t_in, t_k = refs[-4:]
    qd = dq_ref.shape[-1]
    own = add_up(parts)
    d_turned = turn_back(own[:, :HD], cos_ref[0], sin_ref[0])
    back, terms = rms_back(d_turned, raw_ref[0], g_k)
    t_k[...] = terms
    d_ref[:, :qd] = dq_ref[...]
    d_ref[:, qd : qd + HD] = back.astype(BF)
    d_ref[:, qd + HD :] = own[:, HD:].astype(BF)
    d_normed = dot(d_ref[...], w_ref[...], NT)
    back, terms = rms_back(d_normed, x_ref[0, 0].astype(F32), g_in)
    t_in[...] = terms
    in_ref[0, 0] = dh_ref[...] + back


def weights_kernel(short, wrows, micro, core, *refs):
    normed, d_raw, terms = refs[0], refs[1 : 1 + micro], refs[1 + micro : 1 + 7 * micro]
    mine, other, total = refs[1 + 7 * micro :]
    width = normed.shape[-1]
    ind = d_raw[0].shape[-1]
    weights = None
    for index in range(micro):
        term = dot(normed[index], d_raw[index][...], TN)
        weights = term if weights is None else weights + term
    total[:, :ind] = weights
    sums = []
    for kind in range(6):
        value = terms[kind * micro][...]
        for index in range(1, micro):
            value = value + terms[kind * micro + index][...]
        sums.append(value)
    place = spots(short, wrows, width)
    heads = [dot(jnp.broadcast_to(s, (8, HD)).astype(BF), place, NT)[:1] for s in sums[4:]]
    rows = jnp.concatenate(sums[:4] + heads + [jnp.zeros((LANES - 6, width), F32)], axis=0)
    total[:, ind:] = jnp.transpose(rows)
    odd = core[0] == 1
    for index in range(mine.shape[0] // wrows):
        at = slice(index * wrows, (index + 1) * wrows)
        first = total[2 * index * wrows : (2 * index + 1) * wrows]
        second = total[(2 * index + 1) * wrows : (2 * index + 2) * wrows]
        mine[at] = jnp.where(odd, second, first).astype(BF)
        other[at] = jnp.where(odd, first, second).astype(BF)


def on_value(scalar, count, body):
    for value in range(count):

        @pl.when(scalar == value)
        def _(value=value):
            body(value)


def line_kernel(place, *refs):
    blocks, out = refs[:-1], refs[-1]
    count, rows = len(blocks), blocks[0].shape[1]

    def body(d):
        for by, ref in enumerate(blocks):
            at = (d - by) % count
            out[at * rows : (at + 1) * rows] = ref[0]

    on_value(place[0], count, body)


def terms_kernel(count, kinds, has_got, *refs):
    lefts, rights, refs = refs[:count], refs[count : count + count * kinds], refs[count + count * kinds :]
    gots, outs = refs[: kinds if has_got else 0], refs[-kinds:]
    for kind in range(kinds):
        total = None
        for left, right in zip(lefts, rights[kind * count :]):
            term = dot(left[...], right[...], TN)
            total = term if total is None else total + term
        total = total[: outs[kind].shape[0]]
        if has_got:
            total = total + gots[kind][...].astype(F32)
        outs[kind][...] = total.astype(BF)


def fold_chips_kernel(dp, place, mine, got, line, *sends):
    chips = len(sends) + 1
    rows = line.shape[0] // dp

    def body(chip):
        for index in range(dp):
            for bit in range(chips):
                start = (index * chips + (chip ^ bit)) * rows
                value = mine[start : start + rows].astype(F32) + got[start : start + rows].astype(F32)
                at = slice(index * rows, (index + 1) * rows)
                if bit:
                    sends[bit - 1][at] = value.astype(BF)
                else:
                    line[at] = value

    on_value(place[0], chips, body)


def fold_line_kernel(dp, count, place, *refs):
    parts, (own, *sends) = refs[:count], refs[count:]
    rows = own.shape[0]

    def body(d):
        for by in range(dp):
            start = (d + by) % dp * rows
            value = parts[0][start : start + rows]
            for part in parts[1:]:
                value = value + part[start : start + rows].astype(F32)
            if by:
                sends[by - 1][...] = value.astype(BF)
            else:
                own[...] = value

    on_value(place[0], dp, body)


def finish_kernel(count, *refs):
    parts, outs = refs[:count], refs[count:]
    total = add_up(parts)
    start = 0
    for out in outs[:-1]:
        out[...] = total[:, start : start + out.shape[1]]
        start += out.shape[1]
    outs[-1][...] = jnp.transpose(total[:, start:])[:8]


def after(value, *others):
    return lax.optimization_barrier((value,) + others)[0]


def xor_permute(value, bit, size):
    return lax.ppermute(value, "seq", [(i, i ^ bit) for i in range(size)])


def from_behind(value, by, size):
    pairs = [(i, i + by) for i in range(size) if 0 <= i + by < size]
    return lax.ppermute(value, "seq", pairs)


def near_blocks(own, size):
    return [xor_permute(own, bit, size) for bit in (2, 4, 6)]


class Order:
    def __init__(self):
        self.last = None

    def behind(self, value):
        return value if self.last is None else after(value, self.last)

    def step(self, value):
        self.last = value
        return value


def around(value, by, dp):
    return lax.ppermute(value, "dp", [(i, (i + by) % dp) for i in range(dp)])


def along(value, by, dp):
    return lax.ppermute(value, "dp", [(i, i + by) for i in range(dp) if 0 <= i + by < dp])


def add_up_arrays(parts):
    return functools.reduce(lambda a, b: a + b.astype(F32), parts[1:], parts[0])


VMEM = pl.BlockSpec(memory_space=pltpu.VMEM)
SMEM = pl.BlockSpec(memory_space=pltpu.SMEM)


def plain(array):
    return (array, VMEM)


def fold_chips(mine, got, dp, seq, order):
    dims = (mine.shape[0] * 2 // seq, mine.shape[1])
    chip = order.behind((lax.axis_index("seq") >> 1).reshape(1))
    line, *sends = call(
        functools.partial(fold_chips_kernel, dp),
        None,
        [(chip, SMEM), plain(mine), plain(got)],
        [(shape(dims, F32), VMEM)] + [(shape(dims, BF), VMEM)] * 3,
        name="fold_chips",
    )
    order.step(sends)
    return [line] + [xor_permute(send, bit, seq) for send, bit in zip(sends, (2, 4, 6))]


def fold_line(parts, dp, order):
    dims = (parts[0].shape[0] // dp, parts[0].shape[1])
    place = order.behind(lax.axis_index("dp").reshape(1))
    own, *sends = call(
        functools.partial(fold_line_kernel, dp, len(parts)),
        None,
        [(place, SMEM)] + [plain(part) for part in parts],
        [(shape(dims, F32), VMEM)] + [(shape(dims, BF), VMEM)] * (dp - 1),
        name="fold_line",
    )
    order.step(sends)
    return [own] + [around(send, by, dp) for by, send in enumerate(sends, 1)]


def shards(
    dp,
    seq,
    layer_input,
    out_cotangent,
    seq_lengths,
    inputnorm,
    queryproj,
    keyproj,
    valueproj,
    querynorm,
    keynorm,
    outproj,
    attnnorm,
    prefeednorm,
    gateproj,
    upproj,
    downproj,
    postfeednorm,
):
    micro, _, rows, width = layer_input.shape
    devices = dp * seq
    wrows = width // devices
    qd = queryproj.shape[1]
    ind = qd + 2 * HD
    ff = gateproj.shape[1]
    chunk = ff // devices
    own_ff = dp * chunk
    pad = -(-own_ff // LANES) * LANES
    reach = WINDOW // rows
    split = seq == 8 and dp == 4

    base = lax.axis_index("seq") * rows
    positions = base + jnp.arange(rows, dtype=jnp.int32)
    inverse = jnp.power(F32(10000.0), -2.0 * jnp.arange(HALF, dtype=F32) / HD)
    lengths = seq_lengths[:, 0, 0]
    relative = positions[None, :] & (lengths[:, None] - 1)
    angles = relative.astype(F32)[:, :, None] * inverse
    cosine, sine = jnp.cos(angles), jnp.sin(angles)

    order = Order()
    short = querynorm.shape[0]
    fill = (0, wrows - short)
    gains = [inputnorm, attnnorm, prefeednorm, postfeednorm, jnp.pad(querynorm, fill), jnp.pad(keynorm, fill)]
    gains = jnp.pad(jnp.stack(gains, axis=1), ((0, 0), (0, LANES - len(gains))))
    packed = jnp.concatenate([queryproj, keyproj, valueproj, gains], axis=1)
    along_dp = lax.axis_index("dp").reshape(1)
    if split:
        orows = outproj.shape[0]
        both = jnp.concatenate([packed, jnp.pad(outproj, ((0, wrows - orows), (0, 0)))], axis=1)
        both = order.step(lax.optimization_barrier(both[None]))
        line = [around(both, by, dp) for by in range(1, dp)]

    [gate_up] = call(
        functools.partial(owner_kernel, dp),
        None,
        [plain(gateproj), plain(upproj)],
        [(shape((seq, wrows, 2 * pad), BF), VMEM)],
        name="owner",
    )
    w_down = lax.all_gather(downproj, "dp", axis=0, tiled=True)
    if split:
        gate_up, cosine, sine, line[0] = order.step(order.behind((gate_up, cosine, sine, line[0])))
    gate_up = lax.all_to_all(gate_up, "seq", 0, 0).reshape(seq * wrows, 2 * pad)
    if split:
        [line] = call(
            line_kernel,
            None,
            [(along_dp, SMEM)] + [plain(block) for block in [both] + order.behind(line)],
            [(shape((dp * wrows, both.shape[2]), BF), VMEM)],
            name="line",
        )
        lines = [line] + near_blocks(order.step(line), seq)
        lines = order.step(order.behind(lines))
        others = [xor_permute(line, 1, seq) for line in lines]
        others, w_down = order.step(order.behind((others, w_down)))
        w_in, w_out = call(
            functools.partial(untangle_kernel, dp, seq),
            None,
            [(lax.axis_index("seq").reshape(1), SMEM)] + [plain(line) for line in lines + others],
            [(shape((width, ind + LANES), BF), VMEM), (shape((qd, width), BF), VMEM)],
            name="untangle",
        )
    else:
        w_in = lax.all_gather(packed[None], BOTH, axis=0, tiled=True).reshape(width, -1)
        w_out = lax.all_gather(outproj, BOTH, axis=0, tiled=True)
    w_gu = [lax.all_gather(gate_up, "dp", axis=0, tiled=True)]
    [w_down] = call(
        pad_kernel, None, [plain(order.behind(w_down))], [(shape((pad, width), BF), VMEM)], name="pad"
    )
    w_down = [order.step(w_down)]
    if split:
        w_down = order.step(order.behind(w_down + [xor_permute(w_down[0], 1, seq)]))

    def of_micro(array, index):
        dims = array.shape[1:]
        return (array, pl.BlockSpec((1,) + dims, lambda *_: (index,) + (0,) * len(dims)))

    def full(array):
        return (array, whole(array))

    def new(dims, dtype):
        return (shape(dims, dtype), pl.BlockSpec(dims, lambda *_: (0,) * len(dims)))

    smem = pl.BlockSpec(memory_space=pltpu.SMEM)
    each = lambda *dims: pl.BlockSpec((1,) + dims, lambda i: (i,) + (0,) * len(dims))
    w_in_spec = pl.BlockSpec((width, ind), lambda *_: (0, 0))

    cosine = order.behind(cosine)
    gains_spec = pl.BlockSpec((width, LANES), lambda *_: (0, ind // LANES))
    normed_in, raw, query, pair, gains = call(
        functools.partial(project_kernel, short, wrows),
        (micro,),
        [(layer_input, each(1, rows, width)), (w_in, w_in_spec), (w_in, gains_spec)]
        + [(cosine, each(rows, HALF)), (sine, each(rows, HALF))],
        [
            (shape((micro, rows, width), BF), each(rows, width)),
            (shape((micro, rows, qd + HD), F32), each(rows, qd + HD)),
            (shape((micro, rows, qd), BF), each(rows, qd)),
            (shape((micro, rows, 2 * HD), BF), each(rows, 2 * HD)),
            new((8, width), F32),
        ],
        name="project",
    )

    order.step(pair)
    behind = [from_behind(pair, by, seq) for by in range(1, reach + 1)]
    states = []
    for index in range(micro):
        place = order.behind(jnp.stack([lengths[index], base]))
        pairs = [of_micro(p, index) for p in [pair] + behind]
        attended, attn_out, hidden, normed_ffn = call(
            functools.partial(attend_kernel, reach),
            (1,),
            [(place, smem), of_micro(layer_input, index), of_micro(query, index)]
            + pairs
            + [full(w_out), full(gains)],
            [new((rows, qd), BF), new((rows, width), F32), new((rows, width), F32), new((rows, width), BF)],
            name="attend",
        )
        order.step(normed_ffn)
        s = dict(place=place, pairs=pairs, attended=attended, attn_out=attn_out, hidden=hidden)
        s["sent"] = near_blocks(normed_ffn, seq) if split else None
        s["nf"] = normed_ffn
        states.append(s)

    if split:
        states[0]["sent"] = order.step(order.behind(states[0]["sent"]))
        w_gu.append(xor_permute(order.step(order.behind(w_gu[0])), 1, seq))
    halves = len(w_gu)

    def blocks(array):
        return (array, pl.BlockSpec((rows, array.shape[1]), lambda i: (i, 0)))

    def made(count, columns):
        return (shape((count, columns), BF), pl.BlockSpec((rows, columns), lambda i: (i, 0)))

    def fixed(array):
        return (array, pl.BlockSpec(array.shape, lambda *_: (0,) * array.ndim, pipeline_mode=pl.Buffered(1)))

    def block(index_of, columns):
        return pl.BlockSpec((rows, columns), index_of)

    any_spec = pl.BlockSpec(memory_space=pl.ANY)

    def ffn(pieces):
        if not split:
            count = pieces[0].shape[0] // rows
            results = call(
                functools.partial(ffn_grid_kernel, halves),
                (count,),
                [blocks(pieces[0])] + [fixed(w) for w in w_gu] + [fixed(w) for w in w_down],
                [made(count * rows, pad)] * 3 + [made(count * rows, width)],
                name="ffn",
            )
            return pieces[0], results[:1], results[1:2], results[2:3], results[3:]
        count = len(pieces)
        results = call(
            functools.partial(ffn_kernel, count, halves),
            None,
            [plain(array) for array in pieces + list(w_gu) + list(w_down)],
            [(shape((count * rows, width), BF), any_spec)]
            + [(shape((count * rows, pad), BF), any_spec)] * (3 * halves)
            + [(shape((rows, width), BF), VMEM)] * count,
            scratch=[pltpu.VMEM((count * rows, pad), BF)] * (3 * halves)
            + [pltpu.SemaphoreType.DMA((count * (1 + 3 * halves),))],
            name="ffn",
        )
        kinds = [results[1 + i * halves : 1 + (i + 1) * halves] for i in range(3)]
        return results[0], *kinds, results[1 + 3 * halves :]

    def ffn_backward(pieces, gate, up):
        if not split:
            count = pieces[0].shape[0] // rows
            results = call(
                functools.partial(ffn_back_grid_kernel, halves),
                (count,),
                [blocks(pieces[0]), *map(blocks, gate), *map(blocks, up)]
                + [fixed(w) for w in w_gu]
                + [fixed(w) for w in w_down],
                [made(count * rows, pad)] * 2 + [made(count * rows, width)],
                name="ffn_back",
            )
            return pieces[0], results[:1], results[1:2], results[2:]
        count = len(pieces)
        results = call(
            functools.partial(ffn_back_kernel, count, halves),
            None,
            [plain(piece) for piece in pieces]
            + [(array, any_spec) for array in [*gate, *up]]
            + [plain(array) for array in list(w_gu) + list(w_down)],
            [(shape((count * rows, width), BF), any_spec)]
            + [(shape((count * rows, pad), BF), any_spec)] * (2 * halves)
            + [(shape((rows, width), BF), VMEM)] * count,
            scratch=[pltpu.VMEM((count * rows, pad), BF)] * (4 * halves)
            + [pltpu.SemaphoreType.DMA((count * (1 + 2 * halves),)), pltpu.SemaphoreType.DMA((count * 2 * halves,))],
            name="ffn_back",
        )
        return results[0], results[1 : 1 + halves], results[1 + halves : 1 + 2 * halves], results[1 + 2 * halves :]

    def pieces_of(own, near):
        if not split:
            return [lax.all_gather(order.behind(own), "seq", axis=0, tiled=True)]
        return [order.behind(own)] + list(near)

    def scatter(parts):
        if not split:
            return [lax.psum_scatter(parts[0], "seq", scatter_dimension=0, tiled=True)]
        return [parts[0]] + [xor_permute(part, bit, seq) for part, bit in zip(parts[1:], (2, 4, 6))]

    for s in states:
        pieces = pieces_of(s["nf"], s["sent"])
        s["tokens"], s["gate"], s["up"], s["act"], parts = ffn(pieces)
        order.step(parts)
        s["terms"] = scatter(parts)

    layer_out = None
    result = shape((micro, 1, rows, width), F32)
    for index, s in enumerate(states):
        parts = s["terms"]
        chain = [] if layer_out is None else [(layer_out, pl.BlockSpec(memory_space=pl.ANY))]
        layer_out, s["d_ffn"], s["t_post"] = call(
            functools.partial(middle_kernel, len(parts), bool(chain)),
            (1,),
            [full(p) for p in parts]
            + [of_micro(out_cotangent, index), full(s["hidden"]), full(order.behind(gains))]
            + chain,
            [(result, of_micro(result, index)[1]), new((rows, width), BF), new((1, width), F32)],
            aliases={len(parts) + 3: 0} if chain else None,
            name="middle",
        )
        order.step(s["d_ffn"])
        s["sent"] = near_blocks(s["d_ffn"], seq) if split else None

    def join(pieces):
        [joined] = call(
            join_kernel,
            None,
            [(piece, any_spec) for piece in pieces],
            [(shape((len(pieces) * rows, width), BF), any_spec)],
            scratch=[pltpu.SemaphoreType.DMA((len(pieces),))],
            name="join",
        )
        return joined

    def over_tokens(left, rights, half, gots=(), high_out=None):
        of = lambda s, name: s[name] if name in ("tokens", "d_tokens") else s[name][half]
        lefts = order.behind([of(s, left) for s in states])
        others = [of(s, right) for right in rights for s in states]
        count, high, wide = lefts[0].shape[0], lefts[0].shape[1], others[0].shape[1]
        by_rows = high % 384 == 0
        moving = lambda columns: pl.BlockSpec((count, columns), lambda i: (0, i))
        staying = lambda columns: pl.BlockSpec((count, columns), lambda i: (0, 0), pipeline_mode=pl.Buffered(1))
        if by_rows:
            steps, left_spec, right_spec = high // 384, moving(384), staying(wide)
            out_spec = pl.BlockSpec((384, wide), lambda i: (i, 0))
        else:
            steps, left_spec, right_spec = wide // 384, staying(high), moving(384)
            out_spec = pl.BlockSpec((high_out or high, 384), lambda i: (0, i))
        results = call(
            functools.partial(terms_kernel, micro, len(rights), bool(gots)),
            (steps,),
            [(a, left_spec) for a in lefts] + [(b, right_spec) for b in others] + [(got, out_spec) for got in gots],
            [(shape((high_out or high, wide), BF), out_spec)] * len(rights),
            name="terms",
        )
        return order.step(results)

    def weight_terms(left, rights, high_out=None, meanwhile=None):
        if not split:
            if meanwhile is not None:
                meanwhile()
            yield from over_tokens(left, rights, 0, (), high_out)
            return
        others = over_tokens(left, rights, 1, (), high_out)
        if meanwhile is not None:
            meanwhile()
            others = order.behind(others)
        gots = [xor_permute(other, 1, seq) for other in others]
        if meanwhile is not None:
            attend_back(micro - 1)
        for right, got in zip(rights, gots):
            yield over_tokens(left, [right], 0, [got], high_out)[0]

    def ffn_back(s):
        pieces = pieces_of(s["d_ffn"], s["sent"])
        tokens, s["d_gate"], s["d_up"], parts = ffn_backward(pieces, s["gate"], s["up"])
        s.setdefault("d_tokens", tokens)
        order.step(parts)
        s["terms"] = scatter(parts)

    for s in states[:-1]:
        ffn_back(s)
    late = states[-1]
    if split:
        late["sent"] = order.step(order.behind(late["sent"]))
        late["d_tokens"] = order.step(join([late["d_ffn"]] + list(late["sent"])))
        down_terms = next(weight_terms("act", ["d_tokens"], own_ff))
        ffn_back(late)
    else:
        ffn_back(late)
        down_terms = next(weight_terms("act", ["d_tokens"], own_ff))
    down_grad = lax.psum_scatter(down_terms, "dp", scatter_dimension=0, tiled=True)
    for s in states[:-1]:
        s["terms"] = order.step(order.behind(s["terms"]))

    def attend_back(index):
        s = states[index]
        parts = s["terms"]
        backs = call(
            functools.partial(attend_back_kernel, reach, len(parts)),
            (1,),
            [(order.behind(s["place"]), smem)]
            + [full(p) for p in parts]
            + [of_micro(out_cotangent, index), full(s["hidden"]), full(s["attn_out"]), of_micro(query, index)]
            + [of_micro(raw, index), of_micro(cosine, index), of_micro(sine, index)]
            + [full(w_out), full(gains)]
            + s["pairs"],
            [new((rows, width), F32), new((rows, width), BF), new((rows, qd), BF)]
            + [new((1, width), F32), new((1, width), F32), new((1, HD), F32)]
            + [new((rows, 2 * HD), BF)] * reach
            + [new((rows, 2 * HD), F32)],
            scratch=[pltpu.VMEM((rows, 2 * HD), F32)] * reach,
            name="attend_back",
        )
        s["d_hidden"], s["d_attn"], s["d_raw_q"], s["t_pre"], s["t_attn"], s["t_query"] = backs[:6]
        order.step(s["d_attn"])
        sent, own = backs[6 : 6 + reach], backs[-1]
        s["d_pairs"] = [own] + [from_behind(value, -by, seq) for by, value in enumerate(sent, 1)]

    def project_back(index, input_grad):
        s = states[index]
        terms = s["d_pairs"]
        chain = [] if input_grad is None else [(input_grad, pl.BlockSpec(memory_space=pl.ANY))]
        keys_spec = pl.BlockSpec((1, rows, HD), lambda *_: (index, 0, qd // HD))
        input_grad, s["d_raw"], s["t_in"], s["t_keys"] = call(
            functools.partial(project_back_kernel, len(terms), bool(chain)),
            (1,),
            [full(t) for t in terms]
            + [(raw, keys_spec), full(s["d_raw_q"]), of_micro(cosine, index), of_micro(sine, index), (w_in, w_in_spec)]
            + [of_micro(layer_input, index), full(s["d_hidden"]), full(order.behind(gains))]
            + chain,
            [(result, of_micro(result, index)[1]), new((rows, ind), BF), new((1, width), F32), new((1, HD), F32)],
            aliases={len(terms) + 8: 0} if chain else None,
            name="project_back",
        )
        order.step(s["d_raw"])
        s["normed_in"] = normed_in[index]
        return input_grad

    def to_columns(part):
        part = lax.all_to_all(part.reshape(seq, wrows, pad), "seq", 0, 0)
        [columns] = call(
            functools.partial(columns_kernel, dp),
            None,
            [plain(part)],
            [(shape((wrows, ff), F32), VMEM)],
            name="columns",
        )
        return columns

    input_grad = None
    scattered = lambda terms: lax.psum_scatter(terms, "dp", scatter_dimension=0, tiled=True)
    def meanwhile():
        for index in range(micro - 1):
            attend_back(index)
        nonlocal down_grad
        down_grad, states[-1]["terms"] = order.step(order.behind((down_grad, states[-1]["terms"])))

    gate_up_terms = weight_terms("tokens", ["d_gate", "d_up"], None, meanwhile)
    gate_sum = scattered(next(gate_up_terms))
    if not split:
        attend_back(micro - 1)
    core = lax.axis_index("seq") & 1
    out_terms = order.step(sum(dot(s["attended"], order.behind(s["d_attn"]), TN) for s in states).astype(BF))
    if split:
        view = out_terms.reshape(devices // 2, 2, qd // devices, width)
        mine, other = (
            lax.dynamic_index_in_dim(view, at.astype(jnp.uint32), 1, keepdims=False).reshape(-1, width)
            for at in (core, 1 - core)
        )
        got = xor_permute(other, 1, seq)
    input_grad = project_back(micro - 1, input_grad)
    if split:
        out_parts = fold_chips(mine, got, dp, seq, order)
    else:
        out_grad = lax.psum_scatter(out_terms, BOTH, scatter_dimension=0, tiled=True).astype(F32)
    for index in range(micro - 1):
        input_grad = project_back(index, input_grad)
    up_sum = scattered(next(gate_up_terms))
    if split:
        out_parts = fold_line(out_parts, dp, order)
    sums = [s[name] for name in ("t_in", "t_attn", "t_pre", "t_post", "t_query", "t_keys") for s in states]
    half_out = (shape((devices // 2 * wrows, ind + LANES), BF), VMEM)
    mine, other = call(
        functools.partial(weights_kernel, short, wrows, micro),
        None,
        [(order.behind((core if split else jnp.int32(0)).reshape(1)), smem), plain(normed_in)]
        + [plain(s["d_raw"]) for s in states]
        + [plain(term) for term in sums],
        [half_out, half_out],
        scratch=[pltpu.VMEM((width, ind + LANES), F32)],
        name="weights",
    )
    order.step(other)
    if split:
        got = xor_permute(other, 1, seq)
        in_parts = fold_chips(mine, got, dp, seq, order)
        out_grad = order.step(add_up_arrays(order.behind(out_parts)))
        gate_grad = order.step(to_columns(gate_sum))
        in_parts = fold_line(in_parts, dp, order)
        up_grad = to_columns(order.behind(up_sum))
    else:
        halves_of = [part.reshape(devices // 2, wrows, -1) for part in (mine, other)]
        whole_terms = jnp.stack(halves_of, axis=1).reshape(devices, wrows, -1)
        in_parts = [lax.psum_scatter(whole_terms, BOTH, scatter_dimension=0, tiled=True)[0]]
    q_grad, k_grad, v_grad, gain_sum = call(
        functools.partial(finish_kernel, len(in_parts)),
        None,
        [plain(part) for part in in_parts],
        [(shape((wrows, columns), F32), VMEM) for columns in (qd, HD, HD)] + [(shape((8, wrows), F32), VMEM)],
        name="finish",
    )

    if not split:
        gate_grad, up_grad = to_columns(gate_sum), to_columns(up_sum)
    down_grad = order.behind(down_grad).astype(F32)

    return (
        layer_out,
        input_grad,
        gain_sum[0],
        q_grad,
        k_grad,
        v_grad,
        gain_sum[4, :short],
        gain_sum[5, :short],
        out_grad,
        gain_sum[1],
        gain_sum[2],
        gate_grad,
        up_grad,
        down_grad,
        gain_sum[3],
    )


def solution(mesh):
    dp, seq = mesh.shape["dp"], mesh.shape["seq"]
    acts = P(None, "dp", "seq", None)
    vector = P(BOTH)
    matrix = P(BOTH, None)
    weights = (vector,) + (matrix,) * 3 + (vector,) * 2 + (matrix, vector, vector) + (matrix,) * 3 + (vector,)
    return jax.shard_map(
        functools.partial(shards, dp, seq),
        mesh=mesh,
        in_specs=(acts, acts, P(None, "dp", None)) + weights,
        out_specs=(acts, acts) + weights,
        check_vma=False,
    )
```

```python
import functools
import math

import jax
import jax.numpy as jnp
from jax import lax
from jax.experimental import pallas as pl
from jax.experimental.pallas import tpu as pltpu
from jax.sharding import PartitionSpec as P

HEADS = 4
HD = 256
HALF = HD // 2
WINDOW = 512
EPS = 1e-06
LANES = 128
FACTOR = 1.0 / math.sqrt(HD)
GELU_C = math.sqrt(2.0 / math.pi)
NEG = -1e30

BF = jnp.bfloat16
F32 = jnp.float32
BOTH = ("dp", "seq")
BITS = (6, 2, 4)
NN = ((1,), (0,))
NT = ((1,), (1,))
TN = ((0,), (0,))


def dot(left, right, dims=NN):
    return lax.dot_general(left, right, (dims, ((), ())), preferred_element_type=F32)


def shape(dims, dtype):
    return jax.ShapeDtypeStruct(dims, dtype)


def whole(array):
    return pl.BlockSpec(array.shape, lambda *_: (0,) * array.ndim)


def call(body, grid, inputs, outs, scratch=(), aliases=None, name=None):
    return pl.pallas_call(
        body,
        **({} if grid is None else {"grid": grid}),
        in_specs=[spec for _, spec in inputs],
        out_specs=[spec for _, spec in outs],
        out_shape=[made for made, _ in outs],
        scratch_shapes=list(scratch),
        input_output_aliases=aliases or {},
        compiler_params=pltpu.CompilerParams(vmem_limit_bytes=58 * 2**20),
        cost_estimate=pl.CostEstimate(flops=0, bytes_accessed=1, transcendentals=0),
        name=name,
    )(*[array for array, _ in inputs])


def scale_of(values):
    return lax.rsqrt(jnp.mean(values * values, axis=-1, keepdims=True) + EPS)


def rms(values, gain):
    return values * scale_of(values) * (1.0 + gain)


def rms_back(grad, values, gain):
    scale = scale_of(values)
    normed = values * scale
    inner = grad * (1.0 + gain)
    back = scale * (inner - normed * jnp.mean(inner * normed, axis=-1, keepdims=True))
    return back, jnp.sum(grad * normed, axis=0, keepdims=True)


def turn(values, cosine, sine):
    first, second = values[:, :HALF], values[:, HALF:]
    return jnp.concatenate([first * cosine - second * sine, second * cosine + first * sine], axis=1)


def turn_back(grad, cosine, sine):
    first, second = grad[:, :HALF], grad[:, HALF:]
    return jnp.concatenate([first * cosine + second * sine, second * cosine - first * sine], axis=1)


def gelu_parts(value):
    inner = GELU_C * (value + 0.044715 * value * value * value)
    tanh = jnp.tanh(inner)
    gelu = 0.5 * value * (1.0 + tanh)
    slope = 0.5 * (1.0 + tanh) + 0.5 * value * (1.0 - tanh * tanh) * GELU_C * (1.0 + 3 * 0.044715 * value * value)
    return gelu, slope


def spots(short, wrows, width):
    row = lax.broadcasted_iota(jnp.int32, (width, HD), 0)
    entry = lax.broadcasted_iota(jnp.int32, (width, HD), 1)
    bits = short.bit_length() - 1
    return (row == (entry >> bits) * wrows + (entry & (short - 1))).astype(F32).astype(BF)


def project_kernel(
    short, wrows, x_ref, w_ref, packed_ref, cos_ref, sin_ref, normed_ref, raw_ref, q_ref, pair_ref, gains_ref
):
    qd = q_ref.shape[-1]
    width = x_ref.shape[-1]
    gains_ref[...] = jnp.transpose(packed_ref[...].astype(F32))[:8]
    heads = dot(packed_ref[...], spots(short, wrows, width), TN)
    gains_ref[4:6, :HD] = heads[4:6]
    g_q, g_k = heads[4:5], heads[5:6]
    normed = rms(x_ref[0, 0].astype(F32), gains_ref[0:1]).astype(BF)
    normed_ref[0] = normed
    raw = dot(normed, w_ref[...])
    raw_ref[0] = raw[:, : qd + HD]
    cosine, sine = cos_ref[0], sin_ref[0]
    for head in range(qd // HD):
        at = slice(head * HD, (head + 1) * HD)
        q_ref[0, :, at] = (turn(rms(raw[:, at], g_q), cosine, sine) * FACTOR).astype(BF)
    keys = turn(rms(raw[:, qd : qd + HD], g_k), cosine, sine)
    pair_ref[0, :, :HD] = keys.astype(BF)
    pair_ref[0, :, HD:] = raw[:, qd + HD :].astype(BF)


def masks_of(rows, reach, place):
    length, base = place[0], place[1]
    query = lax.broadcasted_iota(jnp.int32, (rows, rows), 0)
    keys = lax.broadcasted_iota(jnp.int32, (rows, rows), 1)
    first = base & -length
    masks = []
    for by in range(reach + 1):
        behind = query - keys + by * rows
        valid = jnp.where(base - by * rows >= first, WINDOW, -1)
        masks.append((behind >= 0) & (behind < valid))
    return masks


def probs_of(query, pairs, masks):
    scores = [jnp.where(m, dot(query, p[:, :HD], NT), NEG) for p, m in zip(pairs, masks)]
    top = functools.reduce(jnp.maximum, [jnp.max(s, axis=-1, keepdims=True) for s in scores])
    raised = [jnp.exp(s - top) for s in scores]
    total = functools.reduce(jnp.add, [jnp.sum(e, axis=-1, keepdims=True) for e in raised])
    return [e * (1.0 / total) for e in raised]


def attend_kernel(reach, place, x_ref, q_ref, *rest):
    pairs_refs, (w_out, gains, att_ref, out_ref, hidden_ref, nf_ref) = rest[: reach + 1], rest[reach + 1 :]
    pairs = [p[...].reshape(p.shape[-2:]) for p in pairs_refs]
    masks = masks_of(pairs[0].shape[0], reach, place)
    qd = q_ref.shape[-1]
    for head in range(qd // HD):
        at = slice(head * HD, (head + 1) * HD)
        probs = probs_of(q_ref[0, :, at], pairs, masks)
        mixed = sum(dot(p.astype(BF), v[:, HD:]) for p, v in zip(probs, pairs))
        att_ref[:, at] = mixed.astype(BF)
    out = dot(att_ref[...], w_out[...])
    out_ref[...] = out
    hidden = x_ref[0, 0].astype(F32) + rms(out, gains[1:2])
    hidden_ref[...] = hidden
    nf_ref[...] = rms(hidden, gains[2:3]).astype(BF)


def ffn_rows(tokens, w_gu, w_down, store):
    total = None
    for half, (gu, down) in enumerate(zip(w_gu, w_down)):
        pad = down.shape[0]
        both = dot(tokens, gu[...])
        gate, up = both[:, :pad], both[:, pad:]
        gelu, slope = gelu_parts(gate)
        act = (gelu * up).astype(BF)
        store(half, gelu.astype(BF), (up * slope).astype(BF), act)
        part = dot(act, down[...])
        total = part if total is None else total + part
    return total.astype(BF)


def ffn_back_rows(tokens, kept, w_gu, w_down, store):
    total = None
    for half, (gu, down) in enumerate(zip(w_gu, w_down)):
        gelu, rise = kept(half)
        d_act = dot(tokens, down[...], NT)
        d_gate = (d_act * rise.astype(F32)).astype(BF)
        d_up = (d_act * gelu.astype(F32)).astype(BF)
        store(half, d_gate, d_up)
        pad = down.shape[0]
        part = dot(d_gate, gu[:, :pad], NT) + dot(d_up, gu[:, pad:], NT)
        total = part if total is None else total + part
    return total.astype(BF)


def ffn_grid_kernel(halves, t_ref, *refs):
    w_gu, w_down, refs = refs[:halves], refs[halves : 2 * halves], refs[2 * halves :]

    def store(half, *values):
        for kind, value in enumerate(values):
            refs[kind * halves + half][...] = value

    refs[-1][...] = ffn_rows(t_ref[...], w_gu, w_down, store)


def ffn_back_grid_kernel(halves, t_ref, *refs):
    gelus, rises, w_gu, w_down = (refs[i * halves : (i + 1) * halves] for i in range(4))
    refs = refs[4 * halves :]

    def store(half, *values):
        for kind, value in enumerate(values):
            refs[kind * halves + half][...] = value

    kept = lambda half: (gelus[half][...], rises[half][...])
    refs[-1][...] = ffn_back_rows(t_ref[...], kept, w_gu, w_down, store)


class Leaving:
    def __init__(self, sems):
        self.sems, self.copies = sems, []

    def send(self, source, target):
        copy = pltpu.make_async_copy(source, target, self.sems.at[len(self.copies)])
        copy.start()
        self.copies.append(copy)

    def wait(self):
        for copy in self.copies:
            copy.wait()


class Weights:
    def __init__(self, sources, buffers, sems):
        self.buffers = buffers
        self.copies = []
        for index, (source, buffer) in enumerate(zip(sources, buffers)):
            self.copies.append(pltpu.make_async_copy(source, buffer, sems.at[index]))
        self.used = [False] * len(self.copies)

    def start(self, index):
        self.copies[index].start()

    def __getitem__(self, index):
        if not self.used[index]:
            self.copies[index].wait()
            self.used[index] = True
        return self.buffers[index]


class Lazy:
    def __init__(self, weights, index):
        self.weights, self.index = weights, index

    @property
    def shape(self):
        return self.weights.buffers[self.index].shape

    def __getitem__(self, at):
        return self.weights[self.index][at]


def lazy_weights(sources, buffers, sems, halves, first):
    weights = Weights(sources, buffers, sems)
    for half in range(halves):
        for kind in first:
            weights.start(kind * halves + half)
    return [Lazy(weights, half) for half in range(halves)], [Lazy(weights, halves + half) for half in range(halves)]


def ffn_kernel(count, halves, *refs):
    tokens, refs = refs[:count], refs[count:]
    sources, refs = refs[: 2 * halves], refs[2 * halves :]
    t_out, outs, parts = refs[0], refs[1 : 1 + 3 * halves], refs[1 + 3 * halves : 1 + 3 * halves + count]
    refs = refs[1 + 3 * halves + count :]
    buffers, w_buffers, sems, w_sems = refs[: 3 * halves], refs[3 * halves : -2], refs[-2], refs[-1]
    w_gu, w_down = lazy_weights(sources, w_buffers, w_sems, halves, (0, 1))
    leaving = Leaving(sems)
    rows = tokens[0].shape[0]
    for index in range(count):
        at = pl.ds(index * rows, rows)
        leaving.send(tokens[index], t_out.at[at])

        def store(half, *values):
            for kind, value in enumerate(values):
                slot = kind * halves + half
                buffers[slot][at] = value
                leaving.send(buffers[slot].at[at], outs[slot].at[at])

        parts[index][...] = ffn_rows(tokens[index][...], w_gu, w_down, store)
    leaving.wait()


def ffn_back_kernel(count, halves, *refs):
    tokens, refs = refs[:count], refs[count:]
    gelus, rises, sources = refs[:halves], refs[halves : 2 * halves], refs[2 * halves : 4 * halves]
    t_out, refs = refs[4 * halves], refs[4 * halves + 1 :]
    outs, parts = refs[: 2 * halves], refs[2 * halves : 2 * halves + count]
    refs = refs[2 * halves + count :]
    kept_in, buffers, w_buffers = (refs[i * 2 * halves : (i + 1) * 2 * halves] for i in range(3))
    sems, in_sems, w_sems = refs[6 * halves :]
    w_gu, w_down = lazy_weights(sources, w_buffers, w_sems, halves, (1, 0))
    leaving = Leaving(sems)
    rows = tokens[0].shape[0]
    arriving = {}
    for index in range(count):
        at = pl.ds(index * rows, rows)
        for half in range(halves):
            for kind, source in enumerate((gelus[half], rises[half])):
                slot = kind * halves + half
                copy = pltpu.make_async_copy(source.at[at], kept_in[slot].at[at], in_sems.at[index * 2 * halves + slot])
                copy.start()
                arriving[index, slot] = copy
    for index in range(count):
        at = pl.ds(index * rows, rows)
        leaving.send(tokens[index], t_out.at[at])

        def kept(half):
            for slot in (half, halves + half):
                arriving[index, slot].wait()
            return kept_in[half][at], kept_in[halves + half][at]

        def store(half, *values):
            for kind, value in enumerate(values):
                slot = kind * halves + half
                buffers[slot][at] = value
                leaving.send(buffers[slot].at[at], outs[slot].at[at])

        parts[index][...] = ffn_back_rows(tokens[index][...], kept, w_gu, w_down, store)
    leaving.wait()


def untangle_kernel(dp, seq, place, *refs):
    lines, out = refs[:-1], refs[-1]
    rows = out.shape[0] // (dp * seq)

    def body(me):
        for index, ref in enumerate(lines):
            at = me ^ (index % 4 * 2) ^ (index // 4)
            for d in range(dp):
                start, to = d * rows, (d * seq + at) * rows
                out[to : to + rows] = ref[start : start + rows]

    on_value(place[0], seq, body)


def pad_kernel(in_ref, out_ref):
    rows = in_ref.shape[0]
    out_ref[:rows] = in_ref[...]
    out_ref[rows:] = jnp.zeros((out_ref.shape[0] - rows, out_ref.shape[1]), out_ref.dtype)


def join_kernel(*refs):
    rows = refs[0].shape[0]
    for index, ref in enumerate(refs[:-1]):
        refs[-1][index * rows : (index + 1) * rows] = ref[...]


def owner_kernel(dp, gate_ref, up_ref, out_ref):
    seq, rows, columns = out_ref.shape
    pad = columns // 2
    chunk = gate_ref.shape[1] // (dp * seq)
    zeros = [] if pad == dp * chunk else [jnp.zeros((rows, pad - dp * chunk), BF)]
    for to in range(seq):
        for half, ref in enumerate((gate_ref, up_ref)):
            cuts = [ref[:, (d * seq + to) * chunk : (d * seq + to + 1) * chunk] for d in range(dp)]
            out_ref[to, :, half * pad : (half + 1) * pad] = jnp.concatenate(cuts + zeros, axis=1)


def columns_kernel(dp, in_ref, out_ref):
    seq = in_ref.shape[0]
    chunk = out_ref.shape[1] // (dp * seq)
    for d in range(dp):
        for at in range(seq):
            start = (d * seq + at) * chunk
            out_ref[:, start : start + chunk] = in_ref[at, :, d * chunk : (d + 1) * chunk].astype(F32)


def add_up(refs):
    total = refs[0][...].astype(F32)
    for ref in refs[1:]:
        total = total + ref[...].astype(F32)
    return total


def middle_kernel(count, chained, *refs):
    parts, (dy_ref, hidden_ref, gains), (out_ref, d_ref, t_ref) = refs[:count], refs[count : count + 3], refs[-3:]
    g_post = gains[3:4]
    ffn_out = add_up(parts)
    out_ref[0, 0] = hidden_ref[...] + rms(ffn_out, g_post)
    back, terms = rms_back(dy_ref[0, 0].astype(F32), ffn_out, g_post)
    d_ref[...] = back.astype(BF)
    t_ref[...] = terms


def attend_back_kernel(reach, count, place, *refs):
    parts, refs = refs[:count], refs[count:]
    dy_ref, hidden_ref, out_ref, q_ref, raw_ref, cos_ref, sin_ref, w_out, gains = refs[:9]
    pairs_refs, refs = refs[9 : 10 + reach], refs[10 + reach :]
    g_attn, g_pre, g_q = gains[1:2], gains[2:3], gains[4:5, :HD]
    dh_ref, da_ref, dq_ref, t_pre, t_attn, t_q = refs[:6]
    back_refs, own_ref, sums = refs[6 : 6 + reach], refs[6 + reach], refs[7 + reach :]
    d_hidden, terms = rms_back(add_up(parts), hidden_ref[...], g_pre)
    t_pre[...] = terms
    d_hidden = d_hidden + dy_ref[0, 0].astype(F32)
    dh_ref[...] = d_hidden
    d_attn, terms = rms_back(d_hidden, out_ref[...], g_attn)
    t_attn[...] = terms
    d_attn = d_attn.astype(BF)
    da_ref[...] = d_attn
    d_heads = dot(d_attn, w_out[...], NT).astype(BF)
    pairs = [p[...].reshape(p.shape[-2:]) for p in pairs_refs]
    masks = masks_of(pairs[0].shape[0], reach, place)
    into = (own_ref,) + tuple(sums)
    total_q = None
    for head in range(q_ref.shape[-1] // HD):
        at = slice(head * HD, (head + 1) * HD)
        query, d_head = q_ref[0, :, at], d_heads[:, at]
        probs = probs_of(query, pairs, masks)
        d_probs = [dot(d_head, p[:, HD:], NT) for p in pairs]
        inner = sum(jnp.sum(p * d, axis=-1, keepdims=True) for p, d in zip(probs, d_probs))
        d_scores = [(p * (d - inner)).astype(BF) for p, d in zip(probs, d_probs)]
        d_query = sum(dot(d, p[:, :HD]) for d, p in zip(d_scores, pairs))
        for ref, d, p in zip(into, d_scores, probs):
            d_keys = dot(d, query, TN)
            d_value = dot(p.astype(BF), d_head, TN)
            if head == 0:
                ref[:, :HD] = d_keys
                ref[:, HD:] = d_value
            else:
                ref[:, :HD] += d_keys
                ref[:, HD:] += d_value
        d_turned = turn_back(d_query * FACTOR, cos_ref[0], sin_ref[0])
        back, terms = rms_back(d_turned, raw_ref[0, :, at], g_q)
        dq_ref[:, at] = back.astype(BF)
        total_q = terms if total_q is None else total_q + terms
    t_q[...] = total_q
    for ref, value in zip(back_refs, sums):
        ref[...] = value[...].astype(BF)


def project_back_kernel(count, chained, *refs):
    parts, refs = refs[:count], refs[count:]
    raw_ref, dq_ref, cos_ref, sin_ref, w_ref, x_ref, dh_ref, gains = refs[:8]
    g_in, g_k = gains[0:1], gains[5:6, :HD]
    in_ref, d_ref, t_in, t_k = refs[-4:]
    qd = dq_ref.shape[-1]
    own = add_up(parts)
    d_turned = turn_back(own[:, :HD], cos_ref[0], sin_ref[0])
    back, terms = rms_back(d_turned, raw_ref[0], g_k)
    t_k[...] = terms
    d_ref[:, :qd] = dq_ref[...]
    d_ref[:, qd : qd + HD] = back.astype(BF)
    d_ref[:, qd + HD :] = own[:, HD:].astype(BF)
    d_normed = dot(d_ref[...], w_ref[...], NT)
    back, terms = rms_back(d_normed, x_ref[0, 0].astype(F32), g_in)
    t_in[...] = terms
    in_ref[0, 0] = dh_ref[...] + back


def weights_kernel(short, wrows, micro, core, *refs):
    attended, d_attn, refs = refs[:micro], refs[micro : 2 * micro], refs[2 * micro :]
    normed, d_raw, terms = refs[0], refs[1 : 1 + micro], refs[1 + micro : 1 + 7 * micro]
    mine, other, total, out_total = refs[1 + 7 * micro :]
    out_weights = None
    for left, right in zip(attended, d_attn):
        term = dot(left[...], right[...], TN)
        out_weights = term if out_weights is None else out_weights + term
    out_total[...] = out_weights
    orows = out_total.shape[0] // (2 * (mine.shape[0] // wrows))
    width = normed.shape[-1]
    ind = d_raw[0].shape[-1]
    weights = None
    for index in range(micro):
        term = dot(normed[index], d_raw[index][...], TN)
        weights = term if weights is None else weights + term
    total[:, :ind] = weights
    sums = []
    for kind in range(6):
        value = terms[kind * micro][...]
        for index in range(1, micro):
            value = value + terms[kind * micro + index][...]
        sums.append(value)
    place = spots(short, wrows, width)
    heads = [dot(jnp.broadcast_to(s, (8, HD)).astype(BF), place, NT)[:1] for s in sums[4:]]
    rows = jnp.concatenate(sums[:4] + heads + [jnp.zeros((LANES - 6, width), F32)], axis=0)
    total[:, ind:] = jnp.transpose(rows)
    odd = core[0] == 1
    for index in range(mine.shape[0] // wrows):
        at = slice(index * wrows, (index + 1) * wrows)
        first = total[2 * index * wrows : (2 * index + 1) * wrows]
        second = total[(2 * index + 1) * wrows : (2 * index + 2) * wrows]
        columns = first.shape[1]
        mine[at, :columns] = jnp.where(odd, second, first).astype(BF)
        other[at, :columns] = jnp.where(odd, first, second).astype(BF)
        first = out_total[2 * index * orows : (2 * index + 1) * orows]
        second = out_total[(2 * index + 1) * orows : (2 * index + 2) * orows]
        at = slice(index * wrows, index * wrows + orows)
        mine[at, columns:] = jnp.where(odd, second, first).astype(BF)
        other[at, columns:] = jnp.where(odd, first, second).astype(BF)
        if orows < wrows:
            rest = slice(index * wrows + orows, (index + 1) * wrows)
            for ref in (mine, other):
                ref[rest, columns:] = jnp.zeros((wrows - orows, ref.shape[1] - columns), BF)


def on_value(scalar, count, body):
    for value in range(count):

        @pl.when(scalar == value)
        def _(value=value):
            body(value)


def line_kernel(place, *refs):
    blocks, (in_ref, out_ref) = refs[:-2], refs[-2:]
    count, columns = len(blocks), in_ref.shape[1]
    in_rows, out_rows = in_ref.shape[0] // count, out_ref.shape[0] // count

    def body(d):
        for by, ref in enumerate(blocks):
            at = (d - by) % count
            in_ref[at * in_rows : (at + 1) * in_rows] = ref[0, :in_rows, :columns]
            out_ref[at * out_rows : (at + 1) * out_rows] = ref[0, :out_rows, columns:]

    on_value(place[0], count, body)


def terms_kernel(count, kinds, has_got, *refs):
    lefts, rights, refs = refs[:count], refs[count : count + count * kinds], refs[count + count * kinds :]
    gots, outs = refs[: kinds if has_got else 0], refs[-kinds:]
    for kind in range(kinds):
        total = None
        for left, right in zip(lefts, rights[kind * count :]):
            term = dot(left[...], right[...], TN)
            total = term if total is None else total + term
        total = total[: outs[kind].shape[0]]
        if has_got:
            total = total + gots[kind][...].astype(F32)
        outs[kind][...] = total.astype(BF)


def fold_chips_kernel(dp, place, mine, got, line, *sends):
    chips = len(sends) + 1
    rows = line.shape[0] // dp

    def body(chip):
        for index in range(dp):
            for bit in range(chips):
                start = (index * chips + (chip ^ bit)) * rows
                value = mine[start : start + rows].astype(F32) + got[start : start + rows].astype(F32)
                at = slice(index * rows, (index + 1) * rows)
                if bit:
                    sends[bit - 1][at] = value.astype(BF)
                else:
                    line[at] = value

    on_value(place[0], chips, body)


def fold_line_kernel(dp, count, place, *refs):
    parts, (own, *sends) = refs[:count], refs[count:]
    rows = own.shape[0]

    def body(d):
        for by in range(dp):
            start = (d + by) % dp * rows
            value = parts[0][start : start + rows]
            for part in parts[1:]:
                value = value + part[start : start + rows].astype(F32)
            if by:
                sends[by - 1][...] = value.astype(BF)
            else:
                own[...] = value

    on_value(place[0], dp, body)


def finish_kernel(count, *refs):
    parts, outs = refs[:count], refs[count:]
    total = add_up(parts)
    start = 0
    for out in outs[:-2]:
        out[...] = total[:, start : start + out.shape[1]]
        start += out.shape[1]
    outs[-2][...] = jnp.transpose(total[:, start : start + LANES])[:8]
    outs[-1][...] = total[: outs[-1].shape[0], start + LANES :]


def after(value, *others):
    return lax.optimization_barrier((value,) + others)[0]


def xor_permute(value, bit, size):
    return lax.ppermute(value, "seq", [(i, i ^ bit) for i in range(size)])


def from_behind(value, by, size):
    pairs = [(i, i + by) for i in range(size) if 0 <= i + by < size]
    return lax.ppermute(value, "seq", pairs)


def near_blocks(own, size, bits=(2, 4, 6)):
    return [xor_permute(own, bit, size) for bit in bits]


class Order:
    def __init__(self):
        self.last = None

    def behind(self, value):
        return value if self.last is None else after(value, self.last)

    def step(self, value):
        self.last = value
        return value


def around(value, by, dp):
    return lax.ppermute(value, "dp", [(i, (i + by) % dp) for i in range(dp)])


def along(value, by, dp):
    return lax.ppermute(value, "dp", [(i, i + by) for i in range(dp) if 0 <= i + by < dp])


def add_up_arrays(parts):
    return functools.reduce(lambda a, b: a + b.astype(F32), parts[1:], parts[0])


VMEM = pl.BlockSpec(memory_space=pltpu.VMEM)
SMEM = pl.BlockSpec(memory_space=pltpu.SMEM)


def plain(array):
    return (array, VMEM)


def fold_chips(mine, got, dp, seq, order):
    dims = (mine.shape[0] * 2 // seq, mine.shape[1])
    chip = order.behind((lax.axis_index("seq") >> 1).reshape(1))
    line, *sends = call(
        functools.partial(fold_chips_kernel, dp),
        None,
        [(chip, SMEM), plain(mine), plain(got)],
        [(shape(dims, F32), VMEM)] + [(shape(dims, BF), VMEM)] * 3,
        name="fold_chips",
    )
    order.step(sends)
    return [line] + [xor_permute(send, bit, seq) for send, bit in zip(sends, (2, 4, 6))]


def fold_line(parts, dp, order):
    dims = (parts[0].shape[0] // dp, parts[0].shape[1])
    place = order.behind(lax.axis_index("dp").reshape(1))
    own, *sends = call(
        functools.partial(fold_line_kernel, dp, len(parts)),
        None,
        [(place, SMEM)] + [plain(part) for part in parts],
        [(shape(dims, F32), VMEM)] + [(shape(dims, BF), VMEM)] * (dp - 1),
        name="fold_line",
    )
    order.step(sends)
    return [own] + [around(send, by, dp) for by, send in enumerate(sends, 1)]


def shards(
    dp,
    seq,
    layer_input,
    out_cotangent,
    seq_lengths,
    inputnorm,
    queryproj,
    keyproj,
    valueproj,
    querynorm,
    keynorm,
    outproj,
    attnnorm,
    prefeednorm,
    gateproj,
    upproj,
    downproj,
    postfeednorm,
):
    micro, _, rows, width = layer_input.shape
    devices = dp * seq
    wrows = width // devices
    qd = queryproj.shape[1]
    ind = qd + 2 * HD
    ff = gateproj.shape[1]
    chunk = ff // devices
    own_ff = dp * chunk
    pad = -(-own_ff // LANES) * LANES
    reach = WINDOW // rows
    split = seq == 8 and dp == 4

    base = lax.axis_index("seq") * rows
    positions = base + jnp.arange(rows, dtype=jnp.int32)
    inverse = jnp.power(F32(10000.0), -2.0 * jnp.arange(HALF, dtype=F32) / HD)
    lengths = seq_lengths[:, 0, 0]
    relative = positions[None, :] & (lengths[:, None] - 1)
    angles = relative.astype(F32)[:, :, None] * inverse
    cosine, sine = jnp.cos(angles), jnp.sin(angles)

    order = Order()
    short = querynorm.shape[0]
    fill = (0, wrows - short)
    gains = [inputnorm, attnnorm, prefeednorm, postfeednorm, jnp.pad(querynorm, fill), jnp.pad(keynorm, fill)]
    gains = jnp.pad(jnp.stack(gains, axis=1), ((0, 0), (0, LANES - len(gains))))
    packed = jnp.concatenate([queryproj, keyproj, valueproj, gains], axis=1)
    along_dp = lax.axis_index("dp").reshape(1)
    if split:
        orows = outproj.shape[0]
        both = jnp.concatenate([packed, jnp.pad(outproj, ((0, wrows - orows), (0, 0)))], axis=1)
        both = order.step(lax.optimization_barrier(both[None]))
        line = [around(both, by, dp) for by in range(1, dp)]

    [gate_up] = call(
        functools.partial(owner_kernel, dp),
        None,
        [plain(gateproj), plain(upproj)],
        [(shape((seq, wrows, 2 * pad), BF), VMEM)],
        name="owner",
    )
    w_down = lax.all_gather(downproj, "dp", axis=0, tiled=True)
    gate_up = lax.all_to_all(gate_up, "seq", 0, 0).reshape(seq * wrows, 2 * pad)
    if split:
        gate_up, cosine, sine = order.step(order.behind((gate_up, cosine, sine)))
        in_line, out_line = call(
            line_kernel,
            None,
            [(along_dp, SMEM)] + [plain(block) for block in [both] + order.behind(line)],
            [(shape((dp * wrows, ind + LANES), BF), VMEM), (shape((dp * orows, width), BF), VMEM)],
            name="line",
        )

        def untangle(lines, name):
            [array] = call(
                functools.partial(untangle_kernel, dp, seq),
                None,
                [(lax.axis_index("seq").reshape(1), SMEM)] + [plain(line) for line in lines],
                [(shape((lines[0].shape[0] * seq, lines[0].shape[1]), BF), VMEM)],
                name=name,
            )
            return array

        in_lines = [in_line] + near_blocks(order.step(in_line), seq)
        in_lines = order.step(order.behind(in_lines))
        out_lines = [out_line] + near_blocks(after(out_line, in_lines), seq)
        in_lines = in_lines + [xor_permute(line, 1, seq) for line in in_lines]
        in_lines = order.step(order.behind(in_lines))
        w_in = untangle(in_lines, "untangle_in")
        order.step(w_in)
    else:
        w_in = lax.all_gather(packed[None], BOTH, axis=0, tiled=True).reshape(width, -1)
        w_out = lax.all_gather(outproj, BOTH, axis=0, tiled=True)
    w_gu = [lax.all_gather(gate_up, "dp", axis=0, tiled=True)]
    def of_micro(array, index):
        dims = array.shape[1:]
        return (array, pl.BlockSpec((1,) + dims, lambda *_: (index,) + (0,) * len(dims)))

    def full(array):
        return (array, whole(array))

    def new(dims, dtype):
        return (shape(dims, dtype), pl.BlockSpec(dims, lambda *_: (0,) * len(dims)))

    smem = pl.BlockSpec(memory_space=pltpu.SMEM)
    each = lambda *dims: pl.BlockSpec((1,) + dims, lambda i: (i,) + (0,) * len(dims))
    w_in_spec = pl.BlockSpec((width, ind), lambda *_: (0, 0))

    cosine = order.behind(cosine)
    gains_spec = pl.BlockSpec((width, LANES), lambda *_: (0, ind // LANES))
    normed_in, raw, query, pair, gains = call(
        functools.partial(project_kernel, short, wrows),
        (micro,),
        [(layer_input, each(1, rows, width)), (w_in, w_in_spec), (w_in, gains_spec)]
        + [(cosine, each(rows, HALF)), (sine, each(rows, HALF))],
        [
            (shape((micro, rows, width), BF), each(rows, width)),
            (shape((micro, rows, qd + HD), F32), each(rows, qd + HD)),
            (shape((micro, rows, qd), BF), each(rows, qd)),
            (shape((micro, rows, 2 * HD), BF), each(rows, 2 * HD)),
            new((8, width), F32),
        ],
        name="project",
    )

    order.step(pair)
    behind = [from_behind(pair, by, seq) for by in range(1, reach + 1)]
    if split:
        out_lines = order.step(order.behind(out_lines))
        out_lines = out_lines + [xor_permute(line, 1, seq) for line in out_lines]
        out_lines, w_down = order.step(order.behind((out_lines, w_down)))
        w_out = order.step(untangle(out_lines, "untangle_out"))
    [w_down] = call(
        pad_kernel, None, [plain(order.behind(w_down))], [(shape((pad, width), BF), VMEM)], name="pad"
    )
    w_down = [order.step(w_down)]
    if split:
        w_down = w_down + [xor_permute(w_down[0], 1, seq)]
    states = []
    for index in range(micro):
        place = order.behind(jnp.stack([lengths[index], base]))
        pairs = [of_micro(p, index) for p in [pair] + behind]
        attended, attn_out, hidden, normed_ffn = call(
            functools.partial(attend_kernel, reach),
            (1,),
            [(place, smem), of_micro(layer_input, index), of_micro(query, index)]
            + pairs
            + [full(w_out), full(gains)],
            [new((rows, qd), BF), new((rows, width), F32), new((rows, width), F32), new((rows, width), BF)],
            name="attend",
        )
        order.step(normed_ffn)
        s = dict(place=place, pairs=pairs, attended=attended, attn_out=attn_out, hidden=hidden)
        s["sent"] = near_blocks(normed_ffn, seq, BITS) if split else None
        s["nf"] = normed_ffn
        states.append(s)

    if split:
        states[0]["sent"] = order.step(order.behind(states[0]["sent"]))
        w_gu.append(xor_permute(order.step(order.behind(w_gu[0])), 1, seq))
    halves = len(w_gu)

    def blocks(array):
        return (array, pl.BlockSpec((rows, array.shape[1]), lambda i: (i, 0)))

    def made(count, columns):
        return (shape((count, columns), BF), pl.BlockSpec((rows, columns), lambda i: (i, 0)))

    def fixed(array):
        return (array, pl.BlockSpec(array.shape, lambda *_: (0,) * array.ndim, pipeline_mode=pl.Buffered(1)))

    def block(index_of, columns):
        return pl.BlockSpec((rows, columns), index_of)

    any_spec = pl.BlockSpec(memory_space=pl.ANY)
    w_scratch = [pltpu.VMEM((width, 2 * pad), BF)] * halves + [pltpu.VMEM((pad, width), BF)] * halves

    def ffn(pieces):
        if not split:
            count = pieces[0].shape[0] // rows
            results = call(
                functools.partial(ffn_grid_kernel, halves),
                (count,),
                [blocks(pieces[0])] + [fixed(w) for w in w_gu] + [fixed(w) for w in w_down],
                [made(count * rows, pad)] * 3 + [made(count * rows, width)],
                name="ffn",
            )
            return pieces[0], results[:1], results[1:2], results[2:3], results[3:]
        count = len(pieces)
        results = call(
            functools.partial(ffn_kernel, count, halves),
            None,
            [plain(array) for array in order.behind(pieces)] + [(w, any_spec) for w in [*w_gu, *w_down]],
            [(shape((count * rows, width), BF), any_spec)]
            + [(shape((count * rows, pad), BF), any_spec)] * (3 * halves)
            + [(shape((rows, width), BF), VMEM)] * count,
            scratch=[pltpu.VMEM((count * rows, pad), BF)] * (3 * halves)
            + w_scratch
            + [pltpu.SemaphoreType.DMA((count * (1 + 3 * halves),)), pltpu.SemaphoreType.DMA((2 * halves,))],
            name="ffn",
        )
        kinds = [results[1 + i * halves : 1 + (i + 1) * halves] for i in range(3)]
        return results[0], *kinds, results[1 + 3 * halves :]

    def ffn_backward(pieces, gelu, rise):
        if not split:
            count = pieces[0].shape[0] // rows
            results = call(
                functools.partial(ffn_back_grid_kernel, halves),
                (count,),
                [blocks(pieces[0]), *map(blocks, gelu), *map(blocks, rise)]
                + [fixed(w) for w in w_gu]
                + [fixed(w) for w in w_down],
                [made(count * rows, pad)] * 2 + [made(count * rows, width)],
                name="ffn_back",
            )
            return pieces[0], results[:1], results[1:2], results[2:]
        count = len(pieces)
        results = call(
            functools.partial(ffn_back_kernel, count, halves),
            None,
            [plain(piece) for piece in pieces]
            + [(array, any_spec) for array in [*gelu, *rise, *w_gu, *w_down]],
            [(shape((count * rows, width), BF), any_spec)]
            + [(shape((count * rows, pad), BF), any_spec)] * (2 * halves)
            + [(shape((rows, width), BF), VMEM)] * count,
            scratch=[pltpu.VMEM((count * rows, pad), BF)] * (4 * halves)
            + w_scratch
            + [pltpu.SemaphoreType.DMA((count * (1 + 2 * halves),)), pltpu.SemaphoreType.DMA((count * 2 * halves,))]
            + [pltpu.SemaphoreType.DMA((2 * halves,))],
            name="ffn_back",
        )
        return results[0], results[1 : 1 + halves], results[1 + halves : 1 + 2 * halves], results[1 + 2 * halves :]

    def pieces_of(own, near):
        if not split:
            return [lax.all_gather(order.behind(own), "seq", axis=0, tiled=True)]
        return list(near) + [order.behind(own)]

    def scatter(parts):
        if not split:
            return [lax.psum_scatter(parts[0], "seq", scatter_dimension=0, tiled=True)]
        return [parts[-1]] + [xor_permute(part, bit, seq) for part, bit in zip(parts, BITS)]

    for s in states:
        pieces = pieces_of(s["nf"], s["sent"])
        s["tokens"], s["gelu"], s["rise"], s["act"], parts = ffn(pieces)
        order.step(parts)
        s["terms"] = scatter(parts)

    layer_out = None
    result = shape((micro, 1, rows, width), F32)
    for index, s in enumerate(states):
        parts = s["terms"]
        chain = [] if layer_out is None else [(layer_out, pl.BlockSpec(memory_space=pl.ANY))]
        layer_out, s["d_ffn"], s["t_post"] = call(
            functools.partial(middle_kernel, len(parts), bool(chain)),
            (1,),
            [full(p) for p in parts]
            + [of_micro(out_cotangent, index), full(s["hidden"]), full(order.behind(gains))]
            + chain,
            [(result, of_micro(result, index)[1]), new((rows, width), BF), new((1, width), F32)],
            aliases={len(parts) + 3: 0} if chain else None,
            name="middle",
        )
        order.step(s["d_ffn"])
        s["sent"] = near_blocks(s["d_ffn"], seq, BITS) if split else None

    def join(pieces):
        [joined] = call(
            join_kernel,
            None,
            [plain(piece) for piece in pieces],
            [(shape((len(pieces) * rows, width), BF), VMEM)],
            name="join",
        )
        return joined

    def over_tokens(left, rights, half, gots=(), high_out=None):
        of = lambda s, name: s[name] if name in ("tokens", "d_tokens") else s[name][half]
        lefts = order.behind([of(s, left) for s in states])
        others = [of(s, right) for right in rights for s in states]
        count, high, wide = lefts[0].shape[0], lefts[0].shape[1], others[0].shape[1]
        by_rows = high % 384 == 0
        moving = lambda columns: pl.BlockSpec((count, columns), lambda i: (0, i))
        staying = lambda columns: pl.BlockSpec((count, columns), lambda i: (0, 0), pipeline_mode=pl.Buffered(1))
        if by_rows:
            steps, left_spec, right_spec = high // 384, moving(384), staying(wide)
            out_spec = pl.BlockSpec((384, wide), lambda i: (i, 0))
        else:
            steps, left_spec, right_spec = wide // 384, staying(high), moving(384)
            out_spec = pl.BlockSpec((high_out or high, 384), lambda i: (0, i))
        results = call(
            functools.partial(terms_kernel, micro, len(rights), bool(gots)),
            (steps,),
            [(a, left_spec) for a in lefts] + [(b, right_spec) for b in others] + [(got, out_spec) for got in gots],
            [(shape((high_out or high, wide), BF), out_spec)] * len(rights),
            name="terms",
        )
        return order.step(results)

    def other_terms(left, right, high_out=None):
        return over_tokens(left, [right], 1, (), high_out)[0] if split else None

    def own_terms(left, right, other, high_out=None):
        return over_tokens(left, [right], 0, [xor_permute(other, 1, seq)] if split else (), high_out)[0]

    def ffn_back(s):
        pieces = pieces_of(s["d_ffn"], s["sent"])
        tokens, s["d_gate"], s["d_up"], parts = ffn_backward(pieces, s["gelu"], s["rise"])
        s.setdefault("d_tokens", tokens)
        order.step(parts)
        s["terms"] = scatter(parts)

    for s in states[:-1]:
        ffn_back(s)
    late = states[-1]
    if split:
        late["sent"] = order.step(order.behind(late["sent"]))
        late["d_tokens"] = order.step(join(list(late["sent"]) + [late["d_ffn"]]))
        down_terms = own_terms("act", "d_tokens", other_terms("act", "d_tokens", own_ff), own_ff)
        ffn_back(late)
    else:
        ffn_back(late)
        down_terms = own_terms("act", "d_tokens", None, own_ff)
    down_grad = lax.psum_scatter(down_terms, "dp", scatter_dimension=0, tiled=True)
    for s in states[:-1]:
        s["terms"] = order.step(order.behind(s["terms"]))

    def attend_back(index):
        s = states[index]
        parts = s["terms"]
        backs = call(
            functools.partial(attend_back_kernel, reach, len(parts)),
            (1,),
            [(order.behind(s["place"]), smem)]
            + [full(p) for p in parts]
            + [of_micro(out_cotangent, index), full(s["hidden"]), full(s["attn_out"]), of_micro(query, index)]
            + [of_micro(raw, index), of_micro(cosine, index), of_micro(sine, index)]
            + [full(w_out), full(gains)]
            + s["pairs"],
            [new((rows, width), F32), new((rows, width), BF), new((rows, qd), BF)]
            + [new((1, width), F32), new((1, width), F32), new((1, HD), F32)]
            + [new((rows, 2 * HD), BF)] * reach
            + [new((rows, 2 * HD), F32)],
            scratch=[pltpu.VMEM((rows, 2 * HD), F32)] * reach,
            name="attend_back",
        )
        s["d_hidden"], s["d_attn"], s["d_raw_q"], s["t_pre"], s["t_attn"], s["t_query"] = backs[:6]
        order.step(s["d_attn"])
        sent, own = backs[6 : 6 + reach], backs[-1]
        s["d_pairs"] = [own] + [from_behind(value, -by, seq) for by, value in enumerate(sent, 1)]

    def project_back(index, input_grad):
        s = states[index]
        terms = s["d_pairs"]
        chain = [] if input_grad is None else [(input_grad, pl.BlockSpec(memory_space=pl.ANY))]
        keys_spec = pl.BlockSpec((1, rows, HD), lambda *_: (index, 0, qd // HD))
        input_grad, s["d_raw"], s["t_in"], s["t_keys"] = call(
            functools.partial(project_back_kernel, len(terms), bool(chain)),
            (1,),
            [full(t) for t in terms]
            + [(raw, keys_spec), full(s["d_raw_q"]), of_micro(cosine, index), of_micro(sine, index), (w_in, w_in_spec)]
            + [of_micro(layer_input, index), full(s["d_hidden"]), full(order.behind(gains))]
            + chain,
            [(result, of_micro(result, index)[1]), new((rows, ind), BF), new((1, width), F32), new((1, HD), F32)],
            aliases={len(terms) + 8: 0} if chain else None,
            name="project_back",
        )
        order.step(s["d_raw"])
        s["normed_in"] = normed_in[index]
        return input_grad

    def columns_of(part, index):
        [columns] = call(
            functools.partial(columns_kernel, dp),
            (1,),
            [(part, pl.BlockSpec((seq, wrows, pad), lambda *_: (0, 0, index)))],
            [(shape((wrows, ff), F32), pl.BlockSpec((wrows, ff), lambda *_: (0, 0)))],
            name="columns",
        )
        return columns

    def to_columns(part):
        return columns_of(lax.all_to_all(part.reshape(seq, wrows, pad), "seq", 0, 0), 0)

    input_grad = None
    scattered = lambda terms: lax.psum_scatter(terms, "dp", scatter_dimension=0, tiled=True)
    gate_other = other_terms("tokens", "d_gate")
    for index in range(micro - 1):
        attend_back(index)
    down_grad = order.step(order.behind(down_grad))
    gate_terms = own_terms("tokens", "d_gate", gate_other)
    up_other = other_terms("tokens", "d_up")
    for s in states[:-1]:
        s["d_pairs"] = order.step(order.behind(s["d_pairs"]))
    states[-1]["terms"] = order.step(order.behind(states[-1]["terms"]))
    gate_sum = scattered(order.behind(gate_terms))
    attend_back(micro - 1)
    for index in range(micro):
        input_grad = project_back(index, input_grad)
    core = lax.axis_index("seq") & 1
    sums = [s[name] for name in ("t_in", "t_attn", "t_pre", "t_post", "t_query", "t_keys") for s in states]
    half_out = (shape((devices // 2 * wrows, ind + LANES + width), BF), VMEM)
    mine, other = call(
        functools.partial(weights_kernel, short, wrows, micro),
        None,
        [(order.behind((core if split else jnp.int32(0)).reshape(1)), smem)]
        + [plain(s["attended"]) for s in states]
        + [plain(s["d_attn"]) for s in states]
        + [plain(normed_in)]
        + [plain(s["d_raw"]) for s in states]
        + [plain(term) for term in sums],
        [half_out, half_out],
        scratch=[pltpu.VMEM((width, ind + LANES), F32), pltpu.VMEM((qd, width), F32)],
        name="weights",
    )
    order.step(other)
    if split:
        got = xor_permute(other, 1, seq)
        up_sum = scattered(own_terms("tokens", "d_up", up_other))
        in_parts = fold_chips(mine, got, dp, seq, order)
        both_sums = [part.reshape(seq, wrows, pad) for part in order.behind((gate_sum, up_sum))]
        both_sums = order.step(jnp.concatenate(both_sums, axis=2))
        in_parts = fold_line(in_parts, dp, order)
        both_sums = lax.all_to_all(order.behind(both_sums), "seq", 0, 0)
        gate_grad, up_grad = (columns_of(both_sums, index) for index in range(2))
    else:
        up_sum = scattered(own_terms("tokens", "d_up", None))
        halves_of = [part.reshape(devices // 2, wrows, -1) for part in (mine, other)]
        whole_terms = jnp.stack(halves_of, axis=1).reshape(devices, wrows, -1)
        in_parts = [lax.psum_scatter(whole_terms, BOTH, scatter_dimension=0, tiled=True)[0]]
    q_grad, k_grad, v_grad, gain_sum, out_grad = call(
        functools.partial(finish_kernel, len(in_parts)),
        None,
        [plain(part) for part in in_parts],
        [(shape((wrows, columns), F32), VMEM) for columns in (qd, HD, HD)] + [(shape((8, wrows), F32), VMEM)]
        + [(shape((qd // devices, width), F32), VMEM)],
        name="finish",
    )

    if not split:
        gate_grad, up_grad = to_columns(gate_sum), to_columns(up_sum)
    down_grad = order.behind(down_grad).astype(F32)

    return (
        layer_out,
        input_grad,
        gain_sum[0],
        q_grad,
        k_grad,
        v_grad,
        gain_sum[4, :short],
        gain_sum[5, :short],
        out_grad,
        gain_sum[1],
        gain_sum[2],
        gate_grad,
        up_grad,
        down_grad,
        gain_sum[3],
    )


def solution(mesh):
    dp, seq = mesh.shape["dp"], mesh.shape["seq"]
    acts = P(None, "dp", "seq", None)
    vector = P(BOTH)
    matrix = P(BOTH, None)
    weights = (vector,) + (matrix,) * 3 + (vector,) * 2 + (matrix, vector, vector) + (matrix,) * 3 + (vector,)
    return jax.shard_map(
        functools.partial(shards, dp, seq),
        mesh=mesh,
        in_specs=(acts, acts, P(None, "dp", None)) + weights,
        out_specs=(acts, acts) + weights,
        check_vma=False,
    )
```

```python
import functools
import math

import jax
import jax.numpy as jnp
from jax import lax
from jax.experimental import pallas as pl
from jax.experimental.pallas import tpu as pltpu
from jax.sharding import PartitionSpec as P

HEADS = 4
HD = 256
HALF = HD // 2
WINDOW = 512
EPS = 1e-06
LANES = 128
FACTOR = 1.0 / math.sqrt(HD)
GELU_C = math.sqrt(2.0 / math.pi)
NEG = -1e30

BF = jnp.bfloat16
F32 = jnp.float32
BOTH = ("dp", "seq")
BITS = (6, 2, 4)
NN = ((1,), (0,))
NT = ((1,), (1,))
TN = ((0,), (0,))


def dot(left, right, dims=NN):
    return lax.dot_general(left, right, (dims, ((), ())), preferred_element_type=F32)


def shape(dims, dtype):
    return jax.ShapeDtypeStruct(dims, dtype)


def whole(array):
    return pl.BlockSpec(array.shape, lambda *_: (0,) * array.ndim)


def call(body, grid, inputs, outs, scratch=(), aliases=None, name=None):
    return pl.pallas_call(
        body,
        **({} if grid is None else {"grid": grid}),
        in_specs=[spec for _, spec in inputs],
        out_specs=[spec for _, spec in outs],
        out_shape=[made for made, _ in outs],
        scratch_shapes=list(scratch),
        input_output_aliases=aliases or {},
        compiler_params=pltpu.CompilerParams(vmem_limit_bytes=58 * 2**20),
        cost_estimate=pl.CostEstimate(flops=0, bytes_accessed=1, transcendentals=0),
        name=name,
    )(*[array for array, _ in inputs])


def scale_of(values):
    return lax.rsqrt(jnp.mean(values * values, axis=-1, keepdims=True) + EPS)


def rms(values, gain):
    return values * scale_of(values) * (1.0 + gain)


def rms_back(grad, values, gain):
    scale = scale_of(values)
    normed = values * scale
    inner = grad * (1.0 + gain)
    back = scale * (inner - normed * jnp.mean(inner * normed, axis=-1, keepdims=True))
    return back, jnp.sum(grad * normed, axis=0, keepdims=True)


def turn(values, cosine, sine):
    first, second = values[:, :HALF], values[:, HALF:]
    return jnp.concatenate([first * cosine - second * sine, second * cosine + first * sine], axis=1)


def turn_back(grad, cosine, sine):
    first, second = grad[:, :HALF], grad[:, HALF:]
    return jnp.concatenate([first * cosine + second * sine, second * cosine - first * sine], axis=1)


def gelu_parts(value):
    inner = GELU_C * (value + 0.044715 * value * value * value)
    tanh = jnp.tanh(inner)
    gelu = 0.5 * value * (1.0 + tanh)
    slope = 0.5 * (1.0 + tanh) + 0.5 * value * (1.0 - tanh * tanh) * GELU_C * (1.0 + 3 * 0.044715 * value * value)
    return gelu, slope


def spots(short, wrows, width):
    row = lax.broadcasted_iota(jnp.int32, (width, HD), 0)
    entry = lax.broadcasted_iota(jnp.int32, (width, HD), 1)
    bits = short.bit_length() - 1
    return (row == (entry >> bits) * wrows + (entry & (short - 1))).astype(F32).astype(BF)


def project_kernel(
    short, wrows, x_ref, w_ref, packed_ref, cos_ref, sin_ref, normed_ref, raw_ref, q_ref, pair_ref, gains_ref
):
    qd = q_ref.shape[-1]
    width = x_ref.shape[-1]
    gains_ref[...] = jnp.transpose(packed_ref[...].astype(F32))[:8]
    heads = dot(packed_ref[...], spots(short, wrows, width), TN)
    gains_ref[4:6, :HD] = heads[4:6]
    g_q, g_k = heads[4:5], heads[5:6]
    normed = rms(x_ref[0, 0].astype(F32), gains_ref[0:1]).astype(BF)
    normed_ref[0] = normed
    raw = dot(normed, w_ref[...])
    raw_ref[0] = raw[:, : qd + HD]
    cosine, sine = cos_ref[0], sin_ref[0]
    for head in range(qd // HD):
        at = slice(head * HD, (head + 1) * HD)
        q_ref[0, :, at] = (turn(rms(raw[:, at], g_q), cosine, sine) * FACTOR).astype(BF)
    keys = turn(rms(raw[:, qd : qd + HD], g_k), cosine, sine)
    pair_ref[0, :, :HD] = keys.astype(BF)
    pair_ref[0, :, HD:] = raw[:, qd + HD :].astype(BF)


def masks_of(rows, reach, place):
    length, base = place[0], place[1]
    query = lax.broadcasted_iota(jnp.int32, (rows, rows), 0)
    keys = lax.broadcasted_iota(jnp.int32, (rows, rows), 1)
    first = base & -length
    masks = []
    for by in range(reach + 1):
        behind = query - keys + by * rows
        valid = jnp.where(base - by * rows >= first, WINDOW, -1)
        masks.append((behind >= 0) & (behind < valid))
    return masks


def probs_of(query, pairs, masks):
    scores = [jnp.where(m, dot(query, p[:, :HD], NT), NEG) for p, m in zip(pairs, masks)]
    top = functools.reduce(jnp.maximum, [jnp.max(s, axis=-1, keepdims=True) for s in scores])
    raised = [jnp.exp(s - top) for s in scores]
    total = functools.reduce(jnp.add, [jnp.sum(e, axis=-1, keepdims=True) for e in raised])
    return [e * (1.0 / total) for e in raised]


def attend_kernel(reach, place, x_ref, q_ref, *rest):
    pairs_refs, (w_out, gains, att_ref, out_ref, hidden_ref, nf_ref) = rest[: reach + 1], rest[reach + 1 :]
    pairs = [p[...].reshape(p.shape[-2:]) for p in pairs_refs]
    masks = masks_of(pairs[0].shape[0], reach, place)
    qd = q_ref.shape[-1]
    for head in range(qd // HD):
        at = slice(head * HD, (head + 1) * HD)
        probs = probs_of(q_ref[0, :, at], pairs, masks)
        mixed = sum(dot(p.astype(BF), v[:, HD:]) for p, v in zip(probs, pairs))
        att_ref[:, at] = mixed.astype(BF)
    out = dot(att_ref[...], w_out[...])
    out_ref[...] = out
    hidden = x_ref[0, 0].astype(F32) + rms(out, gains[1:2])
    hidden_ref[...] = hidden
    nf_ref[...] = rms(hidden, gains[2:3]).astype(BF)


def ffn_rows(tokens, w_gu, w_down, store):
    total = None
    for half, (gu, down) in enumerate(zip(w_gu, w_down)):
        pad = down.shape[0]
        both = dot(tokens, gu[...])
        gate, up = both[:, :pad], both[:, pad:]
        gelu, slope = gelu_parts(gate)
        act = (gelu * up).astype(BF)
        store(half, gelu.astype(BF), (up * slope).astype(BF), act)
        part = dot(act, down[...])
        total = part if total is None else total + part
    return total.astype(BF)


def ffn_back_rows(tokens, kept, w_gu, w_down, store):
    total = None
    for half, (gu, down) in enumerate(zip(w_gu, w_down)):
        gelu, rise = kept(half)
        d_act = dot(tokens, down[...], NT)
        d_gate = (d_act * rise.astype(F32)).astype(BF)
        d_up = (d_act * gelu.astype(F32)).astype(BF)
        store(half, d_gate, d_up)
        pad = down.shape[0]
        part = dot(d_gate, gu[:, :pad], NT) + dot(d_up, gu[:, pad:], NT)
        total = part if total is None else total + part
    return total.astype(BF)


def ffn_grid_kernel(halves, t_ref, *refs):
    w_gu, w_down, refs = refs[:halves], refs[halves : 2 * halves], refs[2 * halves :]

    def store(half, *values):
        for kind, value in enumerate(values):
            refs[kind * halves + half][...] = value

    refs[-1][...] = ffn_rows(t_ref[...], w_gu, w_down, store)


def ffn_back_grid_kernel(halves, t_ref, *refs):
    gelus, rises, w_gu, w_down = (refs[i * halves : (i + 1) * halves] for i in range(4))
    refs = refs[4 * halves :]

    def store(half, *values):
        for kind, value in enumerate(values):
            refs[kind * halves + half][...] = value

    kept = lambda half: (gelus[half][...], rises[half][...])
    refs[-1][...] = ffn_back_rows(t_ref[...], kept, w_gu, w_down, store)


class Leaving:
    def __init__(self, sems):
        self.sems, self.copies = sems, []

    def send(self, source, target):
        copy = pltpu.make_async_copy(source, target, self.sems.at[len(self.copies)])
        copy.start()
        self.copies.append(copy)

    def wait(self):
        for copy in self.copies:
            copy.wait()


class Weights:
    def __init__(self, sources, buffers, sems):
        self.buffers = buffers
        self.copies = []
        for index, (source, buffer) in enumerate(zip(sources, buffers)):
            self.copies.append(pltpu.make_async_copy(source, buffer.at[pl.ds(0, source.shape[0])], sems.at[index]))
        self.used = [False] * len(self.copies)

    def start(self, index):
        self.copies[index].start()

    def __getitem__(self, index):
        if not self.used[index]:
            self.copies[index].wait()
            self.used[index] = True
        return self.buffers[index]


class Lazy:
    def __init__(self, weights, index):
        self.weights, self.index = weights, index

    @property
    def shape(self):
        return self.weights.buffers[self.index].shape

    def __getitem__(self, at):
        return self.weights[self.index][at]


def lazy_weights(sources, buffers, sems, halves, first):
    weights = Weights(sources, buffers, sems)
    for source, buffer in zip(sources, buffers):
        rows = source.shape[0]
        if rows < buffer.shape[0]:
            buffer[rows:] = jnp.zeros((buffer.shape[0] - rows, buffer.shape[1]), BF)
    for half in range(halves):
        for kind in first:
            weights.start(kind * halves + half)
    return [Lazy(weights, half) for half in range(halves)], [Lazy(weights, halves + half) for half in range(halves)]


def ffn_kernel(count, halves, *refs):
    tokens, refs = refs[:count], refs[count:]
    sources, refs = refs[: 2 * halves], refs[2 * halves :]
    t_out, outs, parts = refs[0], refs[1 : 1 + 3 * halves], refs[1 + 3 * halves : 1 + 3 * halves + count]
    refs = refs[1 + 3 * halves + count :]
    buffers, w_buffers, sems, w_sems = refs[: 3 * halves], refs[3 * halves : -2], refs[-2], refs[-1]
    w_gu, w_down = lazy_weights(sources, w_buffers, w_sems, halves, (0, 1))
    leaving = Leaving(sems)
    rows = tokens[0].shape[0]
    for index in range(count):
        at = pl.ds(index * rows, rows)
        leaving.send(tokens[index], t_out.at[at])

        def store(half, *values):
            for kind, value in enumerate(values):
                slot = kind * halves + half
                buffers[slot][at] = value
                leaving.send(buffers[slot].at[at], outs[slot].at[at])

        parts[index][...] = ffn_rows(tokens[index][...], w_gu, w_down, store)
    leaving.wait()


def ffn_back_kernel(count, halves, begin, chained, *refs):
    tokens, refs = refs[:count], refs[count:]
    gelus, rises, sources = refs[:halves], refs[halves : 2 * halves], refs[2 * halves : 4 * halves]
    t_out, refs = refs[4 * halves + chained], refs[4 * halves + chained + 1 :]
    outs, parts = refs[: 2 * halves], refs[2 * halves : 2 * halves + count]
    refs = refs[2 * halves + count :]
    kept_in, buffers, w_buffers = (refs[i * 2 * halves : (i + 1) * 2 * halves] for i in range(3))
    sems, in_sems, w_sems = refs[6 * halves :]
    w_gu, w_down = lazy_weights(sources, w_buffers, w_sems, halves, (1, 0))
    leaving = Leaving(sems)
    rows = tokens[0].shape[0]
    arriving = {}
    for index in range(count):
        at, to = pl.ds(index * rows, rows), pl.ds((begin + index) * rows, rows)
        for half in range(halves):
            for kind, source in enumerate((gelus[half], rises[half])):
                slot = kind * halves + half
                copy = pltpu.make_async_copy(source.at[to], kept_in[slot].at[at], in_sems.at[index * 2 * halves + slot])
                copy.start()
                arriving[index, slot] = copy
    for index in range(count):
        at, to = pl.ds(index * rows, rows), pl.ds((begin + index) * rows, rows)
        leaving.send(tokens[index], t_out.at[to])

        def kept(half):
            for slot in (half, halves + half):
                arriving[index, slot].wait()
            return kept_in[half][at], kept_in[halves + half][at]

        def store(half, *values):
            for kind, value in enumerate(values):
                slot = kind * halves + half
                buffers[slot][at] = value
                leaving.send(buffers[slot].at[at], outs[slot].at[to])

        parts[index][...] = ffn_back_rows(tokens[index][...], kept, w_gu, w_down, store)
    leaving.wait()


def untangle_kernel(dp, seq, place, *refs):
    lines, out = refs[:-1], refs[-1]
    rows = out.shape[0] // (dp * seq)

    def body(me):
        for index, ref in enumerate(lines):
            at = me ^ (index % 4 * 2) ^ (index // 4)
            for d in range(dp):
                start, to = d * rows, (d * seq + at) * rows
                out[to : to + rows] = ref[start : start + rows]

    on_value(place[0], seq, body)


def join_kernel(*refs):
    rows = refs[0].shape[0]
    for index, ref in enumerate(refs[:-1]):
        refs[-1][index * rows : (index + 1) * rows] = ref[...]


def owner_kernel(dp, gate_ref, up_ref, out_ref):
    seq, rows, columns = out_ref.shape
    pad = columns // 2
    chunk = gate_ref.shape[1] // (dp * seq)
    zeros = [] if pad == dp * chunk else [jnp.zeros((rows, pad - dp * chunk), BF)]
    for to in range(seq):
        for half, ref in enumerate((gate_ref, up_ref)):
            cuts = [ref[:, (d * seq + to) * chunk : (d * seq + to + 1) * chunk] for d in range(dp)]
            out_ref[to, :, half * pad : (half + 1) * pad] = jnp.concatenate(cuts + zeros, axis=1)


def columns_kernel(dp, in_ref, out_ref):
    seq = in_ref.shape[0]
    chunk = out_ref.shape[1] // (dp * seq)
    for d in range(dp):
        for at in range(seq):
            start = (d * seq + at) * chunk
            out_ref[:, start : start + chunk] = in_ref[at, :, d * chunk : (d + 1) * chunk].astype(F32)


def add_up(refs):
    total = refs[0][...].astype(F32)
    for ref in refs[1:]:
        total = total + ref[...].astype(F32)
    return total


def middle_kernel(count, chained, *refs):
    parts, (dy_ref, hidden_ref, gains), (out_ref, d_ref, t_ref) = refs[:count], refs[count : count + 3], refs[-3:]
    g_post = gains[3:4]
    ffn_out = add_up(parts)
    out_ref[0, 0] = hidden_ref[...] + rms(ffn_out, g_post)
    back, terms = rms_back(dy_ref[0, 0].astype(F32), ffn_out, g_post)
    d_ref[...] = back.astype(BF)
    t_ref[...] = terms


def attend_back_kernel(reach, count, place, *refs):
    parts, refs = refs[:count], refs[count:]
    dy_ref, hidden_ref, out_ref, q_ref, raw_ref, cos_ref, sin_ref, w_out, gains = refs[:9]
    pairs_refs, refs = refs[9 : 10 + reach], refs[10 + reach :]
    g_attn, g_pre, g_q = gains[1:2], gains[2:3], gains[4:5, :HD]
    dh_ref, da_ref, dq_ref, t_pre, t_attn, t_q = refs[:6]
    back_refs, own_ref, sums = refs[6 : 6 + reach], refs[6 + reach], refs[7 + reach :]
    d_hidden, terms = rms_back(add_up(parts), hidden_ref[...], g_pre)
    t_pre[...] = terms
    d_hidden = d_hidden + dy_ref[0, 0].astype(F32)
    dh_ref[...] = d_hidden
    d_attn, terms = rms_back(d_hidden, out_ref[...], g_attn)
    t_attn[...] = terms
    d_attn = d_attn.astype(BF)
    da_ref[...] = d_attn
    d_heads = dot(d_attn, w_out[...], NT).astype(BF)
    pairs = [p[...].reshape(p.shape[-2:]) for p in pairs_refs]
    masks = masks_of(pairs[0].shape[0], reach, place)
    into = (own_ref,) + tuple(sums)
    total_q = None
    for head in range(q_ref.shape[-1] // HD):
        at = slice(head * HD, (head + 1) * HD)
        query, d_head = q_ref[0, :, at], d_heads[:, at]
        probs = probs_of(query, pairs, masks)
        d_probs = [dot(d_head, p[:, HD:], NT) for p in pairs]
        inner = sum(jnp.sum(p * d, axis=-1, keepdims=True) for p, d in zip(probs, d_probs))
        d_scores = [(p * (d - inner)).astype(BF) for p, d in zip(probs, d_probs)]
        d_query = sum(dot(d, p[:, :HD]) for d, p in zip(d_scores, pairs))
        for ref, d, p in zip(into, d_scores, probs):
            d_keys = dot(d, query, TN)
            d_value = dot(p.astype(BF), d_head, TN)
            if head == 0:
                ref[:, :HD] = d_keys
                ref[:, HD:] = d_value
            else:
                ref[:, :HD] += d_keys
                ref[:, HD:] += d_value
        d_turned = turn_back(d_query * FACTOR, cos_ref[0], sin_ref[0])
        back, terms = rms_back(d_turned, raw_ref[0, :, at], g_q)
        dq_ref[:, at] = back.astype(BF)
        total_q = terms if total_q is None else total_q + terms
    t_q[...] = total_q
    for ref, value in zip(back_refs, sums):
        ref[...] = value[...].astype(BF)


def project_back_kernel(count, chained, *refs):
    parts, refs = refs[:count], refs[count:]
    raw_ref, dq_ref, cos_ref, sin_ref, w_ref, x_ref, dh_ref, gains = refs[:8]
    g_in, g_k = gains[0:1], gains[5:6, :HD]
    in_ref, d_ref, t_in, t_k = refs[-4:]
    qd = dq_ref.shape[-1]
    own = add_up(parts)
    d_turned = turn_back(own[:, :HD], cos_ref[0], sin_ref[0])
    back, terms = rms_back(d_turned, raw_ref[0], g_k)
    t_k[...] = terms
    d_ref[:, :qd] = dq_ref[...]
    d_ref[:, qd : qd + HD] = back.astype(BF)
    d_ref[:, qd + HD :] = own[:, HD:].astype(BF)
    d_normed = dot(d_ref[...], w_ref[...], NT)
    back, terms = rms_back(d_normed, x_ref[0, 0].astype(F32), g_in)
    t_in[...] = terms
    in_ref[0, 0] = dh_ref[...] + back


def weights_kernel(short, wrows, micro, core, *refs):
    attended, d_attn, refs = refs[:micro], refs[micro : 2 * micro], refs[2 * micro :]
    normed, d_raw, terms = refs[0], refs[1 : 1 + micro], refs[1 + micro : 1 + 7 * micro]
    mine, other, total, out_total = refs[1 + 7 * micro :]
    out_weights = None
    for left, right in zip(attended, d_attn):
        term = dot(left[...], right[...], TN)
        out_weights = term if out_weights is None else out_weights + term
    out_total[...] = out_weights
    orows = out_total.shape[0] // (2 * (mine.shape[0] // wrows))
    width = normed.shape[-1]
    ind = d_raw[0].shape[-1]
    weights = None
    for index in range(micro):
        term = dot(normed[index], d_raw[index][...], TN)
        weights = term if weights is None else weights + term
    total[:, :ind] = weights
    sums = []
    for kind in range(6):
        value = terms[kind * micro][...]
        for index in range(1, micro):
            value = value + terms[kind * micro + index][...]
        sums.append(value)
    place = spots(short, wrows, width)
    heads = [dot(jnp.broadcast_to(s, (8, HD)).astype(BF), place, NT)[:1] for s in sums[4:]]
    rows = jnp.concatenate(sums[:4] + heads + [jnp.zeros((LANES - 6, width), F32)], axis=0)
    total[:, ind:] = jnp.transpose(rows)
    odd = core[0] == 1
    for index in range(mine.shape[0] // wrows):
        at = slice(index * wrows, (index + 1) * wrows)
        first = total[2 * index * wrows : (2 * index + 1) * wrows]
        second = total[(2 * index + 1) * wrows : (2 * index + 2) * wrows]
        columns = first.shape[1]
        mine[at, :columns] = jnp.where(odd, second, first).astype(BF)
        other[at, :columns] = jnp.where(odd, first, second).astype(BF)
        first = out_total[2 * index * orows : (2 * index + 1) * orows]
        second = out_total[(2 * index + 1) * orows : (2 * index + 2) * orows]
        at = slice(index * wrows, index * wrows + orows)
        mine[at, columns:] = jnp.where(odd, second, first).astype(BF)
        other[at, columns:] = jnp.where(odd, first, second).astype(BF)
        if orows < wrows:
            rest = slice(index * wrows + orows, (index + 1) * wrows)
            for ref in (mine, other):
                ref[rest, columns:] = jnp.zeros((wrows - orows, ref.shape[1] - columns), BF)


def on_value(scalar, count, body):
    for value in range(count):

        @pl.when(scalar == value)
        def _(value=value):
            body(value)


def line_kernel(both_ref, in_ref, out_ref):
    count, columns = both_ref.shape[0], in_ref.shape[1]
    in_rows, out_rows = in_ref.shape[0] // count, out_ref.shape[0] // count
    end = columns + out_ref.shape[1]
    for at in range(count):
        in_ref[at * in_rows : (at + 1) * in_rows] = both_ref[at, :in_rows, :columns]
        out_ref[at * out_rows : (at + 1) * out_rows] = both_ref[at, :out_rows, columns:end]


def terms_kernel(count, kinds, has_got, *refs):
    lefts, rights, refs = refs[:count], refs[count : count + count * kinds], refs[count + count * kinds :]
    gots, outs = refs[: kinds if has_got else 0], refs[-kinds:]
    for kind in range(kinds):
        total = None
        for left, right in zip(lefts, rights[kind * count :]):
            term = dot(left[...], right[...], TN)
            total = term if total is None else total + term
        total = total[: outs[kind].shape[0]]
        if has_got:
            total = total + gots[kind][...].astype(F32)
        outs[kind][...] = total.astype(BF)


def fold_chips_kernel(dp, place, mine, got, line, *sends):
    chips = len(sends) + 1
    rows = line.shape[0] // dp

    def body(chip):
        for index in range(dp):
            for bit in range(chips):
                start = (index * chips + (chip ^ bit)) * rows
                value = mine[start : start + rows].astype(F32) + got[start : start + rows].astype(F32)
                at = slice(index * rows, (index + 1) * rows)
                if bit:
                    sends[bit - 1][at] = value.astype(BF)
                else:
                    line[at] = value

    on_value(place[0], chips, body)


def fold_line_kernel(dp, count, place, *refs):
    parts, (own, *sends) = refs[:count], refs[count:]
    rows = own.shape[0]

    def body(d):
        for by in range(dp):
            start = (d + by) % dp * rows
            value = parts[0][start : start + rows]
            for part in parts[1:]:
                value = value + part[start : start + rows].astype(F32)
            if by:
                sends[by - 1][...] = value.astype(BF)
            else:
                own[...] = value

    on_value(place[0], dp, body)


def finish_kernel(count, *refs):
    parts, outs = refs[:count], refs[count:]
    total = add_up(parts)
    start = 0
    for out in outs[:-2]:
        out[...] = total[:, start : start + out.shape[1]]
        start += out.shape[1]
    outs[-2][...] = jnp.transpose(total[:, start : start + LANES])[:8]
    outs[-1][...] = total[: outs[-1].shape[0], start + LANES :]


def after(value, *others):
    return lax.optimization_barrier((value,) + others)[0]


def xor_permute(value, bit, size):
    return lax.ppermute(value, "seq", [(i, i ^ bit) for i in range(size)])


def from_behind(value, by, size):
    pairs = [(i, i + by) for i in range(size) if 0 <= i + by < size]
    return lax.ppermute(value, "seq", pairs)


def near_blocks(own, size, bits=(2, 4, 6)):
    return [xor_permute(own, bit, size) for bit in bits]


class Order:
    def __init__(self):
        self.last = None

    def behind(self, value):
        return value if self.last is None else after(value, self.last)

    def step(self, value):
        self.last = value
        return value


def around(value, by, dp):
    return lax.ppermute(value, "dp", [(i, (i + by) % dp) for i in range(dp)])


def along(value, by, dp):
    return lax.ppermute(value, "dp", [(i, i + by) for i in range(dp) if 0 <= i + by < dp])


def add_up_arrays(parts):
    return functools.reduce(lambda a, b: a + b.astype(F32), parts[1:], parts[0])


VMEM = pl.BlockSpec(memory_space=pltpu.VMEM)
SMEM = pl.BlockSpec(memory_space=pltpu.SMEM)


def plain(array):
    return (array, VMEM)


def fold_chips(mine, got, dp, seq, order):
    dims = (mine.shape[0] * 2 // seq, mine.shape[1])
    chip = order.behind((lax.axis_index("seq") >> 1).reshape(1))
    line, *sends = call(
        functools.partial(fold_chips_kernel, dp),
        None,
        [(chip, SMEM), plain(mine), plain(got)],
        [(shape(dims, F32), VMEM)] + [(shape(dims, BF), VMEM)] * 3,
        name="fold_chips",
    )
    order.step(sends)
    return [line] + [xor_permute(send, bit, seq) for send, bit in zip(sends, (2, 4, 6))]


def fold_line(parts, dp, order):
    dims = (parts[0].shape[0] // dp, parts[0].shape[1])
    place = order.behind(lax.axis_index("dp").reshape(1))
    own, *sends = call(
        functools.partial(fold_line_kernel, dp, len(parts)),
        None,
        [(place, SMEM)] + [plain(part) for part in parts],
        [(shape(dims, F32), VMEM)] + [(shape(dims, BF), VMEM)] * (dp - 1),
        name="fold_line",
    )
    order.step(sends)
    return [own] + [around(send, by, dp) for by, send in enumerate(sends, 1)]


def shards(
    dp,
    seq,
    layer_input,
    out_cotangent,
    seq_lengths,
    inputnorm,
    queryproj,
    keyproj,
    valueproj,
    querynorm,
    keynorm,
    outproj,
    attnnorm,
    prefeednorm,
    gateproj,
    upproj,
    downproj,
    postfeednorm,
):
    micro, _, rows, width = layer_input.shape
    devices = dp * seq
    wrows = width // devices
    qd = queryproj.shape[1]
    ind = qd + 2 * HD
    ff = gateproj.shape[1]
    chunk = ff // devices
    own_ff = dp * chunk
    pad = -(-own_ff // LANES) * LANES
    reach = WINDOW // rows
    split = seq == 8 and dp == 4

    base = lax.axis_index("seq") * rows
    positions = base + jnp.arange(rows, dtype=jnp.int32)
    inverse = jnp.power(F32(10000.0), -2.0 * jnp.arange(HALF, dtype=F32) / HD)
    lengths = seq_lengths[:, 0, 0]
    relative = positions[None, :] & (lengths[:, None] - 1)
    angles = relative.astype(F32)[:, :, None] * inverse
    cosine, sine = jnp.cos(angles), jnp.sin(angles)

    order = Order()
    short = querynorm.shape[0]
    fill = (0, wrows - short)
    gains = [inputnorm, attnnorm, prefeednorm, postfeednorm, jnp.pad(querynorm, fill), jnp.pad(keynorm, fill)]
    gains = jnp.pad(jnp.stack(gains, axis=1), ((0, 0), (0, LANES - len(gains))))
    packed = jnp.concatenate([queryproj, keyproj, valueproj, gains], axis=1)
    along_dp = lax.axis_index("dp").reshape(1)
    if split:
        orows = outproj.shape[0]
        both = jnp.concatenate([packed, jnp.pad(outproj, ((0, wrows - orows), (0, 0)))], axis=1)
        least = -(-(2**19) // (dp * wrows * LANES)) * LANES
        both = jnp.pad(both, ((0, 0), (0, max(0, least - both.shape[1]))))
        both = order.step(lax.optimization_barrier(both[None]))
        line = lax.all_gather(both, "dp", axis=0, tiled=True)

    [gate_up] = call(
        functools.partial(owner_kernel, dp),
        None,
        [plain(gateproj), plain(upproj)],
        [(shape((seq, wrows, 2 * pad), BF), VMEM)],
        name="owner",
    )
    gate_up = lax.all_to_all(gate_up, "seq", 0, 0).reshape(seq * wrows, 2 * pad)
    w_gu = [lax.all_gather(gate_up, "dp", axis=0, tiled=True)]
    if split:
        cosine, sine, line = order.step(order.behind((cosine, sine, line)))
        downproj = after(downproj, line)
    w_down = lax.all_gather(downproj, "dp", axis=0, tiled=True)
    if split:
        in_line, out_line = call(
            line_kernel,
            None,
            [plain(line)],
            [(shape((dp * wrows, ind + LANES), BF), VMEM), (shape((dp * orows, width), BF), VMEM)],
            name="line",
        )

        def untangle(lines, name):
            [array] = call(
                functools.partial(untangle_kernel, dp, seq),
                None,
                [(lax.axis_index("seq").reshape(1), SMEM)] + [plain(line) for line in lines],
                [(shape((lines[0].shape[0] * seq, lines[0].shape[1]), BF), VMEM)],
                name=name,
            )
            return array

        in_lines = [in_line] + near_blocks(order.step(in_line), seq)
        in_lines = order.step(order.behind(in_lines))
        out_lines = [out_line] + near_blocks(after(out_line, in_lines), seq)
        in_lines = in_lines + [xor_permute(line, 1, seq) for line in in_lines]
        in_lines = order.step(order.behind(in_lines))
        w_in = untangle(in_lines, "untangle_in")
        order.step(w_in)
    else:
        w_in = lax.all_gather(packed[None], BOTH, axis=0, tiled=True).reshape(width, -1)
        w_out = lax.all_gather(outproj, BOTH, axis=0, tiled=True)

    def of_micro(array, index):
        dims = array.shape[1:]
        return (array, pl.BlockSpec((1,) + dims, lambda *_: (index,) + (0,) * len(dims)))

    def full(array):
        return (array, whole(array))

    def new(dims, dtype):
        return (shape(dims, dtype), pl.BlockSpec(dims, lambda *_: (0,) * len(dims)))

    smem = pl.BlockSpec(memory_space=pltpu.SMEM)
    each = lambda *dims: pl.BlockSpec((1,) + dims, lambda i: (i,) + (0,) * len(dims))
    w_in_spec = pl.BlockSpec((width, ind), lambda *_: (0, 0))

    cosine = order.behind(cosine)
    gains_spec = pl.BlockSpec((width, LANES), lambda *_: (0, ind // LANES))
    normed_in, raw, query, pair, gains = call(
        functools.partial(project_kernel, short, wrows),
        (micro,),
        [(layer_input, each(1, rows, width)), (w_in, w_in_spec), (w_in, gains_spec)]
        + [(cosine, each(rows, HALF)), (sine, each(rows, HALF))],
        [
            (shape((micro, rows, width), BF), each(rows, width)),
            (shape((micro, rows, qd + HD), F32), each(rows, qd + HD)),
            (shape((micro, rows, qd), BF), each(rows, qd)),
            (shape((micro, rows, 2 * HD), BF), each(rows, 2 * HD)),
            new((8, width), F32),
        ],
        name="project",
    )

    order.step(pair)
    behind = [from_behind(pair, by, seq) for by in range(1, reach + 1)]
    if split:
        out_lines = order.step(order.behind(out_lines))
        out_lines = out_lines + [xor_permute(line, 1, seq) for line in out_lines]
        out_lines = order.step(order.behind(out_lines))
        w_out = order.step(untangle(out_lines, "untangle_out"))
    states = []
    for index in range(micro):
        place = order.behind(jnp.stack([lengths[index], base]))
        pairs = [of_micro(p, index) for p in [pair] + behind]
        attended, attn_out, hidden, normed_ffn = call(
            functools.partial(attend_kernel, reach),
            (1,),
            [(place, smem), of_micro(layer_input, index), of_micro(query, index)]
            + pairs
            + [full(w_out), full(gains)],
            [new((rows, qd), BF), new((rows, width), F32), new((rows, width), F32), new((rows, width), BF)],
            name="attend",
        )
        order.step(normed_ffn)
        s = dict(place=place, pairs=pairs, attended=attended, attn_out=attn_out, hidden=hidden)
        s["sent"] = near_blocks(normed_ffn, seq, BITS) if split else None
        s["nf"] = normed_ffn
        states.append(s)

    if split:
        states[0]["sent"] = order.step(order.behind(states[0]["sent"]))
        w_gu.append(xor_permute(order.step(order.behind(w_gu[0])), 1, seq))
        w_down = [order.step(order.behind(w_down))]
        w_down.append(xor_permute(w_down[0], 1, seq))
    else:
        w_down = [jnp.pad(w_down, ((0, pad - own_ff), (0, 0)))]
    halves = len(w_gu)

    def blocks(array):
        return (array, pl.BlockSpec((rows, array.shape[1]), lambda i: (i, 0)))

    def made(count, columns):
        return (shape((count, columns), BF), pl.BlockSpec((rows, columns), lambda i: (i, 0)))

    def fixed(array):
        return (array, pl.BlockSpec(array.shape, lambda *_: (0,) * array.ndim, pipeline_mode=pl.Buffered(1)))

    def block(index_of, columns):
        return pl.BlockSpec((rows, columns), index_of)

    any_spec = pl.BlockSpec(memory_space=pl.ANY)
    w_scratch = [pltpu.VMEM((width, 2 * pad), BF)] * halves + [pltpu.VMEM((pad, width), BF)] * halves

    def ffn(pieces):
        if not split:
            count = pieces[0].shape[0] // rows
            results = call(
                functools.partial(ffn_grid_kernel, halves),
                (count,),
                [blocks(pieces[0])] + [fixed(w) for w in w_gu] + [fixed(w) for w in w_down],
                [made(count * rows, pad)] * 3 + [made(count * rows, width)],
                name="ffn",
            )
            return pieces[0], results[:1], results[1:2], results[2:3], results[3:]
        count = len(pieces)
        results = call(
            functools.partial(ffn_kernel, count, halves),
            None,
            [plain(array) for array in order.behind(pieces)] + [(w, any_spec) for w in [*w_gu, *w_down]],
            [(shape((count * rows, width), BF), any_spec)]
            + [(shape((count * rows, pad), BF), any_spec)] * (3 * halves)
            + [(shape((rows, width), BF), VMEM)] * count,
            scratch=[pltpu.VMEM((count * rows, pad), BF)] * (3 * halves)
            + w_scratch
            + [pltpu.SemaphoreType.DMA((count * (1 + 3 * halves),)), pltpu.SemaphoreType.DMA((2 * halves,))],
            name="ffn",
        )
        kinds = [results[1 + i * halves : 1 + (i + 1) * halves] for i in range(3)]
        return results[0], *kinds, results[1 + 3 * halves :]

    def ffn_backward(pieces, gelu, rise, begin=0, total=0, kept=()):
        if not split:
            count = pieces[0].shape[0] // rows
            results = call(
                functools.partial(ffn_back_grid_kernel, halves),
                (count,),
                [blocks(pieces[0]), *map(blocks, gelu), *map(blocks, rise)]
                + [fixed(w) for w in w_gu]
                + [fixed(w) for w in w_down],
                [made(count * rows, pad)] * 2 + [made(count * rows, width)],
                name="ffn_back",
            )
            return pieces[0], results[:1], results[1:2], results[2:]
        count = len(pieces)
        arrays = [*gelu, *rise, *w_gu, *w_down, *kept]
        results = call(
            functools.partial(ffn_back_kernel, count, halves, begin, len(kept)),
            None,
            [plain(piece) for piece in pieces] + [(array, any_spec) for array in arrays],
            [(shape((total * rows, width), BF), any_spec)]
            + [(shape((total * rows, pad), BF), any_spec)] * (2 * halves)
            + [(shape((rows, width), BF), VMEM)] * count,
            scratch=[pltpu.VMEM((count * rows, pad), BF)] * (4 * halves)
            + w_scratch
            + [pltpu.SemaphoreType.DMA((count * (1 + 2 * halves),)), pltpu.SemaphoreType.DMA((count * 2 * halves,))]
            + [pltpu.SemaphoreType.DMA((2 * halves,))],
            aliases={count + len(arrays) - len(kept) + index: index for index in range(len(kept))},
            name="ffn_back",
        )
        return results[0], results[1 : 1 + halves], results[1 + halves : 1 + 2 * halves], results[1 + 2 * halves :]

    def pieces_of(own, near):
        if not split:
            return [lax.all_gather(order.behind(own), "seq", axis=0, tiled=True)]
        return list(near) + [order.behind(own)]

    def scatter(parts):
        if not split:
            return [lax.psum_scatter(parts[0], "seq", scatter_dimension=0, tiled=True)]
        return [parts[-1]] + [xor_permute(part, bit, seq) for part, bit in zip(parts, BITS)]

    for s in states:
        pieces = pieces_of(s["nf"], s["sent"])
        s["tokens"], s["gelu"], s["rise"], s["act"], parts = ffn(pieces)
        order.step(parts)
        s["terms"] = scatter(parts)

    def join(pieces):
        [joined] = call(
            join_kernel,
            None,
            [plain(piece) for piece in pieces],
            [(shape((len(pieces) * rows, width), BF), VMEM)],
            name="join",
        )
        return joined

    def over_tokens(left, rights, half, gots=(), high_out=None):
        of = lambda s, name: s[name] if name in ("tokens", "d_tokens") else s[name][half]
        lefts = order.behind([of(s, left) for s in states])
        others = [of(s, right) for right in rights for s in states]
        count, high, wide = lefts[0].shape[0], lefts[0].shape[1], others[0].shape[1]
        by_rows = high % 384 == 0
        moving = lambda columns: pl.BlockSpec((count, columns), lambda i: (0, i))
        staying = lambda columns: pl.BlockSpec((count, columns), lambda i: (0, 0), pipeline_mode=pl.Buffered(1))
        if by_rows:
            steps, left_spec, right_spec = high // 384, moving(384), staying(wide)
            out_spec = pl.BlockSpec((384, wide), lambda i: (i, 0))
        else:
            steps, left_spec, right_spec = wide // 384, staying(high), moving(384)
            out_spec = pl.BlockSpec((high_out or high, 384), lambda i: (0, i))
        results = call(
            functools.partial(terms_kernel, micro, len(rights), bool(gots)),
            (steps,),
            [(a, left_spec) for a in lefts] + [(b, right_spec) for b in others] + [(got, out_spec) for got in gots],
            [(shape((high_out or high, wide), BF), out_spec)] * len(rights),
            name="terms",
        )
        return order.step(results)

    def other_terms(left, right, high_out=None):
        return over_tokens(left, [right], 1, (), high_out)[0] if split else None

    def own_terms(left, right, other, high_out=None):
        return over_tokens(left, [right], 0, [xor_permute(other, 1, seq)] if split else (), high_out)[0]

    def ffn_back(s, which):
        if not split:
            if which == "rest":
                pieces = pieces_of(s["d_ffn"], s["sent"])
                s["d_tokens"], s["d_gate"], s["d_up"], parts = ffn_backward(pieces, s["gelu"], s["rise"])
                s["terms"] = scatter(order.step(parts))
            return
        own, others = [order.behind(s["d_ffn"])], list(s["sent"])
        total = len(own) + len(others)
        if which == "own":
            s["kept"] = ffn_backward(own, s["gelu"], s["rise"], len(others), total)
            order.step(s["kept"][-1])
            return
        tokens, d_gate, d_up, last = s["kept"]
        others[0] = order.behind(others[0])
        tokens, s["d_gate"], s["d_up"], parts = ffn_backward(
            others, s["gelu"], s["rise"], 0, total, [tokens, *d_gate, *d_up]
        )
        s.setdefault("d_tokens", tokens)
        s["terms"] = scatter(order.step(list(parts)) + list(last))

    layer_out = None
    result = shape((micro, 1, rows, width), F32)
    for index, s in enumerate(states):
        parts = s["terms"]
        chain = [] if layer_out is None else [(layer_out, pl.BlockSpec(memory_space=pl.ANY))]
        layer_out, s["d_ffn"], s["t_post"] = call(
            functools.partial(middle_kernel, len(parts), bool(chain)),
            (1,),
            [full(p) for p in parts]
            + [of_micro(out_cotangent, index), full(s["hidden"]), full(order.behind(gains))]
            + chain,
            [(result, of_micro(result, index)[1]), new((rows, width), BF), new((1, width), F32)],
            aliases={len(parts) + 3: 0} if chain else None,
            name="middle",
        )
        order.step(s["d_ffn"])
        s["sent"] = near_blocks(s["d_ffn"], seq, BITS) if split else None
        ffn_back(s, "own")

    for s in states[:-1]:
        ffn_back(s, "rest")
    late = states[-1]
    if split:
        late["sent"] = order.step(order.behind(late["sent"]))
        late["d_tokens"] = order.step(join(list(late["sent"]) + [late["d_ffn"]]))
        down_other = other_terms("act", "d_tokens", own_ff)
    ffn_back(late, "rest")
    down_terms = own_terms("act", "d_tokens", down_other if split else None, own_ff)
    for s in states[:-1]:
        s["terms"] = order.step(order.behind(s["terms"]))
    down_grad = lax.psum_scatter(order.behind(down_terms), "dp", scatter_dimension=0, tiled=True)

    def attend_back(index):
        s = states[index]
        parts = s["terms"]
        backs = call(
            functools.partial(attend_back_kernel, reach, len(parts)),
            (1,),
            [(order.behind(s["place"]), smem)]
            + [full(p) for p in parts]
            + [of_micro(out_cotangent, index), full(s["hidden"]), full(s["attn_out"]), of_micro(query, index)]
            + [of_micro(raw, index), of_micro(cosine, index), of_micro(sine, index)]
            + [full(w_out), full(gains)]
            + s["pairs"],
            [new((rows, width), F32), new((rows, width), BF), new((rows, qd), BF)]
            + [new((1, width), F32), new((1, width), F32), new((1, HD), F32)]
            + [new((rows, 2 * HD), BF)] * reach
            + [new((rows, 2 * HD), F32)],
            scratch=[pltpu.VMEM((rows, 2 * HD), F32)] * reach,
            name="attend_back",
        )
        s["d_hidden"], s["d_attn"], s["d_raw_q"], s["t_pre"], s["t_attn"], s["t_query"] = backs[:6]
        order.step(s["d_attn"])
        sent, own = backs[6 : 6 + reach], backs[-1]
        s["d_pairs"] = [own] + [from_behind(value, -by, seq) for by, value in enumerate(sent, 1)]

    def project_back(index, input_grad):
        s = states[index]
        terms = s["d_pairs"]
        chain = [] if input_grad is None else [(input_grad, pl.BlockSpec(memory_space=pl.ANY))]
        keys_spec = pl.BlockSpec((1, rows, HD), lambda *_: (index, 0, qd // HD))
        input_grad, s["d_raw"], s["t_in"], s["t_keys"] = call(
            functools.partial(project_back_kernel, len(terms), bool(chain)),
            (1,),
            [full(t) for t in terms]
            + [(raw, keys_spec), full(s["d_raw_q"]), of_micro(cosine, index), of_micro(sine, index), (w_in, w_in_spec)]
            + [of_micro(layer_input, index), full(s["d_hidden"]), full(order.behind(gains))]
            + chain,
            [(result, of_micro(result, index)[1]), new((rows, ind), BF), new((1, width), F32), new((1, HD), F32)],
            aliases={len(terms) + 8: 0} if chain else None,
            name="project_back",
        )
        order.step(s["d_raw"])
        s["normed_in"] = normed_in[index]
        return input_grad

    def columns_of(part, index):
        [columns] = call(
            functools.partial(columns_kernel, dp),
            (1,),
            [(part, pl.BlockSpec((seq, wrows, pad), lambda *_: (0, 0, index)))],
            [(shape((wrows, ff), F32), pl.BlockSpec((wrows, ff), lambda *_: (0, 0)))],
            name="columns",
        )
        return columns

    def to_columns(part):
        return columns_of(lax.all_to_all(part.reshape(seq, wrows, pad), "seq", 0, 0), 0)

    input_grad = None
    scattered = lambda terms: lax.psum_scatter(terms, "dp", scatter_dimension=0, tiled=True)
    gate_other = other_terms("tokens", "d_gate")
    for index in range(micro - 1):
        attend_back(index)
    gate_terms = own_terms("tokens", "d_gate", gate_other)
    up_other = other_terms("tokens", "d_up")
    for s in states[:-1]:
        s["d_pairs"] = order.step(order.behind(s["d_pairs"]))
    states[-1]["terms"], down_grad = order.step(order.behind((states[-1]["terms"], down_grad)))
    gate_sum = scattered(order.behind(gate_terms))
    attend_back(micro - 1)
    for index in range(micro):
        input_grad = project_back(index, input_grad)
    core = lax.axis_index("seq") & 1
    sums = [s[name] for name in ("t_in", "t_attn", "t_pre", "t_post", "t_query", "t_keys") for s in states]
    half_out = (shape((devices // 2 * wrows, ind + LANES + width), BF), VMEM)
    mine, other = call(
        functools.partial(weights_kernel, short, wrows, micro),
        None,
        [(order.behind((core if split else jnp.int32(0)).reshape(1)), smem)]
        + [plain(s["attended"]) for s in states]
        + [plain(s["d_attn"]) for s in states]
        + [plain(normed_in)]
        + [plain(s["d_raw"]) for s in states]
        + [plain(term) for term in sums],
        [half_out, half_out],
        scratch=[pltpu.VMEM((width, ind + LANES), F32), pltpu.VMEM((qd, width), F32)],
        name="weights",
    )
    order.step(other)
    if split:
        got = xor_permute(other, 1, seq)
        up_sum = scattered(own_terms("tokens", "d_up", up_other))
        in_parts = fold_chips(mine, got, dp, seq, order)
        in_parts = order.step(order.behind(in_parts))
        both_sums = [part.reshape(seq, wrows, pad) for part in order.behind((gate_sum, up_sum))]
        both_sums = order.step(jnp.concatenate(both_sums, axis=2))
        both_sums = lax.all_to_all(both_sums, "seq", 0, 0)
        in_parts = fold_line(in_parts, dp, order)
        gate_grad, up_grad = (columns_of(both_sums, index) for index in range(2))
    else:
        up_sum = scattered(own_terms("tokens", "d_up", None))
        halves_of = [part.reshape(devices // 2, wrows, -1) for part in (mine, other)]
        whole_terms = jnp.stack(halves_of, axis=1).reshape(devices, wrows, -1)
        in_parts = [lax.psum_scatter(whole_terms, BOTH, scatter_dimension=0, tiled=True)[0]]
    q_grad, k_grad, v_grad, gain_sum, out_grad = call(
        functools.partial(finish_kernel, len(in_parts)),
        None,
        [plain(part) for part in in_parts],
        [(shape((wrows, columns), F32), VMEM) for columns in (qd, HD, HD)] + [(shape((8, wrows), F32), VMEM)]
        + [(shape((qd // devices, width), F32), VMEM)],
        name="finish",
    )

    if not split:
        gate_grad, up_grad = to_columns(gate_sum), to_columns(up_sum)
    down_grad = order.behind(down_grad).astype(F32)

    return (
        layer_out,
        input_grad,
        gain_sum[0],
        q_grad,
        k_grad,
        v_grad,
        gain_sum[4, :short],
        gain_sum[5, :short],
        out_grad,
        gain_sum[1],
        gain_sum[2],
        gate_grad,
        up_grad,
        down_grad,
        gain_sum[3],
    )


def solution(mesh):
    dp, seq = mesh.shape["dp"], mesh.shape["seq"]
    acts = P(None, "dp", "seq", None)
    vector = P(BOTH)
    matrix = P(BOTH, None)
    weights = (vector,) + (matrix,) * 3 + (vector,) * 2 + (matrix, vector, vector) + (matrix,) * 3 + (vector,)
    return jax.shard_map(
        functools.partial(shards, dp, seq),
        mesh=mesh,
        in_specs=(acts, acts, P(None, "dp", None)) + weights,
        out_specs=(acts, acts) + weights,
        check_vma=False,
    )
```

```python
import functools
import math

import jax
import jax.numpy as jnp
from jax import lax
from jax.experimental import pallas as pl
from jax.experimental.pallas import tpu as pltpu
from jax.sharding import PartitionSpec as P

HEADS = 4
HD = 256
HALF = HD // 2
WINDOW = 512
EPS = 1e-06
LANES = 128
FACTOR = 1.0 / math.sqrt(HD)
GELU_C = math.sqrt(2.0 / math.pi)
NEG = -1e30

BF = jnp.bfloat16
F32 = jnp.float32
BOTH = ("dp", "seq")
BITS = (6, 2, 4)
NN = ((1,), (0,))
NT = ((1,), (1,))
TN = ((0,), (0,))


def dot(left, right, dims=NN):
    return lax.dot_general(left, right, (dims, ((), ())), preferred_element_type=F32)


def shape(dims, dtype):
    return jax.ShapeDtypeStruct(dims, dtype)


def whole(array):
    return pl.BlockSpec(array.shape, lambda *_: (0,) * array.ndim)


def call(body, grid, inputs, outs, scratch=(), aliases=None, name=None):
    return pl.pallas_call(
        body,
        **({} if grid is None else {"grid": grid}),
        in_specs=[spec for _, spec in inputs],
        out_specs=[spec for _, spec in outs],
        out_shape=[made for made, _ in outs],
        scratch_shapes=list(scratch),
        input_output_aliases=aliases or {},
        compiler_params=pltpu.CompilerParams(vmem_limit_bytes=58 * 2**20),
        cost_estimate=pl.CostEstimate(flops=0, bytes_accessed=1, transcendentals=0),
        name=name,
    )(*[array for array, _ in inputs])


def scale_of(values):
    return lax.rsqrt(jnp.mean(values * values, axis=-1, keepdims=True) + EPS)


def rms(values, gain):
    return values * scale_of(values) * (1.0 + gain)


def rms_back(grad, values, gain):
    scale = scale_of(values)
    normed = values * scale
    inner = grad * (1.0 + gain)
    back = scale * (inner - normed * jnp.mean(inner * normed, axis=-1, keepdims=True))
    return back, jnp.sum(grad * normed, axis=0, keepdims=True)


def turn(values, cosine, sine):
    first, second = values[:, :HALF], values[:, HALF:]
    return jnp.concatenate([first * cosine - second * sine, second * cosine + first * sine], axis=1)


def turn_back(grad, cosine, sine):
    first, second = grad[:, :HALF], grad[:, HALF:]
    return jnp.concatenate([first * cosine + second * sine, second * cosine - first * sine], axis=1)


def gelu_parts(value):
    inner = GELU_C * (value + 0.044715 * value * value * value)
    tanh = jnp.tanh(inner)
    gelu = 0.5 * value * (1.0 + tanh)
    slope = 0.5 * (1.0 + tanh) + 0.5 * value * (1.0 - tanh * tanh) * GELU_C * (1.0 + 3 * 0.044715 * value * value)
    return gelu, slope


def spots(short, wrows, width):
    row = lax.broadcasted_iota(jnp.int32, (width, HD), 0)
    entry = lax.broadcasted_iota(jnp.int32, (width, HD), 1)
    bits = short.bit_length() - 1
    return (row == (entry >> bits) * wrows + (entry & (short - 1))).astype(F32).astype(BF)


def project_kernel(
    short, wrows, x_ref, w_ref, packed_ref, cos_ref, sin_ref, normed_ref, raw_ref, q_ref, pair_ref, gains_ref
):
    qd = q_ref.shape[-1]
    width = x_ref.shape[-1]
    gains_ref[...] = jnp.transpose(packed_ref[...].astype(F32))[:8]
    heads = dot(packed_ref[...], spots(short, wrows, width), TN)
    gains_ref[4:6, :HD] = heads[4:6]
    g_q, g_k = heads[4:5], heads[5:6]
    normed = rms(x_ref[0, 0].astype(F32), gains_ref[0:1]).astype(BF)
    normed_ref[0] = normed
    raw = dot(normed, w_ref[...])
    raw_ref[0] = raw[:, : qd + HD]
    cosine, sine = cos_ref[0], sin_ref[0]
    for head in range(qd // HD):
        at = slice(head * HD, (head + 1) * HD)
        q_ref[0, :, at] = (turn(rms(raw[:, at], g_q), cosine, sine) * FACTOR).astype(BF)
    keys = turn(rms(raw[:, qd : qd + HD], g_k), cosine, sine)
    pair_ref[0, :, :HD] = keys.astype(BF)
    pair_ref[0, :, HD:] = raw[:, qd + HD :].astype(BF)


def masks_of(rows, reach, place):
    length, base = place[0], place[1]
    query = lax.broadcasted_iota(jnp.int32, (rows, rows), 0)
    keys = lax.broadcasted_iota(jnp.int32, (rows, rows), 1)
    first = base & -length
    masks = []
    for by in range(reach + 1):
        behind = query - keys + by * rows
        valid = jnp.where(base - by * rows >= first, WINDOW, -1)
        masks.append((behind >= 0) & (behind < valid))
    return masks


def probs_of(query, pairs, masks):
    scores = [jnp.where(m, dot(query, p[:, :HD], NT), NEG) for p, m in zip(pairs, masks)]
    top = functools.reduce(jnp.maximum, [jnp.max(s, axis=-1, keepdims=True) for s in scores])
    raised = [jnp.exp(s - top) for s in scores]
    total = functools.reduce(jnp.add, [jnp.sum(e, axis=-1, keepdims=True) for e in raised])
    return [e * (1.0 / total) for e in raised]


def attend_kernel(reach, place, x_ref, q_ref, *rest):
    pairs_refs, (w_out, gains, att_ref, out_ref, hidden_ref, nf_ref) = rest[: reach + 1], rest[reach + 1 :]
    pairs = [p[...].reshape(p.shape[-2:]) for p in pairs_refs]
    masks = masks_of(pairs[0].shape[0], reach, place)
    qd = q_ref.shape[-1]
    for head in range(qd // HD):
        at = slice(head * HD, (head + 1) * HD)
        probs = probs_of(q_ref[0, :, at], pairs, masks)
        mixed = sum(dot(p.astype(BF), v[:, HD:]) for p, v in zip(probs, pairs))
        att_ref[:, at] = mixed.astype(BF)
    out = dot(att_ref[...], w_out[...])
    out_ref[...] = out
    hidden = x_ref[0, 0].astype(F32) + rms(out, gains[1:2])
    hidden_ref[...] = hidden
    nf_ref[...] = rms(hidden, gains[2:3]).astype(BF)


def ffn_rows(tokens, w_gu, w_down, store):
    total = None
    for half, (gu, down) in enumerate(zip(w_gu, w_down)):
        pad = down.shape[0]
        both = dot(tokens, gu[...])
        gate, up = both[:, :pad], both[:, pad:]
        gelu, slope = gelu_parts(gate)
        act = (gelu * up).astype(BF)
        store(half, gelu.astype(BF), (up * slope).astype(BF), act)
        part = dot(act, down[...])
        total = part if total is None else total + part
    return total.astype(BF)


def ffn_back_rows(tokens, kept, w_gu, w_down, store):
    total = None
    for half, (gu, down) in enumerate(zip(w_gu, w_down)):
        gelu, rise = kept(half)
        d_act = dot(tokens, down[...], NT)
        d_gate = (d_act * rise.astype(F32)).astype(BF)
        d_up = (d_act * gelu.astype(F32)).astype(BF)
        store(half, d_gate, d_up)
        pad = down.shape[0]
        part = dot(d_gate, gu[:, :pad], NT) + dot(d_up, gu[:, pad:], NT)
        total = part if total is None else total + part
    return total.astype(BF)


def ffn_grid_kernel(halves, t_ref, *refs):
    w_gu, w_down, refs = refs[:halves], refs[halves : 2 * halves], refs[2 * halves :]

    def store(half, *values):
        for kind, value in enumerate(values):
            refs[kind * halves + half][...] = value

    refs[-1][...] = ffn_rows(t_ref[...], w_gu, w_down, store)


def ffn_back_grid_kernel(halves, t_ref, *refs):
    gelus, rises, w_gu, w_down = (refs[i * halves : (i + 1) * halves] for i in range(4))
    refs = refs[4 * halves :]

    def store(half, *values):
        for kind, value in enumerate(values):
            refs[kind * halves + half][...] = value

    kept = lambda half: (gelus[half][...], rises[half][...])
    refs[-1][...] = ffn_back_rows(t_ref[...], kept, w_gu, w_down, store)


class Leaving:
    def __init__(self, sems):
        self.sems, self.copies = sems, []

    def send(self, source, target):
        copy = pltpu.make_async_copy(source, target, self.sems.at[len(self.copies)])
        copy.start()
        self.copies.append(copy)

    def wait(self):
        for copy in self.copies:
            copy.wait()


class Weights:
    def __init__(self, sources, buffers, sems):
        self.buffers = buffers
        self.copies = []
        for index, (source, buffer) in enumerate(zip(sources, buffers)):
            self.copies.append(pltpu.make_async_copy(source, buffer.at[pl.ds(0, source.shape[0])], sems.at[index]))
        self.used = [False] * len(self.copies)

    def start(self, index):
        self.copies[index].start()

    def __getitem__(self, index):
        if not self.used[index]:
            self.copies[index].wait()
            self.used[index] = True
        return self.buffers[index]


class Lazy:
    def __init__(self, weights, index):
        self.weights, self.index = weights, index

    @property
    def shape(self):
        return self.weights.buffers[self.index].shape

    def __getitem__(self, at):
        return self.weights[self.index][at]


def lazy_weights(sources, buffers, sems, halves, first):
    weights = Weights(sources, buffers, sems)
    for source, buffer in zip(sources, buffers):
        rows = source.shape[0]
        if rows < buffer.shape[0]:
            buffer[rows:] = jnp.zeros((buffer.shape[0] - rows, buffer.shape[1]), BF)
    for half in range(halves):
        for kind in first:
            weights.start(kind * halves + half)
    return [Lazy(weights, half) for half in range(halves)], [Lazy(weights, halves + half) for half in range(halves)]


def ffn_kernel(count, halves, *refs):
    tokens, refs = refs[:count], refs[count:]
    sources, refs = refs[: 2 * halves], refs[2 * halves :]
    t_out, outs, parts = refs[0], refs[1 : 1 + 3 * halves], refs[1 + 3 * halves : 1 + 3 * halves + count]
    refs = refs[1 + 3 * halves + count :]
    buffers, w_buffers, sems, w_sems = refs[: 3 * halves], refs[3 * halves : -2], refs[-2], refs[-1]
    w_gu, w_down = lazy_weights(sources, w_buffers, w_sems, halves, (0, 1))
    leaving = Leaving(sems)
    rows = tokens[0].shape[0]
    for index in range(count):
        at = pl.ds(index * rows, rows)
        leaving.send(tokens[index], t_out.at[at])

        def store(half, *values):
            for kind, value in enumerate(values):
                slot = kind * halves + half
                buffers[slot][at] = value
                leaving.send(buffers[slot].at[at], outs[slot].at[at])

        parts[index][...] = ffn_rows(tokens[index][...], w_gu, w_down, store)
    leaving.wait()


def ffn_back_kernel(count, halves, begin, chained, *refs):
    tokens, refs = refs[:count], refs[count:]
    gelus, rises, sources = refs[:halves], refs[halves : 2 * halves], refs[2 * halves : 4 * halves]
    t_out, refs = refs[4 * halves + chained], refs[4 * halves + chained + 1 :]
    outs, parts = refs[: 2 * halves], refs[2 * halves : 2 * halves + count]
    refs = refs[2 * halves + count :]
    kept_in, buffers, w_buffers = (refs[i * 2 * halves : (i + 1) * 2 * halves] for i in range(3))
    sems, in_sems, w_sems = refs[6 * halves :]
    w_gu, w_down = lazy_weights(sources, w_buffers, w_sems, halves, (1, 0))
    leaving = Leaving(sems)
    rows = tokens[0].shape[0]
    arriving = {}
    for index in range(count):
        at, to = pl.ds(index * rows, rows), pl.ds((begin + index) * rows, rows)
        for half in range(halves):
            for kind, source in enumerate((gelus[half], rises[half])):
                slot = kind * halves + half
                copy = pltpu.make_async_copy(source.at[to], kept_in[slot].at[at], in_sems.at[index * 2 * halves + slot])
                copy.start()
                arriving[index, slot] = copy
    for index in range(count):
        at, to = pl.ds(index * rows, rows), pl.ds((begin + index) * rows, rows)
        leaving.send(tokens[index], t_out.at[to])

        def kept(half):
            for slot in (half, halves + half):
                arriving[index, slot].wait()
            return kept_in[half][at], kept_in[halves + half][at]

        def store(half, *values):
            for kind, value in enumerate(values):
                slot = kind * halves + half
                buffers[slot][at] = value
                leaving.send(buffers[slot].at[at], outs[slot].at[to])

        parts[index][...] = ffn_back_rows(tokens[index][...], kept, w_gu, w_down, store)
    leaving.wait()


def untangle_kernel(dp, seq, place, *refs):
    lines, out = refs[:-1], refs[-1]
    rows = out.shape[0] // (dp * seq)

    def body(me):
        for index, ref in enumerate(lines):
            at = me ^ (index % 4 * 2) ^ (index // 4)
            for d in range(dp):
                start, to = d * rows, (d * seq + at) * rows
                out[to : to + rows] = ref[start : start + rows]

    on_value(place[0], seq, body)


def join_kernel(*refs):
    rows = refs[0].shape[0]
    for index, ref in enumerate(refs[:-1]):
        refs[-1][index * rows : (index + 1) * rows] = ref[...]


def owner_kernel(dp, gate_ref, up_ref, out_ref):
    seq, rows, columns = out_ref.shape
    pad = columns // 2
    chunk = gate_ref.shape[1] // (dp * seq)
    zeros = [] if pad == dp * chunk else [jnp.zeros((rows, pad - dp * chunk), BF)]
    for to in range(seq):
        for half, ref in enumerate((gate_ref, up_ref)):
            cuts = [ref[:, (d * seq + to) * chunk : (d * seq + to + 1) * chunk] for d in range(dp)]
            out_ref[to, :, half * pad : (half + 1) * pad] = jnp.concatenate(cuts + zeros, axis=1)


def columns_kernel(dp, in_ref, out_ref):
    seq = in_ref.shape[0]
    chunk = out_ref.shape[1] // (dp * seq)
    for d in range(dp):
        for at in range(seq):
            start = (d * seq + at) * chunk
            out_ref[:, start : start + chunk] = in_ref[at, :, d * chunk : (d + 1) * chunk].astype(F32)


def add_up(refs):
    total = refs[0][...].astype(F32)
    for ref in refs[1:]:
        total = total + ref[...].astype(F32)
    return total


def middle_kernel(count, chained, *refs):
    parts, (dy_ref, hidden_ref, gains), (out_ref, d_ref, t_ref) = refs[:count], refs[count : count + 3], refs[-3:]
    g_post = gains[3:4]
    ffn_out = add_up(parts)
    out_ref[0, 0] = hidden_ref[...] + rms(ffn_out, g_post)
    back, terms = rms_back(dy_ref[0, 0].astype(F32), ffn_out, g_post)
    d_ref[...] = back.astype(BF)
    t_ref[...] = terms


def attend_back_kernel(reach, count, place, *refs):
    parts, refs = refs[:count], refs[count:]
    dy_ref, hidden_ref, out_ref, q_ref, raw_ref, cos_ref, sin_ref, w_out, gains = refs[:9]
    pairs_refs, refs = refs[9 : 10 + reach], refs[10 + reach :]
    g_attn, g_pre, g_q = gains[1:2], gains[2:3], gains[4:5, :HD]
    dh_ref, da_ref, dq_ref, t_pre, t_attn, t_q = refs[:6]
    back_refs, own_ref, sums = refs[6 : 6 + reach], refs[6 + reach], refs[7 + reach :]
    d_hidden, terms = rms_back(add_up(parts), hidden_ref[...], g_pre)
    t_pre[...] = terms
    d_hidden = d_hidden + dy_ref[0, 0].astype(F32)
    dh_ref[...] = d_hidden
    d_attn, terms = rms_back(d_hidden, out_ref[...], g_attn)
    t_attn[...] = terms
    d_attn = d_attn.astype(BF)
    da_ref[...] = d_attn
    d_heads = dot(d_attn, w_out[...], NT).astype(BF)
    pairs = [p[...].reshape(p.shape[-2:]) for p in pairs_refs]
    masks = masks_of(pairs[0].shape[0], reach, place)
    into = (own_ref,) + tuple(sums)
    total_q = None
    for head in range(q_ref.shape[-1] // HD):
        at = slice(head * HD, (head + 1) * HD)
        query, d_head = q_ref[0, :, at], d_heads[:, at]
        probs = probs_of(query, pairs, masks)
        d_probs = [dot(d_head, p[:, HD:], NT) for p in pairs]
        inner = sum(jnp.sum(p * d, axis=-1, keepdims=True) for p, d in zip(probs, d_probs))
        d_scores = [(p * (d - inner)).astype(BF) for p, d in zip(probs, d_probs)]
        d_query = sum(dot(d, p[:, :HD]) for d, p in zip(d_scores, pairs))
        for ref, d, p in zip(into, d_scores, probs):
            d_keys = dot(d, query, TN)
            d_value = dot(p.astype(BF), d_head, TN)
            if head == 0:
                ref[:, :HD] = d_keys
                ref[:, HD:] = d_value
            else:
                ref[:, :HD] += d_keys
                ref[:, HD:] += d_value
        d_turned = turn_back(d_query * FACTOR, cos_ref[0], sin_ref[0])
        back, terms = rms_back(d_turned, raw_ref[0, :, at], g_q)
        dq_ref[:, at] = back.astype(BF)
        total_q = terms if total_q is None else total_q + terms
    t_q[...] = total_q
    for ref, value in zip(back_refs, sums):
        ref[...] = value[...].astype(BF)


def project_back_kernel(count, chained, *refs):
    parts, refs = refs[:count], refs[count:]
    raw_ref, dq_ref, cos_ref, sin_ref, w_ref, x_ref, dh_ref, gains = refs[:8]
    g_in, g_k = gains[0:1], gains[5:6, :HD]
    in_ref, d_ref, t_in, t_k = refs[-4:]
    qd = dq_ref.shape[-1]
    own = add_up(parts)
    d_turned = turn_back(own[:, :HD], cos_ref[0], sin_ref[0])
    back, terms = rms_back(d_turned, raw_ref[0], g_k)
    t_k[...] = terms
    d_ref[:, :qd] = dq_ref[...]
    d_ref[:, qd : qd + HD] = back.astype(BF)
    d_ref[:, qd + HD :] = own[:, HD:].astype(BF)
    d_normed = dot(d_ref[...], w_ref[...], NT)
    back, terms = rms_back(d_normed, x_ref[0, 0].astype(F32), g_in)
    t_in[...] = terms
    in_ref[0, 0] = dh_ref[...] + back


def weights_kernel(short, wrows, micro, core, *refs):
    attended, d_attn, refs = refs[:micro], refs[micro : 2 * micro], refs[2 * micro :]
    normed, d_raw, terms = refs[0], refs[1 : 1 + micro], refs[1 + micro : 1 + 7 * micro]
    mine, other, total, out_total = refs[1 + 7 * micro :]
    out_weights = None
    for left, right in zip(attended, d_attn):
        term = dot(left[...], right[...], TN)
        out_weights = term if out_weights is None else out_weights + term
    out_total[...] = out_weights
    orows = out_total.shape[0] // (2 * (mine.shape[0] // wrows))
    width = normed.shape[-1]
    ind = d_raw[0].shape[-1]
    weights = None
    for index in range(micro):
        term = dot(normed[index], d_raw[index][...], TN)
        weights = term if weights is None else weights + term
    total[:, :ind] = weights
    sums = []
    for kind in range(6):
        value = terms[kind * micro][...]
        for index in range(1, micro):
            value = value + terms[kind * micro + index][...]
        sums.append(value)
    place = spots(short, wrows, width)
    heads = [dot(jnp.broadcast_to(s, (8, HD)).astype(BF), place, NT)[:1] for s in sums[4:]]
    rows = jnp.concatenate(sums[:4] + heads + [jnp.zeros((LANES - 6, width), F32)], axis=0)
    total[:, ind:] = jnp.transpose(rows)
    odd = core[0] == 1
    for index in range(mine.shape[0] // wrows):
        at = slice(index * wrows, (index + 1) * wrows)
        first = total[2 * index * wrows : (2 * index + 1) * wrows]
        second = total[(2 * index + 1) * wrows : (2 * index + 2) * wrows]
        columns = first.shape[1]
        mine[at, :columns] = jnp.where(odd, second, first).astype(BF)
        other[at, :columns] = jnp.where(odd, first, second).astype(BF)
        first = out_total[2 * index * orows : (2 * index + 1) * orows]
        second = out_total[(2 * index + 1) * orows : (2 * index + 2) * orows]
        at = slice(index * wrows, index * wrows + orows)
        mine[at, columns:] = jnp.where(odd, second, first).astype(BF)
        other[at, columns:] = jnp.where(odd, first, second).astype(BF)
        if orows < wrows:
            rest = slice(index * wrows + orows, (index + 1) * wrows)
            for ref in (mine, other):
                ref[rest, columns:] = jnp.zeros((wrows - orows, ref.shape[1] - columns), BF)


def on_value(scalar, count, body):
    for value in range(count):

        @pl.when(scalar == value)
        def _(value=value):
            body(value)


def line_kernel(both_ref, in_ref, out_ref):
    count, columns = both_ref.shape[0], in_ref.shape[1]
    in_rows, out_rows = in_ref.shape[0] // count, out_ref.shape[0] // count
    end = columns + out_ref.shape[1]
    for at in range(count):
        in_ref[at * in_rows : (at + 1) * in_rows] = both_ref[at, :in_rows, :columns]
        out_ref[at * out_rows : (at + 1) * out_rows] = both_ref[at, :out_rows, columns:end]


def terms_kernel(count, kinds, has_got, *refs):
    lefts, rights, refs = refs[:count], refs[count : count + count * kinds], refs[count + count * kinds :]
    out = refs[-1]
    wide = out.shape[1] // kinds
    for kind in range(kinds):
        total = None
        for left, right in zip(lefts, rights[kind * count :]):
            term = dot(left[...], right[...], TN)
            total = term if total is None else total + term
        total = total[: out.shape[0]]
        at = slice(kind * wide, (kind + 1) * wide)
        if has_got:
            total = total + refs[0][:, at].astype(F32)
        out[:, at] = total.astype(BF)


def fold_chips_kernel(dp, place, mine, got, line, *sends):
    chips = len(sends) + 1
    rows = line.shape[0] // dp

    def body(chip):
        for index in range(dp):
            for bit in range(chips):
                start = (index * chips + (chip ^ bit)) * rows
                value = mine[start : start + rows].astype(F32) + got[start : start + rows].astype(F32)
                at = slice(index * rows, (index + 1) * rows)
                if bit:
                    sends[bit - 1][at] = value.astype(BF)
                else:
                    line[at] = value

    on_value(place[0], chips, body)


def fold_line_kernel(dp, count, place, *refs):
    parts, (own, *sends) = refs[:count], refs[count:]
    rows = own.shape[0]

    def body(d):
        for by in range(dp):
            start = (d + by) % dp * rows
            value = parts[0][start : start + rows]
            for part in parts[1:]:
                value = value + part[start : start + rows].astype(F32)
            if by:
                sends[by - 1][...] = value.astype(BF)
            else:
                own[...] = value

    on_value(place[0], dp, body)


def finish_kernel(count, *refs):
    parts, outs = refs[:count], refs[count:]
    total = add_up(parts)
    start = 0
    for out in outs[:3]:
        out[...] = total[:, start : start + out.shape[1]]
        start += out.shape[1]
    rows = jnp.transpose(total[:, start : start + LANES])
    for kind, out in enumerate(outs[3:9]):
        out[...] = rows[kind : kind + 1, : out.shape[1]]
    outs[-1][...] = total[: outs[-1].shape[0], start + LANES :]


def after(value, *others):
    return lax.optimization_barrier((value,) + others)[0]


def xor_permute(value, bit, size):
    return lax.ppermute(value, "seq", [(i, i ^ bit) for i in range(size)])


def from_behind(value, by, size):
    pairs = [(i, i + by) for i in range(size) if 0 <= i + by < size]
    return lax.ppermute(value, "seq", pairs)


def near_blocks(own, size, bits=(2, 4, 6)):
    return [xor_permute(own, bit, size) for bit in bits]


class Order:
    def __init__(self):
        self.last = None

    def behind(self, value):
        return value if self.last is None else after(value, self.last)

    def step(self, value):
        self.last = value
        return value


def around(value, by, dp):
    return lax.ppermute(value, "dp", [(i, (i + by) % dp) for i in range(dp)])


def along(value, by, dp):
    return lax.ppermute(value, "dp", [(i, i + by) for i in range(dp) if 0 <= i + by < dp])


def add_up_arrays(parts):
    return functools.reduce(lambda a, b: a + b.astype(F32), parts[1:], parts[0])


VMEM = pl.BlockSpec(memory_space=pltpu.VMEM)
SMEM = pl.BlockSpec(memory_space=pltpu.SMEM)


def plain(array):
    return (array, VMEM)


def fold_chips(mine, got, dp, seq, order):
    dims = (mine.shape[0] * 2 // seq, mine.shape[1])
    chip = order.behind((lax.axis_index("seq") >> 1).reshape(1))
    line, *sends = call(
        functools.partial(fold_chips_kernel, dp),
        None,
        [(chip, SMEM), plain(mine), plain(got)],
        [(shape(dims, F32), VMEM)] + [(shape(dims, BF), VMEM)] * 3,
        name="fold_chips",
    )
    order.step(sends)
    return [line] + [xor_permute(send, bit, seq) for send, bit in zip(sends, (2, 4, 6))]


def fold_line(parts, dp, order):
    dims = (parts[0].shape[0] // dp, parts[0].shape[1])
    place = order.behind(lax.axis_index("dp").reshape(1))
    own, *sends = call(
        functools.partial(fold_line_kernel, dp, len(parts)),
        None,
        [(place, SMEM)] + [plain(part) for part in parts],
        [(shape(dims, F32), VMEM)] + [(shape(dims, BF), VMEM)] * (dp - 1),
        name="fold_line",
    )
    order.step(sends)
    return [own] + [around(send, by, dp) for by, send in enumerate(sends, 1)]


def shards(
    dp,
    seq,
    layer_input,
    out_cotangent,
    seq_lengths,
    inputnorm,
    queryproj,
    keyproj,
    valueproj,
    querynorm,
    keynorm,
    outproj,
    attnnorm,
    prefeednorm,
    gateproj,
    upproj,
    downproj,
    postfeednorm,
):
    micro, _, rows, width = layer_input.shape
    devices = dp * seq
    wrows = width // devices
    qd = queryproj.shape[1]
    ind = qd + 2 * HD
    ff = gateproj.shape[1]
    chunk = ff // devices
    own_ff = dp * chunk
    pad = -(-own_ff // LANES) * LANES
    reach = WINDOW // rows
    split = seq == 8 and dp == 4

    base = lax.axis_index("seq") * rows
    positions = base + jnp.arange(rows, dtype=jnp.int32)
    inverse = jnp.power(F32(10000.0), -2.0 * jnp.arange(HALF, dtype=F32) / HD)
    lengths = seq_lengths[:, 0, 0]
    relative = positions[None, :] & (lengths[:, None] - 1)
    angles = relative.astype(F32)[:, :, None] * inverse
    cosine, sine = jnp.cos(angles), jnp.sin(angles)

    order = Order()
    short = querynorm.shape[0]
    fill = (0, wrows - short)
    gains = [inputnorm, attnnorm, prefeednorm, postfeednorm, jnp.pad(querynorm, fill), jnp.pad(keynorm, fill)]
    gains = jnp.pad(jnp.stack(gains, axis=1), ((0, 0), (0, LANES - len(gains))))
    packed = jnp.concatenate([queryproj, keyproj, valueproj, gains], axis=1)
    along_dp = lax.axis_index("dp").reshape(1)
    if split:
        orows = outproj.shape[0]
        both = jnp.concatenate([packed, jnp.pad(outproj, ((0, wrows - orows), (0, 0)))], axis=1)
        least = -(-(2**19) // (dp * wrows * LANES)) * LANES
        both = jnp.pad(both, ((0, 0), (0, max(0, least - both.shape[1]))))
        both = order.step(lax.optimization_barrier(both[None]))
        line = lax.all_gather(both, "dp", axis=0, tiled=True)

    [gate_up] = call(
        functools.partial(owner_kernel, dp),
        None,
        [plain(gateproj), plain(upproj)],
        [(shape((seq, wrows, 2 * pad), BF), VMEM)],
        name="owner",
    )
    gate_up = lax.all_to_all(gate_up, "seq", 0, 0).reshape(seq * wrows, 2 * pad)
    w_gu = [lax.all_gather(gate_up, "dp", axis=0, tiled=True)]
    if split:
        cosine, sine, line = order.step(order.behind((cosine, sine, line)))
        downproj = after(downproj, line)
    w_down = lax.all_gather(downproj, "dp", axis=0, tiled=True)
    if split:
        in_line, out_line = call(
            line_kernel,
            None,
            [plain(line)],
            [(shape((dp * wrows, ind + LANES), BF), VMEM), (shape((dp * orows, width), BF), VMEM)],
            name="line",
        )

        def untangle(lines, name):
            [array] = call(
                functools.partial(untangle_kernel, dp, seq),
                None,
                [(lax.axis_index("seq").reshape(1), SMEM)] + [plain(line) for line in lines],
                [(shape((lines[0].shape[0] * seq, lines[0].shape[1]), BF), VMEM)],
                name=name,
            )
            return array

        in_lines = [in_line] + near_blocks(order.step(in_line), seq)
        in_lines = order.step(order.behind(in_lines))
        out_lines = [out_line] + near_blocks(after(out_line, in_lines), seq)
        in_lines = in_lines + [xor_permute(line, 1, seq) for line in in_lines]
        in_lines = order.step(order.behind(in_lines))
        w_in = untangle(in_lines, "untangle_in")
        order.step(w_in)
    else:
        w_in = lax.all_gather(packed[None], BOTH, axis=0, tiled=True).reshape(width, -1)
        w_out = lax.all_gather(outproj, BOTH, axis=0, tiled=True)

    def of_micro(array, index):
        dims = array.shape[1:]
        return (array, pl.BlockSpec((1,) + dims, lambda *_: (index,) + (0,) * len(dims)))

    def full(array):
        return (array, whole(array))

    def new(dims, dtype):
        return (shape(dims, dtype), pl.BlockSpec(dims, lambda *_: (0,) * len(dims)))

    smem = pl.BlockSpec(memory_space=pltpu.SMEM)
    each = lambda *dims: pl.BlockSpec((1,) + dims, lambda i: (i,) + (0,) * len(dims))
    w_in_spec = pl.BlockSpec((width, ind), lambda *_: (0, 0))

    cosine = order.behind(cosine)
    gains_spec = pl.BlockSpec((width, LANES), lambda *_: (0, ind // LANES))
    normed_in, raw, query, pair, gains = call(
        functools.partial(project_kernel, short, wrows),
        (micro,),
        [(layer_input, each(1, rows, width)), (w_in, w_in_spec), (w_in, gains_spec)]
        + [(cosine, each(rows, HALF)), (sine, each(rows, HALF))],
        [
            (shape((micro, rows, width), BF), each(rows, width)),
            (shape((micro, rows, qd + HD), F32), each(rows, qd + HD)),
            (shape((micro, rows, qd), BF), each(rows, qd)),
            (shape((micro, rows, 2 * HD), BF), each(rows, 2 * HD)),
            new((8, width), F32),
        ],
        name="project",
    )

    order.step(pair)
    behind = [from_behind(pair, by, seq) for by in range(1, reach + 1)]
    if split:
        out_lines = order.step(order.behind(out_lines))
        out_lines = out_lines + [xor_permute(line, 1, seq) for line in out_lines]
        out_lines = order.step(order.behind(out_lines))
        w_out = order.step(untangle(out_lines, "untangle_out"))
    states = []
    for index in range(micro):
        place = order.behind(jnp.stack([lengths[index], base]))
        pairs = [of_micro(p, index) for p in [pair] + behind]
        attended, attn_out, hidden, normed_ffn = call(
            functools.partial(attend_kernel, reach),
            (1,),
            [(place, smem), of_micro(layer_input, index), of_micro(query, index)]
            + pairs
            + [full(w_out), full(gains)],
            [new((rows, qd), BF), new((rows, width), F32), new((rows, width), F32), new((rows, width), BF)],
            name="attend",
        )
        order.step(normed_ffn)
        s = dict(place=place, pairs=pairs, attended=attended, attn_out=attn_out, hidden=hidden)
        s["sent"] = near_blocks(normed_ffn, seq, BITS) if split else None
        s["nf"] = normed_ffn
        states.append(s)

    if split:
        states[0]["sent"] = order.step(order.behind(states[0]["sent"]))
        w_gu.append(xor_permute(order.step(order.behind(w_gu[0])), 1, seq))
        w_down = [order.step(order.behind(w_down))]
        w_down.append(xor_permute(w_down[0], 1, seq))
    else:
        w_down = [jnp.pad(w_down, ((0, pad - own_ff), (0, 0)))]
    halves = len(w_gu)

    def blocks(array):
        return (array, pl.BlockSpec((rows, array.shape[1]), lambda i: (i, 0)))

    def made(count, columns):
        return (shape((count, columns), BF), pl.BlockSpec((rows, columns), lambda i: (i, 0)))

    def fixed(array):
        return (array, pl.BlockSpec(array.shape, lambda *_: (0,) * array.ndim, pipeline_mode=pl.Buffered(1)))

    def block(index_of, columns):
        return pl.BlockSpec((rows, columns), index_of)

    any_spec = pl.BlockSpec(memory_space=pl.ANY)
    w_scratch = [pltpu.VMEM((width, 2 * pad), BF)] * halves + [pltpu.VMEM((pad, width), BF)] * halves

    def ffn(pieces):
        if not split:
            count = pieces[0].shape[0] // rows
            results = call(
                functools.partial(ffn_grid_kernel, halves),
                (count,),
                [blocks(pieces[0])] + [fixed(w) for w in w_gu] + [fixed(w) for w in w_down],
                [made(count * rows, pad)] * 3 + [made(count * rows, width)],
                name="ffn",
            )
            return pieces[0], results[:1], results[1:2], results[2:3], results[3:]
        count = len(pieces)
        results = call(
            functools.partial(ffn_kernel, count, halves),
            None,
            [plain(array) for array in order.behind(pieces)] + [(w, any_spec) for w in [*w_gu, *w_down]],
            [(shape((count * rows, width), BF), any_spec)]
            + [(shape((count * rows, pad), BF), any_spec)] * (3 * halves)
            + [(shape((rows, width), BF), VMEM)] * count,
            scratch=[pltpu.VMEM((count * rows, pad), BF)] * (3 * halves)
            + w_scratch
            + [pltpu.SemaphoreType.DMA((count * (1 + 3 * halves),)), pltpu.SemaphoreType.DMA((2 * halves,))],
            name="ffn",
        )
        kinds = [results[1 + i * halves : 1 + (i + 1) * halves] for i in range(3)]
        return results[0], *kinds, results[1 + 3 * halves :]

    def ffn_backward(pieces, gelu, rise, begin=0, total=0, kept=()):
        if not split:
            count = pieces[0].shape[0] // rows
            results = call(
                functools.partial(ffn_back_grid_kernel, halves),
                (count,),
                [blocks(pieces[0]), *map(blocks, gelu), *map(blocks, rise)]
                + [fixed(w) for w in w_gu]
                + [fixed(w) for w in w_down],
                [made(count * rows, pad)] * 2 + [made(count * rows, width)],
                name="ffn_back",
            )
            return pieces[0], results[:1], results[1:2], results[2:]
        count = len(pieces)
        arrays = [*gelu, *rise, *w_gu, *w_down, *kept]
        results = call(
            functools.partial(ffn_back_kernel, count, halves, begin, len(kept)),
            None,
            [plain(piece) for piece in pieces] + [(array, any_spec) for array in arrays],
            [(shape((total * rows, width), BF), any_spec)]
            + [(shape((total * rows, pad), BF), any_spec)] * (2 * halves)
            + [(shape((rows, width), BF), VMEM)] * count,
            scratch=[pltpu.VMEM((count * rows, pad), BF)] * (4 * halves)
            + w_scratch
            + [pltpu.SemaphoreType.DMA((count * (1 + 2 * halves),)), pltpu.SemaphoreType.DMA((count * 2 * halves,))]
            + [pltpu.SemaphoreType.DMA((2 * halves,))],
            aliases={count + len(arrays) - len(kept) + index: index for index in range(len(kept))},
            name="ffn_back",
        )
        return results[0], results[1 : 1 + halves], results[1 + halves : 1 + 2 * halves], results[1 + 2 * halves :]

    def pieces_of(own, near):
        if not split:
            return [lax.all_gather(order.behind(own), "seq", axis=0, tiled=True)]
        return list(near) + [order.behind(own)]

    def scatter(parts):
        if not split:
            return [lax.psum_scatter(parts[0], "seq", scatter_dimension=0, tiled=True)]
        return [parts[-1]] + [xor_permute(part, bit, seq) for part, bit in zip(parts, BITS)]

    for s in states:
        pieces = pieces_of(s["nf"], s["sent"])
        s["tokens"], s["gelu"], s["rise"], s["act"], parts = ffn(pieces)
        order.step(parts)
        s["terms"] = scatter(parts)

    def join(pieces):
        [joined] = call(
            join_kernel,
            None,
            [plain(piece) for piece in pieces],
            [(shape((len(pieces) * rows, width), BF), VMEM)],
            name="join",
        )
        return joined

    def over_tokens(left, rights, half, got=None, high_out=None):
        of = lambda s, name: s[name] if name in ("tokens", "d_tokens") else s[name][half]
        lefts = order.behind([of(s, left) for s in states])
        others = [of(s, right) for right in rights for s in states]
        count, high, wide = lefts[0].shape[0], lefts[0].shape[1], others[0].shape[1]
        by_rows = high % 384 == 0
        moving = lambda columns: pl.BlockSpec((count, columns), lambda i: (0, i))
        staying = lambda columns: pl.BlockSpec((count, columns), lambda i: (0, 0), pipeline_mode=pl.Buffered(1))
        if by_rows:
            steps, left_spec, right_spec = high // 384, moving(384), staying(wide)
            out_spec = pl.BlockSpec((384, wide * len(rights)), lambda i: (i, 0))
        else:
            steps, left_spec, right_spec = wide // 384, staying(high), moving(384)
            out_spec = pl.BlockSpec((high_out or high, 384), lambda i: (0, i))
        [made_terms] = call(
            functools.partial(terms_kernel, micro, len(rights), got is not None),
            (steps,),
            [(a, left_spec) for a in lefts]
            + [(b, right_spec) for b in others]
            + ([] if got is None else [(got, out_spec)]),
            [(shape((high_out or high, wide * len(rights)), BF), out_spec)],
            name="terms",
        )
        return order.step(made_terms)

    def other_terms(left, rights, high_out=None):
        return over_tokens(left, rights, 1, None, high_out) if split else None

    def own_terms(left, rights, other, high_out=None):
        return over_tokens(left, rights, 0, xor_permute(other, 1, seq) if split else None, high_out)

    def ffn_back(s, which):
        if not split:
            if which == "rest":
                pieces = pieces_of(s["d_ffn"], s["sent"])
                s["d_tokens"], s["d_gate"], s["d_up"], parts = ffn_backward(pieces, s["gelu"], s["rise"])
                s["terms"] = scatter(order.step(parts))
            return
        own, others = [order.behind(s["d_ffn"])], list(s["sent"])
        total = len(own) + len(others)
        if which == "own":
            s["kept"] = ffn_backward(own, s["gelu"], s["rise"], len(others), total)
            order.step(s["kept"][-1])
            return
        tokens, d_gate, d_up, last = s["kept"]
        others[0] = order.behind(others[0])
        tokens, s["d_gate"], s["d_up"], parts = ffn_backward(
            others, s["gelu"], s["rise"], 0, total, [tokens, *d_gate, *d_up]
        )
        s.setdefault("d_tokens", tokens)
        s["terms"] = scatter(order.step(list(parts)) + list(last))

    layer_out = None
    result = shape((micro, 1, rows, width), F32)
    for index, s in enumerate(states):
        parts = s["terms"]
        chain = [] if layer_out is None else [(layer_out, pl.BlockSpec(memory_space=pl.ANY))]
        layer_out, s["d_ffn"], s["t_post"] = call(
            functools.partial(middle_kernel, len(parts), bool(chain)),
            (1,),
            [full(p) for p in parts]
            + [of_micro(out_cotangent, index), full(s["hidden"]), full(order.behind(gains))]
            + chain,
            [(result, of_micro(result, index)[1]), new((rows, width), BF), new((1, width), F32)],
            aliases={len(parts) + 3: 0} if chain else None,
            name="middle",
        )
        order.step(s["d_ffn"])
        s["sent"] = near_blocks(s["d_ffn"], seq, BITS) if split else None
        ffn_back(s, "own")

    for s in states[:-1]:
        ffn_back(s, "rest")
    late = states[-1]
    if split:
        late["sent"] = order.step(order.behind(late["sent"]))
        late["d_tokens"] = order.step(join(list(late["sent"]) + [late["d_ffn"]]))
        down_other = other_terms("act", ["d_tokens"], own_ff)
    ffn_back(late, "rest")
    down_terms = own_terms("act", ["d_tokens"], down_other if split else None, own_ff)
    for s in states[:-1]:
        s["terms"] = order.step(order.behind(s["terms"]))
    down_grad = lax.psum_scatter(order.behind(down_terms), "dp", scatter_dimension=0, tiled=True)

    def attend_back(index):
        s = states[index]
        parts = s["terms"]
        backs = call(
            functools.partial(attend_back_kernel, reach, len(parts)),
            (1,),
            [(order.behind(s["place"]), smem)]
            + [full(p) for p in parts]
            + [of_micro(out_cotangent, index), full(s["hidden"]), full(s["attn_out"]), of_micro(query, index)]
            + [of_micro(raw, index), of_micro(cosine, index), of_micro(sine, index)]
            + [full(w_out), full(gains)]
            + s["pairs"],
            [new((rows, width), F32), new((rows, width), BF), new((rows, qd), BF)]
            + [new((1, width), F32), new((1, width), F32), new((1, HD), F32)]
            + [new((rows, 2 * HD), BF)] * reach
            + [new((rows, 2 * HD), F32)],
            scratch=[pltpu.VMEM((rows, 2 * HD), F32)] * reach,
            name="attend_back",
        )
        s["d_hidden"], s["d_attn"], s["d_raw_q"], s["t_pre"], s["t_attn"], s["t_query"] = backs[:6]
        order.step(s["d_attn"])
        sent, own = backs[6 : 6 + reach], backs[-1]
        s["d_pairs"] = [own] + [from_behind(value, -by, seq) for by, value in enumerate(sent, 1)]

    def project_back(index, input_grad):
        s = states[index]
        terms = s["d_pairs"]
        chain = [] if input_grad is None else [(input_grad, pl.BlockSpec(memory_space=pl.ANY))]
        keys_spec = pl.BlockSpec((1, rows, HD), lambda *_: (index, 0, qd // HD))
        input_grad, s["d_raw"], s["t_in"], s["t_keys"] = call(
            functools.partial(project_back_kernel, len(terms), bool(chain)),
            (1,),
            [full(t) for t in terms]
            + [(raw, keys_spec), full(s["d_raw_q"]), of_micro(cosine, index), of_micro(sine, index), (w_in, w_in_spec)]
            + [of_micro(layer_input, index), full(s["d_hidden"]), full(order.behind(gains))]
            + chain,
            [(result, of_micro(result, index)[1]), new((rows, ind), BF), new((1, width), F32), new((1, HD), F32)],
            aliases={len(terms) + 8: 0} if chain else None,
            name="project_back",
        )
        order.step(s["d_raw"])
        s["normed_in"] = normed_in[index]
        return input_grad

    def columns_of(part, index):
        [columns] = call(
            functools.partial(columns_kernel, dp),
            (1,),
            [(part, pl.BlockSpec((seq, wrows, pad), lambda *_: (0, 0, index)))],
            [(shape((wrows, ff), F32), pl.BlockSpec((wrows, ff), lambda *_: (0, 0)))],
            name="columns",
        )
        return columns

    input_grad = None
    gu_other = other_terms("tokens", ["d_gate", "d_up"])
    for index in range(micro - 1):
        attend_back(index)
    gu_terms = own_terms("tokens", ["d_gate", "d_up"], gu_other)
    for s in states[:-1]:
        s["d_pairs"] = order.step(order.behind(s["d_pairs"]))
    states[-1]["terms"], down_grad = order.step(order.behind((states[-1]["terms"], down_grad)))
    gu_sum = lax.psum_scatter(order.behind(gu_terms), "dp", scatter_dimension=0, tiled=True)
    attend_back(micro - 1)
    for index in range(micro):
        input_grad = project_back(index, input_grad)
    core = lax.axis_index("seq") & 1
    sums = [s[name] for name in ("t_in", "t_attn", "t_pre", "t_post", "t_query", "t_keys") for s in states]
    half_out = (shape((devices // 2 * wrows, ind + LANES + width), BF), VMEM)
    mine, other = call(
        functools.partial(weights_kernel, short, wrows, micro),
        None,
        [(order.behind((core if split else jnp.int32(0)).reshape(1)), smem)]
        + [plain(s["attended"]) for s in states]
        + [plain(s["d_attn"]) for s in states]
        + [plain(normed_in)]
        + [plain(s["d_raw"]) for s in states]
        + [plain(term) for term in sums],
        [half_out, half_out],
        scratch=[pltpu.VMEM((width, ind + LANES), F32), pltpu.VMEM((qd, width), F32)],
        name="weights",
    )
    order.step(other)
    if split:
        got = xor_permute(other, 1, seq)
        in_parts = fold_chips(mine, got, dp, seq, order)
        in_parts = order.step(order.behind(in_parts))
        gu_sum = order.step(order.behind(gu_sum).reshape(seq, wrows, 2 * pad))
        gu_sum = lax.all_to_all(gu_sum, "seq", 0, 0)
        in_parts = fold_line(in_parts, dp, order)
        gu_sum = order.behind(gu_sum)
        gate_grad, up_grad = order.step([columns_of(gu_sum, index) for index in range(2)])
    else:
        halves_of = [part.reshape(devices // 2, wrows, -1) for part in (mine, other)]
        whole_terms = jnp.stack(halves_of, axis=1).reshape(devices, wrows, -1)
        in_parts = [lax.psum_scatter(whole_terms, BOTH, scatter_dimension=0, tiled=True)[0]]
    q_grad, k_grad, v_grad, *gain_sum, out_grad = call(
        functools.partial(finish_kernel, len(in_parts)),
        None,
        [plain(part) for part in order.behind(list(in_parts))],
        [(shape((wrows, columns), F32), VMEM) for columns in (qd, HD, HD)]
        + [(shape((1, size), F32), VMEM) for size in [wrows] * 4 + [short] * 2]
        + [(shape((qd // devices, width), F32), VMEM)],
        name="finish",
    )

    if not split:
        gu_sum = lax.all_to_all(gu_sum.reshape(seq, wrows, 2 * pad), "seq", 0, 0)
        gate_grad, up_grad = (columns_of(gu_sum, index) for index in range(2))
    down_grad = order.behind(down_grad).astype(F32)

    return (
        layer_out,
        input_grad,
        gain_sum[0].reshape(wrows),
        q_grad,
        k_grad,
        v_grad,
        gain_sum[4].reshape(short),
        gain_sum[5].reshape(short),
        out_grad,
        gain_sum[1].reshape(wrows),
        gain_sum[2].reshape(wrows),
        gate_grad,
        up_grad,
        down_grad,
        gain_sum[3].reshape(wrows),
    )


def solution(mesh):
    dp, seq = mesh.shape["dp"], mesh.shape["seq"]
    acts = P(None, "dp", "seq", None)
    vector = P(BOTH)
    matrix = P(BOTH, None)
    weights = (vector,) + (matrix,) * 3 + (vector,) * 2 + (matrix, vector, vector) + (matrix,) * 3 + (vector,)
    return jax.shard_map(
        functools.partial(shards, dp, seq),
        mesh=mesh,
        in_specs=(acts, acts, P(None, "dp", None)) + weights,
        out_specs=(acts, acts) + weights,
        check_vma=False,
    )
```

```python
import functools
import math

import jax
import jax.numpy as jnp
from jax import lax
from jax.experimental import pallas as pl
from jax.experimental.pallas import tpu as pltpu
from jax.sharding import PartitionSpec as P

HEADS = 4
HD = 256
HALF = HD // 2
WINDOW = 512
EPS = 1e-06
LANES = 128
FACTOR = 1.0 / math.sqrt(HD)
GELU_C = math.sqrt(2.0 / math.pi)
NEG = -1e30

BF = jnp.bfloat16
F32 = jnp.float32
BOTH = ("dp", "seq")
BITS = (6, 2, 4)
NN = ((1,), (0,))
NT = ((1,), (1,))
TN = ((0,), (0,))


def dot(left, right, dims=NN):
    return lax.dot_general(left, right, (dims, ((), ())), preferred_element_type=F32)


def shape(dims, dtype):
    return jax.ShapeDtypeStruct(dims, dtype)


def whole(array):
    return pl.BlockSpec(array.shape, lambda *_: (0,) * array.ndim)


def call(body, grid, inputs, outs, scratch=(), aliases=None, name=None):
    return pl.pallas_call(
        body,
        **({} if grid is None else {"grid": grid}),
        in_specs=[spec for _, spec in inputs],
        out_specs=[spec for _, spec in outs],
        out_shape=[made for made, _ in outs],
        scratch_shapes=list(scratch),
        input_output_aliases=aliases or {},
        compiler_params=pltpu.CompilerParams(vmem_limit_bytes=58 * 2**20),
        cost_estimate=pl.CostEstimate(flops=0, bytes_accessed=1, transcendentals=0),
        name=name,
    )(*[array for array, _ in inputs])


def scale_of(values):
    return lax.rsqrt(jnp.mean(values * values, axis=-1, keepdims=True) + EPS)


def rms(values, gain):
    return values * scale_of(values) * (1.0 + gain)


def rms_back(grad, values, gain):
    scale = scale_of(values)
    normed = values * scale
    inner = grad * (1.0 + gain)
    back = scale * (inner - normed * jnp.mean(inner * normed, axis=-1, keepdims=True))
    return back, jnp.sum(grad * normed, axis=0, keepdims=True)


def turn(values, cosine, sine):
    first, second = values[:, :HALF], values[:, HALF:]
    return jnp.concatenate([first * cosine - second * sine, second * cosine + first * sine], axis=1)


def turn_back(grad, cosine, sine):
    first, second = grad[:, :HALF], grad[:, HALF:]
    return jnp.concatenate([first * cosine + second * sine, second * cosine - first * sine], axis=1)


def gelu_parts(value):
    inner = GELU_C * (value + 0.044715 * value * value * value)
    tanh = jnp.tanh(inner)
    gelu = 0.5 * value * (1.0 + tanh)
    slope = 0.5 * (1.0 + tanh) + 0.5 * value * (1.0 - tanh * tanh) * GELU_C * (1.0 + 3 * 0.044715 * value * value)
    return gelu, slope


def spots(short, wrows, width):
    row = lax.broadcasted_iota(jnp.int32, (width, HD), 0)
    entry = lax.broadcasted_iota(jnp.int32, (width, HD), 1)
    bits = short.bit_length() - 1
    return (row == (entry >> bits) * wrows + (entry & (short - 1))).astype(F32).astype(BF)


def project_kernel(
    short, wrows, x_ref, w_ref, packed_ref, cos_ref, sin_ref, normed_ref, raw_ref, q_ref, pair_ref, gains_ref
):
    qd = q_ref.shape[-1]
    width = x_ref.shape[-1]
    gains_ref[...] = jnp.transpose(packed_ref[...].astype(F32))[:8]
    heads = dot(packed_ref[...], spots(short, wrows, width), TN)
    gains_ref[4:6, :HD] = heads[4:6]
    g_q, g_k = heads[4:5], heads[5:6]
    normed = rms(x_ref[0, 0].astype(F32), gains_ref[0:1]).astype(BF)
    normed_ref[0] = normed
    raw = dot(normed, w_ref[...])
    raw_ref[0] = raw[:, : qd + HD]
    cosine, sine = cos_ref[0], sin_ref[0]
    for head in range(qd // HD):
        at = slice(head * HD, (head + 1) * HD)
        q_ref[0, :, at] = (turn(rms(raw[:, at], g_q), cosine, sine) * FACTOR).astype(BF)
    keys = turn(rms(raw[:, qd : qd + HD], g_k), cosine, sine)
    pair_ref[0, :, :HD] = keys.astype(BF)
    pair_ref[0, :, HD:] = raw[:, qd + HD :].astype(BF)


def masks_of(rows, reach, place):
    length, base = place[0], place[1]
    query = lax.broadcasted_iota(jnp.int32, (rows, rows), 0)
    keys = lax.broadcasted_iota(jnp.int32, (rows, rows), 1)
    first = base & -length
    masks = []
    for by in range(reach + 1):
        behind = query - keys + by * rows
        valid = jnp.where(base - by * rows >= first, WINDOW, -1)
        masks.append((behind >= 0) & (behind < valid))
    return masks


def probs_of(query, pairs, masks):
    scores = [jnp.where(m, dot(query, p[:, :HD], NT), NEG) for p, m in zip(pairs, masks)]
    top = functools.reduce(jnp.maximum, [jnp.max(s, axis=-1, keepdims=True) for s in scores])
    raised = [jnp.exp(s - top) for s in scores]
    total = functools.reduce(jnp.add, [jnp.sum(e, axis=-1, keepdims=True) for e in raised])
    return [e * (1.0 / total) for e in raised]


def attend_kernel(reach, place, x_ref, q_ref, *rest):
    pairs_refs, (w_out, gains, att_ref, out_ref, hidden_ref, nf_ref) = rest[: reach + 1], rest[reach + 1 :]
    pairs = [p[...].reshape(p.shape[-2:]) for p in pairs_refs]
    masks = masks_of(pairs[0].shape[0], reach, place)
    qd = q_ref.shape[-1]
    for head in range(qd // HD):
        at = slice(head * HD, (head + 1) * HD)
        probs = probs_of(q_ref[0, :, at], pairs, masks)
        mixed = sum(dot(p.astype(BF), v[:, HD:]) for p, v in zip(probs, pairs))
        att_ref[:, at] = mixed.astype(BF)
    out = dot(att_ref[...], w_out[...])
    out_ref[...] = out
    hidden = x_ref[0, 0].astype(F32) + rms(out, gains[1:2])
    hidden_ref[...] = hidden
    nf_ref[...] = rms(hidden, gains[2:3]).astype(BF)


def ffn_rows(tokens, w_gu, w_down, store):
    total = None
    for half, (gu, down) in enumerate(zip(w_gu, w_down)):
        pad = down.shape[0]
        both = dot(tokens, gu[...])
        gate, up = both[:, :pad], both[:, pad:]
        gelu, slope = gelu_parts(gate)
        act = (gelu * up).astype(BF)
        store(half, gelu.astype(BF), (up * slope).astype(BF), act)
        part = dot(act, down[...])
        total = part if total is None else total + part
    return total.astype(BF)


def ffn_back_rows(tokens, kept, w_gu, w_down, store):
    total = None
    for half, (gu, down) in enumerate(zip(w_gu, w_down)):
        gelu, rise = kept(half)
        d_act = dot(tokens, down[...], NT)
        d_gate = (d_act * rise.astype(F32)).astype(BF)
        d_up = (d_act * gelu.astype(F32)).astype(BF)
        store(half, d_gate, d_up)
        pad = down.shape[0]
        part = dot(d_gate, gu[:, :pad], NT) + dot(d_up, gu[:, pad:], NT)
        total = part if total is None else total + part
    return total.astype(BF)


def ffn_grid_kernel(halves, t_ref, *refs):
    w_gu, w_down, refs = refs[:halves], refs[halves : 2 * halves], refs[2 * halves :]

    def store(half, *values):
        for kind, value in enumerate(values):
            refs[kind * halves + half][...] = value

    refs[-1][...] = ffn_rows(t_ref[...], w_gu, w_down, store)


def ffn_back_grid_kernel(halves, t_ref, *refs):
    gelus, rises, w_gu, w_down = (refs[i * halves : (i + 1) * halves] for i in range(4))
    refs = refs[4 * halves :]

    def store(half, *values):
        for kind, value in enumerate(values):
            refs[kind * halves + half][...] = value

    kept = lambda half: (gelus[half][...], rises[half][...])
    refs[-1][...] = ffn_back_rows(t_ref[...], kept, w_gu, w_down, store)


class Leaving:
    def __init__(self, sems):
        self.sems, self.copies = sems, []

    def send(self, source, target):
        copy = pltpu.make_async_copy(source, target, self.sems.at[len(self.copies)])
        copy.start()
        self.copies.append(copy)

    def wait(self):
        for copy in self.copies:
            copy.wait()


class Weights:
    def __init__(self, sources, buffers, sems):
        self.buffers = buffers
        self.copies = []
        for index, (source, buffer) in enumerate(zip(sources, buffers)):
            self.copies.append(pltpu.make_async_copy(source, buffer.at[pl.ds(0, source.shape[0])], sems.at[index]))
        self.used = [False] * len(self.copies)

    def start(self, index):
        self.copies[index].start()

    def __getitem__(self, index):
        if not self.used[index]:
            self.copies[index].wait()
            self.used[index] = True
        return self.buffers[index]


class Lazy:
    def __init__(self, weights, index):
        self.weights, self.index = weights, index

    @property
    def shape(self):
        return self.weights.buffers[self.index].shape

    def __getitem__(self, at):
        return self.weights[self.index][at]


def lazy_weights(sources, buffers, sems, halves, first):
    weights = Weights(sources, buffers, sems)
    for source, buffer in zip(sources, buffers):
        rows = source.shape[0]
        if rows < buffer.shape[0]:
            buffer[rows:] = jnp.zeros((buffer.shape[0] - rows, buffer.shape[1]), BF)
    for half in range(halves):
        for kind in first:
            weights.start(kind * halves + half)
    return [Lazy(weights, half) for half in range(halves)], [Lazy(weights, halves + half) for half in range(halves)]


def ffn_kernel(count, halves, *refs):
    tokens, refs = refs[:count], refs[count:]
    sources, refs = refs[: 2 * halves], refs[2 * halves :]
    t_out, outs, parts = refs[0], refs[1 : 1 + 3 * halves], refs[1 + 3 * halves : 1 + 3 * halves + count]
    refs = refs[1 + 3 * halves + count :]
    buffers, w_buffers, sems, w_sems = refs[: 3 * halves], refs[3 * halves : -2], refs[-2], refs[-1]
    w_gu, w_down = lazy_weights(sources, w_buffers, w_sems, halves, (0, 1))
    leaving = Leaving(sems)
    rows = tokens[0].shape[0]
    for index in range(count):
        at = pl.ds(index * rows, rows)
        leaving.send(tokens[index], t_out.at[at])

        def store(half, *values):
            for kind, value in enumerate(values):
                slot = kind * halves + half
                buffers[slot][at] = value
                leaving.send(buffers[slot].at[at], outs[slot].at[at])

        parts[index][...] = ffn_rows(tokens[index][...], w_gu, w_down, store)
    leaving.wait()


def ffn_back_kernel(count, halves, begin, chained, *refs):
    tokens, refs = refs[:count], refs[count:]
    gelus, rises, sources = refs[:halves], refs[halves : 2 * halves], refs[2 * halves : 4 * halves]
    t_out, refs = refs[4 * halves + chained], refs[4 * halves + chained + 1 :]
    outs, parts = refs[: 2 * halves], refs[2 * halves : 2 * halves + count]
    refs = refs[2 * halves + count :]
    kept_in, buffers, w_buffers = (refs[i * 2 * halves : (i + 1) * 2 * halves] for i in range(3))
    sems, in_sems, w_sems = refs[6 * halves :]
    w_gu, w_down = lazy_weights(sources, w_buffers, w_sems, halves, (1, 0))
    leaving = Leaving(sems)
    rows = tokens[0].shape[0]
    arriving = {}
    for index in range(count):
        at, to = pl.ds(index * rows, rows), pl.ds((begin + index) * rows, rows)
        for half in range(halves):
            for kind, source in enumerate((gelus[half], rises[half])):
                slot = kind * halves + half
                copy = pltpu.make_async_copy(source.at[to], kept_in[slot].at[at], in_sems.at[index * 2 * halves + slot])
                copy.start()
                arriving[index, slot] = copy
    for index in range(count):
        at, to = pl.ds(index * rows, rows), pl.ds((begin + index) * rows, rows)
        leaving.send(tokens[index], t_out.at[to])

        def kept(half):
            for slot in (half, halves + half):
                arriving[index, slot].wait()
            return kept_in[half][at], kept_in[halves + half][at]

        def store(half, *values):
            for kind, value in enumerate(values):
                slot = kind * halves + half
                buffers[slot][at] = value
                leaving.send(buffers[slot].at[at], outs[slot].at[to])

        parts[index][...] = ffn_back_rows(tokens[index][...], kept, w_gu, w_down, store)
    leaving.wait()


def untangle_kernel(dp, seq, place, *refs):
    lines, out = refs[:-1], refs[-1]
    rows = out.shape[0] // (dp * seq)

    def body(me):
        for index, ref in enumerate(lines):
            at = me ^ (index % 4 * 2) ^ (index // 4)
            for d in range(dp):
                start, to = d * rows, (d * seq + at) * rows
                out[to : to + rows] = ref[start : start + rows]

    on_value(place[0], seq, body)


def join_kernel(*refs):
    rows = refs[0].shape[0]
    for index, ref in enumerate(refs[:-1]):
        refs[-1][index * rows : (index + 1) * rows] = ref[...]


def owner_kernel(dp, gate_ref, up_ref, out_ref):
    seq, rows, columns = out_ref.shape
    pad = columns // 2
    chunk = gate_ref.shape[1] // (dp * seq)
    zeros = [] if pad == dp * chunk else [jnp.zeros((rows, pad - dp * chunk), BF)]
    for to in range(seq):
        for half, ref in enumerate((gate_ref, up_ref)):
            cuts = [ref[:, (d * seq + to) * chunk : (d * seq + to + 1) * chunk] for d in range(dp)]
            out_ref[to, :, half * pad : (half + 1) * pad] = jnp.concatenate(cuts + zeros, axis=1)


def columns_kernel(dp, in_ref, out_ref):
    seq = in_ref.shape[0]
    chunk = out_ref.shape[1] // (dp * seq)
    for d in range(dp):
        for at in range(seq):
            start = (d * seq + at) * chunk
            out_ref[:, start : start + chunk] = in_ref[at, :, d * chunk : (d + 1) * chunk].astype(F32)


def add_up(refs):
    total = refs[0][...].astype(F32)
    for ref in refs[1:]:
        total = total + ref[...].astype(F32)
    return total


def middle_kernel(count, chained, *refs):
    parts, (dy_ref, hidden_ref, gains), (out_ref, d_ref, t_ref) = refs[:count], refs[count : count + 3], refs[-3:]
    g_post = gains[3:4]
    ffn_out = add_up(parts)
    out_ref[0, 0] = hidden_ref[...] + rms(ffn_out, g_post)
    back, terms = rms_back(dy_ref[0, 0].astype(F32), ffn_out, g_post)
    d_ref[...] = back.astype(BF)
    t_ref[...] = terms


def attend_back_kernel(reach, count, place, *refs):
    parts, refs = refs[:count], refs[count:]
    dy_ref, hidden_ref, out_ref, q_ref, raw_ref, cos_ref, sin_ref, w_out, gains = refs[:9]
    pairs_refs, refs = refs[9 : 10 + reach], refs[10 + reach :]
    g_attn, g_pre, g_q = gains[1:2], gains[2:3], gains[4:5, :HD]
    dh_ref, da_ref, dq_ref, t_pre, t_attn, t_q = refs[:6]
    back_refs, own_ref, sums = refs[6 : 6 + reach], refs[6 + reach], refs[7 + reach :]
    d_hidden, terms = rms_back(add_up(parts), hidden_ref[...], g_pre)
    t_pre[...] = terms
    d_hidden = d_hidden + dy_ref[0, 0].astype(F32)
    dh_ref[...] = d_hidden
    d_attn, terms = rms_back(d_hidden, out_ref[...], g_attn)
    t_attn[...] = terms
    d_attn = d_attn.astype(BF)
    da_ref[...] = d_attn
    d_heads = dot(d_attn, w_out[...], NT).astype(BF)
    pairs = [p[...].reshape(p.shape[-2:]) for p in pairs_refs]
    masks = masks_of(pairs[0].shape[0], reach, place)
    into = (own_ref,) + tuple(sums)
    total_q = None
    for head in range(q_ref.shape[-1] // HD):
        at = slice(head * HD, (head + 1) * HD)
        query, d_head = q_ref[0, :, at], d_heads[:, at]
        probs = probs_of(query, pairs, masks)
        d_probs = [dot(d_head, p[:, HD:], NT) for p in pairs]
        inner = sum(jnp.sum(p * d, axis=-1, keepdims=True) for p, d in zip(probs, d_probs))
        d_scores = [(p * (d - inner)).astype(BF) for p, d in zip(probs, d_probs)]
        d_query = sum(dot(d, p[:, :HD]) for d, p in zip(d_scores, pairs))
        for ref, d, p in zip(into, d_scores, probs):
            d_keys = dot(d, query, TN)
            d_value = dot(p.astype(BF), d_head, TN)
            if head == 0:
                ref[:, :HD] = d_keys
                ref[:, HD:] = d_value
            else:
                ref[:, :HD] += d_keys
                ref[:, HD:] += d_value
        d_turned = turn_back(d_query * FACTOR, cos_ref[0], sin_ref[0])
        back, terms = rms_back(d_turned, raw_ref[0, :, at], g_q)
        dq_ref[:, at] = back.astype(BF)
        total_q = terms if total_q is None else total_q + terms
    t_q[...] = total_q
    for ref, value in zip(back_refs, sums):
        ref[...] = value[...].astype(BF)


def project_back_kernel(count, chained, *refs):
    parts, refs = refs[:count], refs[count:]
    raw_ref, dq_ref, cos_ref, sin_ref, w_ref, x_ref, dh_ref, gains = refs[:8]
    g_in, g_k = gains[0:1], gains[5:6, :HD]
    in_ref, d_ref, t_in, t_k = refs[-4:]
    qd = dq_ref.shape[-1]
    own = add_up(parts)
    d_turned = turn_back(own[:, :HD], cos_ref[0], sin_ref[0])
    back, terms = rms_back(d_turned, raw_ref[0], g_k)
    t_k[...] = terms
    d_ref[:, :qd] = dq_ref[...]
    d_ref[:, qd : qd + HD] = back.astype(BF)
    d_ref[:, qd + HD :] = own[:, HD:].astype(BF)
    d_normed = dot(d_ref[...], w_ref[...], NT)
    back, terms = rms_back(d_normed, x_ref[0, 0].astype(F32), g_in)
    t_in[...] = terms
    in_ref[0, 0] = dh_ref[...] + back


def weights_kernel(short, wrows, micro, core, *refs):
    attended, d_attn, refs = refs[:micro], refs[micro : 2 * micro], refs[2 * micro :]
    normed, d_raw, terms = refs[0], refs[1 : 1 + micro], refs[1 + micro : 1 + 7 * micro]
    mine, other, total, out_total = refs[1 + 7 * micro :]
    out_weights = None
    for left, right in zip(attended, d_attn):
        term = dot(left[...], right[...], TN)
        out_weights = term if out_weights is None else out_weights + term
    out_total[...] = out_weights
    orows = out_total.shape[0] // (2 * (mine.shape[0] // wrows))
    width = normed.shape[-1]
    ind = d_raw[0].shape[-1]
    weights = None
    for index in range(micro):
        term = dot(normed[index], d_raw[index][...], TN)
        weights = term if weights is None else weights + term
    total[:, :ind] = weights
    sums = []
    for kind in range(6):
        value = terms[kind * micro][...]
        for index in range(1, micro):
            value = value + terms[kind * micro + index][...]
        sums.append(value)
    place = spots(short, wrows, width)
    heads = [dot(jnp.broadcast_to(s, (8, HD)).astype(BF), place, NT)[:1] for s in sums[4:]]
    rows = jnp.concatenate(sums[:4] + heads + [jnp.zeros((LANES - 6, width), F32)], axis=0)
    total[:, ind:] = jnp.transpose(rows)
    odd = core[0] == 1
    for index in range(mine.shape[0] // wrows):
        at = slice(index * wrows, (index + 1) * wrows)
        first = total[2 * index * wrows : (2 * index + 1) * wrows]
        second = total[(2 * index + 1) * wrows : (2 * index + 2) * wrows]
        columns = first.shape[1]
        mine[at, :columns] = jnp.where(odd, second, first).astype(BF)
        other[at, :columns] = jnp.where(odd, first, second).astype(BF)
        first = out_total[2 * index * orows : (2 * index + 1) * orows]
        second = out_total[(2 * index + 1) * orows : (2 * index + 2) * orows]
        at = slice(index * wrows, index * wrows + orows)
        mine[at, columns:] = jnp.where(odd, second, first).astype(BF)
        other[at, columns:] = jnp.where(odd, first, second).astype(BF)
        if orows < wrows:
            rest = slice(index * wrows + orows, (index + 1) * wrows)
            for ref in (mine, other):
                ref[rest, columns:] = jnp.zeros((wrows - orows, ref.shape[1] - columns), BF)


def on_value(scalar, count, body):
    for value in range(count):

        @pl.when(scalar == value)
        def _(value=value):
            body(value)


def line_kernel(both_ref, in_ref, out_ref):
    count, columns = both_ref.shape[0], in_ref.shape[1]
    in_rows, out_rows = in_ref.shape[0] // count, out_ref.shape[0] // count
    end = columns + out_ref.shape[1]
    for at in range(count):
        in_ref[at * in_rows : (at + 1) * in_rows] = both_ref[at, :in_rows, :columns]
        out_ref[at * out_rows : (at + 1) * out_rows] = both_ref[at, :out_rows, columns:end]


def terms_kernel(count, kinds, has_got, *refs):
    lefts, rights, refs = refs[:count], refs[count : count + count * kinds], refs[count + count * kinds :]
    out = refs[-1]
    wide = out.shape[1] // kinds
    for kind in range(kinds):
        total = None
        for left, right in zip(lefts, rights[kind * count :]):
            term = dot(left[...], right[...], TN)
            total = term if total is None else total + term
        total = total[: out.shape[0]]
        at = slice(kind * wide, (kind + 1) * wide)
        if has_got:
            total = total + refs[0][:, at].astype(F32)
        out[:, at] = total.astype(BF)


def fold_chips_kernel(dp, place, mine, got, line, *sends):
    chips = len(sends) + 1
    rows = line.shape[0] // dp

    def body(chip):
        for index in range(dp):
            for bit in range(chips):
                start = (index * chips + (chip ^ bit)) * rows
                value = mine[start : start + rows].astype(F32) + got[start : start + rows].astype(F32)
                at = slice(index * rows, (index + 1) * rows)
                if bit:
                    sends[bit - 1][at] = value.astype(BF)
                else:
                    line[at] = value

    on_value(place[0], chips, body)


def fold_line_kernel(dp, count, place, *refs):
    parts, (own, *sends) = refs[:count], refs[count:]
    rows = own.shape[0]

    def body(d):
        for by in range(dp):
            start = (d + by) % dp * rows
            value = parts[0][start : start + rows]
            for part in parts[1:]:
                value = value + part[start : start + rows].astype(F32)
            if by:
                sends[by - 1][...] = value.astype(BF)
            else:
                own[...] = value

    on_value(place[0], dp, body)


def finish_kernel(count, *refs):
    parts, outs = refs[:count], refs[count:]
    total = add_up(parts)
    start = 0
    for out in outs[:3]:
        out[...] = total[:, start : start + out.shape[1]]
        start += out.shape[1]
    rows = jnp.transpose(total[:, start : start + LANES])
    for kind, out in enumerate(outs[3:9]):
        out[...] = rows[kind : kind + 1, : out.shape[1]]
    outs[-1][...] = total[: outs[-1].shape[0], start + LANES :]


def after(value, *others):
    return lax.optimization_barrier((value,) + others)[0]


def xor_permute(value, bit, size):
    return lax.ppermute(value, "seq", [(i, i ^ bit) for i in range(size)])


def from_behind(value, by, size):
    pairs = [(i, i + by) for i in range(size) if 0 <= i + by < size]
    return lax.ppermute(value, "seq", pairs)


def near_blocks(own, size, bits=(2, 4, 6)):
    return [xor_permute(own, bit, size) for bit in bits]


class Order:
    def __init__(self):
        self.last = None

    def behind(self, value):
        return value if self.last is None else after(value, self.last)

    def step(self, value):
        self.last = value
        return value


def around(value, by, dp):
    return lax.ppermute(value, "dp", [(i, (i + by) % dp) for i in range(dp)])


def along(value, by, dp):
    return lax.ppermute(value, "dp", [(i, i + by) for i in range(dp) if 0 <= i + by < dp])


def add_up_arrays(parts):
    return functools.reduce(lambda a, b: a + b.astype(F32), parts[1:], parts[0])


VMEM = pl.BlockSpec(memory_space=pltpu.VMEM)
SMEM = pl.BlockSpec(memory_space=pltpu.SMEM)


def plain(array):
    return (array, VMEM)


def fold_chips(mine, got, dp, seq, order):
    dims = (mine.shape[0] * 2 // seq, mine.shape[1])
    chip = order.behind((lax.axis_index("seq") >> 1).reshape(1))
    line, *sends = call(
        functools.partial(fold_chips_kernel, dp),
        None,
        [(chip, SMEM), plain(mine), plain(got)],
        [(shape(dims, F32), VMEM)] + [(shape(dims, BF), VMEM)] * 3,
        name="fold_chips",
    )
    order.step(sends)
    return [line] + [xor_permute(send, bit, seq) for send, bit in zip(sends, (2, 4, 6))]


def fold_line(parts, dp, order):
    dims = (parts[0].shape[0] // dp, parts[0].shape[1])
    place = order.behind(lax.axis_index("dp").reshape(1))
    own, *sends = call(
        functools.partial(fold_line_kernel, dp, len(parts)),
        None,
        [(place, SMEM)] + [plain(part) for part in parts],
        [(shape(dims, F32), VMEM)] + [(shape(dims, BF), VMEM)] * (dp - 1),
        name="fold_line",
    )
    order.step(sends)
    return [own] + [around(send, by, dp) for by, send in enumerate(sends, 1)]


def shards(
    dp,
    seq,
    layer_input,
    out_cotangent,
    seq_lengths,
    inputnorm,
    queryproj,
    keyproj,
    valueproj,
    querynorm,
    keynorm,
    outproj,
    attnnorm,
    prefeednorm,
    gateproj,
    upproj,
    downproj,
    postfeednorm,
):
    micro, _, rows, width = layer_input.shape
    devices = dp * seq
    wrows = width // devices
    qd = queryproj.shape[1]
    ind = qd + 2 * HD
    ff = gateproj.shape[1]
    chunk = ff // devices
    own_ff = dp * chunk
    pad = -(-own_ff // LANES) * LANES
    reach = WINDOW // rows
    split = seq == 8 and dp == 4

    base = lax.axis_index("seq") * rows
    positions = base + jnp.arange(rows, dtype=jnp.int32)
    inverse = jnp.power(F32(10000.0), -2.0 * jnp.arange(HALF, dtype=F32) / HD)
    lengths = seq_lengths[:, 0, 0]
    relative = positions[None, :] & (lengths[:, None] - 1)
    angles = relative.astype(F32)[:, :, None] * inverse
    cosine, sine = jnp.cos(angles), jnp.sin(angles)

    order = Order()
    short = querynorm.shape[0]
    fill = (0, wrows - short)
    gains = [inputnorm, attnnorm, prefeednorm, postfeednorm, jnp.pad(querynorm, fill), jnp.pad(keynorm, fill)]
    gains = jnp.pad(jnp.stack(gains, axis=1), ((0, 0), (0, LANES - len(gains))))
    packed = jnp.concatenate([queryproj, keyproj, valueproj, gains], axis=1)
    along_dp = lax.axis_index("dp").reshape(1)
    if split:
        orows = outproj.shape[0]
        both = jnp.concatenate([packed, jnp.pad(outproj, ((0, wrows - orows), (0, 0)))], axis=1)
        least = -(-(2**19) // (dp * wrows * LANES)) * LANES
        both = jnp.pad(both, ((0, 0), (0, max(0, least - both.shape[1]))))
        both = order.step(lax.optimization_barrier(both[None]))
        line = lax.all_gather(both, "dp", axis=0, tiled=True)

    [gate_up] = call(
        functools.partial(owner_kernel, dp),
        None,
        [plain(gateproj), plain(upproj)],
        [(shape((seq, wrows, 2 * pad), BF), VMEM)],
        name="owner",
    )
    gate_up = lax.all_to_all(gate_up, "seq", 0, 0).reshape(seq * wrows, 2 * pad)
    w_gu = [lax.all_gather(gate_up, "dp", axis=0, tiled=True)]
    if split:
        cosine, sine, line = order.step(order.behind((cosine, sine, line)))
        downproj = after(downproj, line)
    w_down = lax.all_gather(downproj, "dp", axis=0, tiled=True)
    if split:
        in_line, out_line = call(
            line_kernel,
            None,
            [plain(line)],
            [(shape((dp * wrows, ind + LANES), BF), VMEM), (shape((dp * orows, width), BF), VMEM)],
            name="line",
        )

        def untangle(lines, name):
            [array] = call(
                functools.partial(untangle_kernel, dp, seq),
                None,
                [(lax.axis_index("seq").reshape(1), SMEM)] + [plain(line) for line in lines],
                [(shape((lines[0].shape[0] * seq, lines[0].shape[1]), BF), VMEM)],
                name=name,
            )
            return array

        in_lines = [in_line] + near_blocks(order.step(in_line), seq)
        in_lines = order.step(order.behind(in_lines))
        out_lines = [out_line] + near_blocks(after(out_line, in_lines), seq)
        in_lines = in_lines + [xor_permute(line, 1, seq) for line in in_lines]
        in_lines = order.step(order.behind(in_lines))
        w_in = untangle(in_lines, "untangle_in")
        order.step(w_in)
    else:
        w_in = lax.all_gather(packed[None], BOTH, axis=0, tiled=True).reshape(width, -1)
        w_out = lax.all_gather(outproj, BOTH, axis=0, tiled=True)

    def of_micro(array, index):
        dims = array.shape[1:]
        return (array, pl.BlockSpec((1,) + dims, lambda *_: (index,) + (0,) * len(dims)))

    def full(array):
        return (array, whole(array))

    def new(dims, dtype):
        return (shape(dims, dtype), pl.BlockSpec(dims, lambda *_: (0,) * len(dims)))

    smem = pl.BlockSpec(memory_space=pltpu.SMEM)
    each = lambda *dims: pl.BlockSpec((1,) + dims, lambda i: (i,) + (0,) * len(dims))
    w_in_spec = pl.BlockSpec((width, ind), lambda *_: (0, 0))

    cosine = order.behind(cosine)
    gains_spec = pl.BlockSpec((width, LANES), lambda *_: (0, ind // LANES))
    normed_in, raw, query, pair, gains = call(
        functools.partial(project_kernel, short, wrows),
        (micro,),
        [(layer_input, each(1, rows, width)), (w_in, w_in_spec), (w_in, gains_spec)]
        + [(cosine, each(rows, HALF)), (sine, each(rows, HALF))],
        [
            (shape((micro, rows, width), BF), each(rows, width)),
            (shape((micro, rows, qd + HD), F32), each(rows, qd + HD)),
            (shape((micro, rows, qd), BF), each(rows, qd)),
            (shape((micro, rows, 2 * HD), BF), each(rows, 2 * HD)),
            new((8, width), F32),
        ],
        name="project",
    )

    order.step(pair)
    behind = [from_behind(pair, by, seq) for by in range(1, reach + 1)]
    if split:
        out_lines = order.step(order.behind(out_lines))
        out_lines = out_lines + [xor_permute(line, 1, seq) for line in out_lines]
        out_lines = order.step(order.behind(out_lines))
        w_out = order.step(untangle(out_lines, "untangle_out"))
    states = []
    for index in range(micro):
        place = order.behind(jnp.stack([lengths[index], base]))
        pairs = [of_micro(p, index) for p in [pair] + behind]
        attended, attn_out, hidden, normed_ffn = call(
            functools.partial(attend_kernel, reach),
            (1,),
            [(place, smem), of_micro(layer_input, index), of_micro(query, index)]
            + pairs
            + [full(w_out), full(gains)],
            [new((rows, qd), BF), new((rows, width), F32), new((rows, width), F32), new((rows, width), BF)],
            name="attend",
        )
        order.step(normed_ffn)
        s = dict(place=place, pairs=pairs, attended=attended, attn_out=attn_out, hidden=hidden)
        s["sent"] = near_blocks(normed_ffn, seq, BITS) if split else None
        s["nf"] = normed_ffn
        states.append(s)

    if split:
        states[0]["sent"] = order.step(order.behind(states[0]["sent"]))
        w_gu.append(xor_permute(order.step(order.behind(w_gu[0])), 1, seq))
        w_down = [order.step(order.behind(w_down))]
        w_down.append(xor_permute(w_down[0], 1, seq))
    else:
        w_down = [jnp.pad(w_down, ((0, pad - own_ff), (0, 0)))]
    halves = len(w_gu)

    def blocks(array):
        return (array, pl.BlockSpec((rows, array.shape[1]), lambda i: (i, 0)))

    def made(count, columns):
        return (shape((count, columns), BF), pl.BlockSpec((rows, columns), lambda i: (i, 0)))

    def fixed(array):
        return (array, pl.BlockSpec(array.shape, lambda *_: (0,) * array.ndim, pipeline_mode=pl.Buffered(1)))

    def block(index_of, columns):
        return pl.BlockSpec((rows, columns), index_of)

    any_spec = pl.BlockSpec(memory_space=pl.ANY)
    w_scratch = [pltpu.VMEM((width, 2 * pad), BF)] * halves + [pltpu.VMEM((pad, width), BF)] * halves

    def ffn(pieces):
        if not split:
            count = pieces[0].shape[0] // rows
            results = call(
                functools.partial(ffn_grid_kernel, halves),
                (count,),
                [blocks(pieces[0])] + [fixed(w) for w in w_gu] + [fixed(w) for w in w_down],
                [made(count * rows, pad)] * 3 + [made(count * rows, width)],
                name="ffn",
            )
            return pieces[0], results[:1], results[1:2], results[2:3], results[3:]
        count = len(pieces)
        results = call(
            functools.partial(ffn_kernel, count, halves),
            None,
            [plain(array) for array in order.behind(pieces)] + [(w, any_spec) for w in [*w_gu, *w_down]],
            [(shape((count * rows, width), BF), any_spec)]
            + [(shape((count * rows, pad), BF), any_spec)] * (3 * halves)
            + [(shape((rows, width), BF), VMEM)] * count,
            scratch=[pltpu.VMEM((count * rows, pad), BF)] * (3 * halves)
            + w_scratch
            + [pltpu.SemaphoreType.DMA((count * (1 + 3 * halves),)), pltpu.SemaphoreType.DMA((2 * halves,))],
            name="ffn",
        )
        kinds = [results[1 + i * halves : 1 + (i + 1) * halves] for i in range(3)]
        return results[0], *kinds, results[1 + 3 * halves :]

    def ffn_backward(pieces, gelu, rise, begin=0, total=0, kept=()):
        if not split:
            count = pieces[0].shape[0] // rows
            results = call(
                functools.partial(ffn_back_grid_kernel, halves),
                (count,),
                [blocks(pieces[0]), *map(blocks, gelu), *map(blocks, rise)]
                + [fixed(w) for w in w_gu]
                + [fixed(w) for w in w_down],
                [made(count * rows, pad)] * 2 + [made(count * rows, width)],
                name="ffn_back",
            )
            return pieces[0], results[:1], results[1:2], results[2:]
        count = len(pieces)
        arrays = [*gelu, *rise, *w_gu, *w_down, *kept]
        results = call(
            functools.partial(ffn_back_kernel, count, halves, begin, len(kept)),
            None,
            [plain(piece) for piece in pieces] + [(array, any_spec) for array in arrays],
            [(shape((total * rows, width), BF), any_spec)]
            + [(shape((total * rows, pad), BF), any_spec)] * (2 * halves)
            + [(shape((rows, width), BF), VMEM)] * count,
            scratch=[pltpu.VMEM((count * rows, pad), BF)] * (4 * halves)
            + w_scratch
            + [pltpu.SemaphoreType.DMA((count * (1 + 2 * halves),)), pltpu.SemaphoreType.DMA((count * 2 * halves,))]
            + [pltpu.SemaphoreType.DMA((2 * halves,))],
            aliases={count + len(arrays) - len(kept) + index: index for index in range(len(kept))},
            name="ffn_back",
        )
        return results[0], results[1 : 1 + halves], results[1 + halves : 1 + 2 * halves], results[1 + 2 * halves :]

    def pieces_of(own, near):
        if not split:
            return [lax.all_gather(order.behind(own), "seq", axis=0, tiled=True)]
        return list(near) + [order.behind(own)]

    def scatter(parts):
        if not split:
            return [lax.psum_scatter(parts[0], "seq", scatter_dimension=0, tiled=True)]
        return [parts[-1]] + [xor_permute(part, bit, seq) for part, bit in zip(parts, BITS)]

    for s in states:
        pieces = pieces_of(s["nf"], s["sent"])
        s["tokens"], s["gelu"], s["rise"], s["act"], parts = ffn(pieces)
        order.step(parts)
        s["terms"] = scatter(parts)

    def join(pieces):
        [joined] = call(
            join_kernel,
            None,
            [plain(piece) for piece in pieces],
            [(shape((len(pieces) * rows, width), BF), VMEM)],
            name="join",
        )
        return joined

    def over_tokens(left, rights, half, got=None, high_out=None):
        of = lambda s, name: s[name] if name in ("tokens", "d_tokens") else s[name][half]
        lefts = order.behind([of(s, left) for s in states])
        others = [of(s, right) for right in rights for s in states]
        count, high, wide = lefts[0].shape[0], lefts[0].shape[1], others[0].shape[1]
        by_rows = high % 384 == 0
        moving = lambda columns: pl.BlockSpec((count, columns), lambda i: (0, i))
        staying = lambda columns: pl.BlockSpec((count, columns), lambda i: (0, 0), pipeline_mode=pl.Buffered(1))
        if by_rows:
            steps, left_spec, right_spec = high // 384, moving(384), staying(wide)
            out_spec = pl.BlockSpec((384, wide * len(rights)), lambda i: (i, 0))
        else:
            steps, left_spec, right_spec = wide // 384, staying(high), moving(384)
            out_spec = pl.BlockSpec((high_out or high, 384), lambda i: (0, i))
        [made_terms] = call(
            functools.partial(terms_kernel, micro, len(rights), got is not None),
            (steps,),
            [(a, left_spec) for a in lefts]
            + [(b, right_spec) for b in others]
            + ([] if got is None else [(got, out_spec)]),
            [(shape((high_out or high, wide * len(rights)), BF), out_spec)],
            name="terms",
        )
        return order.step(made_terms)

    def other_terms(left, rights, high_out=None):
        return over_tokens(left, rights, 1, None, high_out) if split else None

    def own_terms(left, rights, other, high_out=None):
        return over_tokens(left, rights, 0, xor_permute(other, 1, seq) if split else None, high_out)

    def ffn_back(s, which):
        if not split:
            if which == "rest":
                pieces = pieces_of(s["d_ffn"], s["sent"])
                s["d_tokens"], s["d_gate"], s["d_up"], parts = ffn_backward(pieces, s["gelu"], s["rise"])
                s["terms"] = scatter(order.step(parts))
            return
        own, others = [order.behind(s["d_ffn"])], list(s["sent"])
        total = len(own) + len(others)
        if which == "own":
            s["kept"] = ffn_backward(own, s["gelu"], s["rise"], len(others), total)
            order.step(s["kept"][-1])
            return
        tokens, d_gate, d_up, last = s["kept"]
        others[0] = order.behind(others[0])
        tokens, s["d_gate"], s["d_up"], parts = ffn_backward(
            others, s["gelu"], s["rise"], 0, total, [tokens, *d_gate, *d_up]
        )
        s.setdefault("d_tokens", tokens)
        s["terms"] = scatter(order.step(list(parts)) + list(last))

    layer_out = None
    result = shape((micro, 1, rows, width), F32)
    for index, s in enumerate(states):
        parts = s["terms"]
        chain = [] if layer_out is None else [(layer_out, pl.BlockSpec(memory_space=pl.ANY))]
        layer_out, s["d_ffn"], s["t_post"] = call(
            functools.partial(middle_kernel, len(parts), bool(chain)),
            (1,),
            [full(p) for p in parts]
            + [of_micro(out_cotangent, index), full(s["hidden"]), full(order.behind(gains))]
            + chain,
            [(result, of_micro(result, index)[1]), new((rows, width), BF), new((1, width), F32)],
            aliases={len(parts) + 3: 0} if chain else None,
            name="middle",
        )
        order.step(s["d_ffn"])
        s["sent"] = near_blocks(s["d_ffn"], seq, BITS) if split else None
        ffn_back(s, "own")

    for s in states[:-1]:
        ffn_back(s, "rest")
    late = states[-1]
    if split:
        late["sent"] = order.step(order.behind(late["sent"]))
        late["d_tokens"] = order.step(join(list(late["sent"]) + [late["d_ffn"]]))
        down_other = other_terms("act", ["d_tokens"], own_ff)
    ffn_back(late, "rest")
    down_terms = own_terms("act", ["d_tokens"], down_other if split else None, own_ff)
    for s in states[:-1]:
        s["terms"] = order.step(order.behind(s["terms"]))
    down_grad = lax.psum_scatter(order.behind(down_terms), "dp", scatter_dimension=0, tiled=True)

    def attend_back(index):
        s = states[index]
        parts = s["terms"]
        backs = call(
            functools.partial(attend_back_kernel, reach, len(parts)),
            (1,),
            [(order.behind(s["place"]), smem)]
            + [full(p) for p in parts]
            + [of_micro(out_cotangent, index), full(s["hidden"]), full(s["attn_out"]), of_micro(query, index)]
            + [of_micro(raw, index), of_micro(cosine, index), of_micro(sine, index)]
            + [full(w_out), full(gains)]
            + s["pairs"],
            [new((rows, width), F32), new((rows, width), BF), new((rows, qd), BF)]
            + [new((1, width), F32), new((1, width), F32), new((1, HD), F32)]
            + [new((rows, 2 * HD), BF)] * reach
            + [new((rows, 2 * HD), F32)],
            scratch=[pltpu.VMEM((rows, 2 * HD), F32)] * reach,
            name="attend_back",
        )
        s["d_hidden"], s["d_attn"], s["d_raw_q"], s["t_pre"], s["t_attn"], s["t_query"] = backs[:6]
        order.step(s["d_attn"])
        sent, own = backs[6 : 6 + reach], backs[-1]
        s["d_pairs"] = [own] + [from_behind(value, -by, seq) for by, value in enumerate(sent, 1)]

    def project_back(index, input_grad):
        s = states[index]
        terms = s["d_pairs"]
        chain = [] if input_grad is None else [(input_grad, pl.BlockSpec(memory_space=pl.ANY))]
        keys_spec = pl.BlockSpec((1, rows, HD), lambda *_: (index, 0, qd // HD))
        input_grad, s["d_raw"], s["t_in"], s["t_keys"] = call(
            functools.partial(project_back_kernel, len(terms), bool(chain)),
            (1,),
            [full(t) for t in terms]
            + [(raw, keys_spec), full(s["d_raw_q"]), of_micro(cosine, index), of_micro(sine, index), (w_in, w_in_spec)]
            + [of_micro(layer_input, index), full(s["d_hidden"]), full(order.behind(gains))]
            + chain,
            [(result, of_micro(result, index)[1]), new((rows, ind), BF), new((1, width), F32), new((1, HD), F32)],
            aliases={len(terms) + 8: 0} if chain else None,
            name="project_back",
        )
        order.step(s["d_raw"])
        s["normed_in"] = normed_in[index]
        return input_grad

    def columns_of(part, index):
        [columns] = call(
            functools.partial(columns_kernel, dp),
            (1,),
            [(part, pl.BlockSpec((seq, wrows, pad), lambda *_: (0, 0, index)))],
            [(shape((wrows, ff), F32), pl.BlockSpec((wrows, ff), lambda *_: (0, 0)))],
            name="columns",
        )
        return columns

    input_grad = None
    gu_other = other_terms("tokens", ["d_gate", "d_up"])
    for index in range(micro - 1):
        attend_back(index)
    gu_terms = own_terms("tokens", ["d_gate", "d_up"], gu_other)
    for s in states[:-1]:
        s["d_pairs"] = order.step(order.behind(s["d_pairs"]))
    states[-1]["terms"] = order.step(order.behind(states[-1]["terms"]))
    attend_back(micro - 1)
    down_grad = order.step(order.behind(down_grad))
    gu_sum = lax.psum_scatter(order.behind(gu_terms), "dp", scatter_dimension=0, tiled=True)
    for index in range(micro):
        input_grad = project_back(index, input_grad)
    core = lax.axis_index("seq") & 1
    sums = [s[name] for name in ("t_in", "t_attn", "t_pre", "t_post", "t_query", "t_keys") for s in states]
    half_out = (shape((devices // 2 * wrows, ind + LANES + width), BF), VMEM)
    mine, other = call(
        functools.partial(weights_kernel, short, wrows, micro),
        None,
        [(order.behind((core if split else jnp.int32(0)).reshape(1)), smem)]
        + [plain(s["attended"]) for s in states]
        + [plain(s["d_attn"]) for s in states]
        + [plain(normed_in)]
        + [plain(s["d_raw"]) for s in states]
        + [plain(term) for term in sums],
        [half_out, half_out],
        scratch=[pltpu.VMEM((width, ind + LANES), F32), pltpu.VMEM((qd, width), F32)],
        name="weights",
    )
    order.step(other)
    if split:
        got = xor_permute(other, 1, seq)
        down_grad = order.step(order.behind(down_grad).astype(F32))
        in_parts = fold_chips(mine, got, dp, seq, order)
        gu_sum = order.step(order.behind(gu_sum).reshape(seq, wrows, 2 * pad))
        in_parts = order.step(order.behind(in_parts))
        gu_sum = lax.all_to_all(order.behind(gu_sum), "seq", 0, 0)
        in_parts = fold_line(in_parts, dp, order)
        gu_sum = order.behind(gu_sum)
        gate_grad, up_grad = order.step([columns_of(gu_sum, index) for index in range(2)])
    else:
        halves_of = [part.reshape(devices // 2, wrows, -1) for part in (mine, other)]
        whole_terms = jnp.stack(halves_of, axis=1).reshape(devices, wrows, -1)
        in_parts = [lax.psum_scatter(whole_terms, BOTH, scatter_dimension=0, tiled=True)[0]]
    q_grad, k_grad, v_grad, *gain_sum, out_grad = call(
        functools.partial(finish_kernel, len(in_parts)),
        None,
        [plain(part) for part in order.behind(list(in_parts))],
        [(shape((wrows, columns), F32), VMEM) for columns in (qd, HD, HD)]
        + [(shape((1, size), F32), VMEM) for size in [wrows] * 4 + [short] * 2]
        + [(shape((qd // devices, width), F32), VMEM)],
        name="finish",
    )

    if not split:
        gu_sum = lax.all_to_all(gu_sum.reshape(seq, wrows, 2 * pad), "seq", 0, 0)
        gate_grad, up_grad = (columns_of(gu_sum, index) for index in range(2))
        down_grad = down_grad.astype(F32)

    return (
        layer_out,
        input_grad,
        gain_sum[0].reshape(wrows),
        q_grad,
        k_grad,
        v_grad,
        gain_sum[4].reshape(short),
        gain_sum[5].reshape(short),
        out_grad,
        gain_sum[1].reshape(wrows),
        gain_sum[2].reshape(wrows),
        gate_grad,
        up_grad,
        down_grad,
        gain_sum[3].reshape(wrows),
    )


def solution(mesh):
    dp, seq = mesh.shape["dp"], mesh.shape["seq"]
    acts = P(None, "dp", "seq", None)
    vector = P(BOTH)
    matrix = P(BOTH, None)
    weights = (vector,) + (matrix,) * 3 + (vector,) * 2 + (matrix, vector, vector) + (matrix,) * 3 + (vector,)
    return jax.shard_map(
        functools.partial(shards, dp, seq),
        mesh=mesh,
        in_specs=(acts, acts, P(None, "dp", None)) + weights,
        out_specs=(acts, acts) + weights,
        check_vma=False,
    )
```
